32 devices in a mesh: groups: 2 (over y), space: 4 (over x, core), tm: 4 (over z).
Axes of the slice: x: 2, y: 2, z: 4, core: 2. Of those that a mesh axis runs over, the one named last changes fastest.
Arguments:
- couplings: float32 [9, 4, 4, 2, 4, 96, 192], P(None, 'tm', 'space'), may hold values from -0.15625 to 0.15625
- source: float32 [4, 4, 2, 4, 96, 256], P('tm', 'space'), may hold values from -6 to 6
- initial: float32 [4, 4, 2, 4, 96, 256], P('tm', 'space'), may hold values from -6 to 6
- vectors: float32 [512, 4, 4, 2, 4, 192], P(None, 'tm', 'space'), may hold values from -0.0390625 to 0.0390625
- inverse_eigen: float32 [2, 512], replicated, may hold values from -20 to 20
Outputs:
- solution: float32 [8, 4, 2, 4, 96, 256], P(('groups', 'tm'), 'space'), parts along dimension 0
- residual: float32 [8, 4, 2, 4, 96, 256], P(('groups', 'tm'), 'space'), parts along dimension 0
The draws below stay inside these ranges and needn't reach their ends.
There are 2 independent parts, one for each index of `groups`. The reference program is written for one: setup_inputs(seed, part) draws one part's arguments, and reference() takes and returns one part's arrays. A program takes and returns all parts, laid end to end along the dimension named above; an argument that names none is the same for every part. Nothing has to cross between parts.
All inputs are finite; a program needn't handle non-finite values.
Results may differ from the reference program's by a relative error of at most 0.0001.
Values sent between devices are 32-bit elements; how exact they have to be, the bound alone decides.
A program may use at most 64 MiB of HBM per device.

```python
import jax
import jax.numpy as jnp
from jax import lax

NC = 96
NR = 128
NV = 512
LX = 4
LY = 2
ITERS = 2
NZ = 4
NT = 4


def block_scale(rng, shape, cuts, smallest, top_value):
    level, own = 1.0, jax.random.fold_in(rng, 6)
    for dim, blocks in cuts:
        steps = jnp.exp(jax.random.uniform(jax.random.fold_in(own, dim), (blocks,), jnp.float32, smallest / len(cuts), top_value / len(cuts)))
        level = level * jnp.repeat(steps, shape[dim] // blocks).reshape([-1 if axis == dim else 1 for axis in range(len(shape))])
    return level


def bell_draw(rng, dims, deviation, most, split=(), dtype=jnp.bfloat16):
    gain = block_scale(rng, dims, split, -0.22, 0.18) if split else 1.0
    drawn = jax.random.normal(rng, dims, jnp.float32) * deviation * gain
    return jnp.minimum(jnp.maximum(drawn, -most), most).astype(dtype)


def setup_inputs(seed: int = 0, part: int = 0) -> dict:
    streams_of = jax.random.split(jax.random.key(seed), 6)
    couplings = bell_draw(streams_of[0], (9, NT, NZ, LY, LX, NC, 2 * NC), (18 * NC) ** -0.5, 0.15625, ((1, 4), (2, 4)), jnp.float32)
    source = bell_draw(streams_of[1], (NT, NZ, LY, LX, NC, 2 * NR), 1.0, 6.0, ((0, 4), (1, 4)), jnp.float32)
    initial = bell_draw(streams_of[2], (NT, NZ, LY, LX, NC, 2 * NR), 1.0, 6.0, ((0, 4), (1, 4)), jnp.float32)
    vectors = bell_draw(streams_of[3], (NV, NT, NZ, LY, LX, 2 * NC), (2 * NC * LX * LY * NZ * NT) ** -0.5, 0.0390625, ((1, 4), (2, 4)), jnp.float32)
    inverse_eigen = jnp.clip(jax.random.uniform(streams_of[4], (2, NV), jnp.float32, -20.0, 20.0), -20.0, 20.0)
    return {"couplings": couplings, "source": source, "initial": initial, "vectors": vectors, "inverse_eigen": inverse_eigen}


def coupled(matrix, spinor):
    middle = spinor.shape[-1] // 2
    turned = jnp.concatenate([-spinor[..., middle:], spinor[..., :middle]], axis=-1)
    stacked = jnp.concatenate([spinor, turned], axis=-2)
    return jnp.einsum("tzyxij,tzyxjn->tzyxin", matrix, stacked, precision=lax.Precision.HIGHEST)


def apply_operator(spinor, couplings):
    forward_t = jnp.roll(spinor, -1, 0)
    forward_t = forward_t.at[-1].multiply(-1.0)
    backward_t = jnp.roll(spinor, 1, 0)
    backward_t = backward_t.at[0].multiply(-1.0)
    neighbours = [spinor, jnp.roll(spinor, -1, 3), jnp.roll(spinor, 1, 3), jnp.roll(spinor, -1, 2), jnp.roll(spinor, 1, 2), jnp.roll(spinor, -1, 1), jnp.roll(spinor, 1, 1), forward_t, backward_t]
    summed = jnp.zeros_like(spinor)
    for direction in range(9):
        summed = summed + coupled(couplings[direction], neighbours[direction])
    return summed


def deflate(residual, vectors, inverse_eigen):
    middle = residual.shape[-1] // 2
    number = vectors.shape[0]
    negated = jnp.concatenate([residual[..., middle:], -residual[..., :middle]], axis=-1)
    stacked = jnp.concatenate([residual, negated], axis=-2)
    coefficients = jnp.dot(vectors.reshape(number, -1), stacked.reshape(-1, stacked.shape[-1]), precision=lax.Precision.HIGHEST, preferred_element_type=jnp.float32)
    eigen_real = inverse_eigen[0][:, None]
    eigen_imag = inverse_eigen[1][:, None]
    coef_real = coefficients[:, :middle]
    coef_imag = coefficients[:, middle:]
    scaled_real = eigen_real * coef_real - eigen_imag * coef_imag
    scaled_imag = eigen_real * coef_imag + eigen_imag * coef_real
    dstack = jnp.stack([jnp.concatenate([scaled_real, scaled_imag], axis=-1), jnp.concatenate([-scaled_imag, scaled_real], axis=-1)])
    halves = vectors.reshape(vectors.shape[:-1] + (2, vectors.shape[-1] // 2))
    return jnp.einsum("ktzyxci,ckn->tzyxin", halves, dstack, precision=lax.Precision.HIGHEST)


def reference(couplings, source, initial, vectors, inverse_eigen):
    iterate = initial
    residual = source
    for sweep in range(ITERS):
        residual = source - apply_operator(iterate, couplings)
        iterate = iterate + deflate(residual, vectors, inverse_eigen) + 0.5 * residual
    return iterate, residual
```

```python
import functools

import jax
import jax.numpy as jnp
from jax import lax
from jax.experimental import pallas as pl
from jax.experimental.pallas import tpu as pltpu
from jax.sharding import PartitionSpec as P

ITERS = 2
MESH = pl.DeviceIdType.MESH
F32 = jnp.float32
BF16 = jnp.bfloat16


def split(value):
    high = value.astype(BF16)
    low = (value - high.astype(F32)).astype(BF16)
    return high, low


def dot(a, b):
    return jnp.dot(a, b, preferred_element_type=F32)


class Dims:
    def __init__(self, mesh, ly, lx, nc, full, nv):
        self.ng, self.ns, self.nt = mesh.shape["groups"], mesh.shape["space"], mesh.shape["tm"]
        self.ly, self.lx, self.nc, self.full, self.nv = ly, lx, nc, full, nv
        assert self.ng == 2 and ly == 2
        self.width = full // self.ng
        self.sites = ly * lx
        self.members = self.ns // 2 * self.nt
        self.half = nv // 2
        self.pieces = min(self.members, self.half // 8)
        self.rows = self.half // self.pieces


def kernel(
    D, coup_h, src_h, x0_h, vec_h, eig_h, sol, res,
    coup, src, x0f, vec, eig, local_sem,
    x0, x1, r0, r1, x1o, r1o,
    m_hi, m_lo, h_hi, h_lo, wk_hi, wk_lo, wt_hi, wt_lo, acc, dst,
    halo, part, core_in, mine, rs_in, dfull, dother, eig_t,
    halo_send, halo_recv, core_send, core_recv, rs_send, rs_recv, ag_send, ag_recv, re_send, re_recv,
    y_send, y_recv, yx_send, yx_recv, yr_send, yr_recv, r2_send, r2_recv,
):
    ns, nt, sites, nc, lx, ly = D.ns, D.nt, D.sites, D.nc, D.lx, D.ly
    nv, half, rows, pieces, members, width, full = D.nv, D.half, D.rows, D.pieces, D.members, D.width, D.full
    me_g, me_s, me_t = lax.axis_index("groups"), lax.axis_index("space"), lax.axis_index("tm")
    parity = lax.rem(me_s, 2)
    pairs = ns // 2
    rank = me_t * pairs + me_s // 2
    partner = {"groups": me_g, "space": me_s + 1 - 2 * parity, "tm": me_t}
    other_group = {"groups": 1 - me_g, "space": me_s, "tm": me_t}

    loads = [
        pltpu.make_async_copy(x0_h, x0f, local_sem.at[0]),
        pltpu.make_async_copy(coup_h, coup, local_sem.at[1]),
        pltpu.make_async_copy(src_h, src, local_sem.at[2]),
        pltpu.make_async_copy(eig_h, eig, local_sem.at[3]),
        pltpu.make_async_copy(vec_h, vec, local_sem.at[4]),
    ]
    for load in loads:
        load.start()

    barrier = pltpu.get_barrier_semaphore()
    total = ns * nt
    flat = me_t * ns + me_s

    def greet(o, carry):
        other = lax.rem(flat + o, total)
        pl.semaphore_signal(
            barrier, inc=1,
            device_id={"groups": me_g, "space": lax.rem(other, ns), "tm": other // ns}, device_id_type=MESH,
        )
        return carry

    lax.fori_loop(1, total, greet, 0)
    pl.semaphore_signal(barrier, inc=1, device_id=other_group, device_id_type=MESH)

    first_half = lax.broadcasted_iota(jnp.int32, (nc, width), 1) < width // 2

    def turn(v):
        return pltpu.roll(v, width // 2, 1)

    def times_i(v):
        turned = turn(v)
        return jnp.where(lax.broadcasted_iota(jnp.int32, v.shape, 1) < width // 2, -turned, turned)

    def take_half(value):
        re, im = value[:, 0:width], value[:, width:full]
        stay = jnp.where(me_g == 0, re, im)
        move = jnp.where(me_g == 0, im, re)
        return jnp.where(first_half == (me_g == 0), stay, turn(move))

    def join(own, other):
        g0 = jnp.where(me_g == 0, own, other)
        g1 = jnp.where(me_g == 0, other, own)
        return jnp.concatenate(
            [jnp.where(first_half, g0, turn(g1)), jnp.where(first_half, turn(g0), g1)], axis=1
        )

    def stacked(value, turned):
        high, low = split(value)
        t_high, t_low = split(turned)
        return jnp.concatenate(
            [jnp.concatenate([high, t_high], axis=0), jnp.concatenate([low, t_low], axis=0)], axis=1
        )

    def product(hi, lo, rhs):
        one = dot(hi, rhs)
        return one[:, 0:width] + one[:, width:2 * width] + dot(lo, rhs[:, 0:width])

    up_s, down_s = lax.rem(me_s + 1, ns), lax.rem(me_s + ns - 1, ns)
    up_t, down_t = lax.rem(me_t + 1, nt), lax.rem(me_t + nt - 1, nt)
    targets = (
        (2, {"groups": me_g, "space": me_s, "tm": down_t}),
        (3, {"groups": me_g, "space": me_s, "tm": up_t}),
        (0, {"groups": me_g, "space": down_s, "tm": me_t}),
        (1, {"groups": me_g, "space": up_s, "tm": me_t}),
    )

    def halo_copy(it, site, slot, target):
        source = x0 if it == 0 else x1
        return pltpu.make_async_remote_copy(
            src_ref=source.at[site],
            dst_ref=halo.at[it, slot, site],
            send_sem=halo_send.at[it, slot, site],
            recv_sem=halo_recv.at[it, slot, site],
            device_id=target,
            device_id_type=MESH,
        )

    def send_halo(it, site):
        for slot, target in targets:
            halo_copy(it, site, slot, target).start()

    def x1_copy(site):
        return pltpu.make_async_remote_copy(
            src_ref=x1.at[site], dst_ref=x1o.at[site], send_sem=yx_send.at[site], recv_sem=yx_recv.at[site],
            device_id=other_group, device_id_type=MESH,
        )

    def r1_copy(site):
        return pltpu.make_async_remote_copy(
            src_ref=r1.at[site], dst_ref=r1o.at[site], send_sem=yr_send.at[site], recv_sem=yr_recv.at[site],
            device_id=other_group, device_id_type=MESH,
        )

    def loop(start, stop, action):
        def body(o, carry):
            action(o)
            return carry

        lax.fori_loop(start, stop, body, 0)

    loads[0].wait()
    pl.semaphore_wait(barrier, total)

    def begin(site):
        x0[site] = take_half(x0f[site])
        send_halo(0, site)

    loop(0, sites, begin)

    sign_up = jnp.where(me_t == nt - 1, -1.0, 1.0).astype(F32)
    sign_down = jnp.where(me_t == 0, -1.0, 1.0).astype(F32)

    loads[1].wait()

    def outs_of(site):
        y, x = site // lx, lax.rem(site, lx)
        return (
            site,
            y * lx + lax.rem(x + lx - 1, lx),
            y * lx + lax.rem(x + 1, lx),
            lax.rem(y + 1, ly) * lx + x,
        )

    def prepare_matrices(site):
        for d, out in enumerate(outs_of(site)):
            value = coup[d, out] if d < 3 else coup[3, out] + coup[4, out]
            high, low = split(value)
            m_hi[site, d * nc:(d + 1) * nc, :] = high
            m_lo[site, d * nc:(d + 1) * nc, :] = low
        for d, sign in enumerate((None, None, sign_up, sign_down)):
            value = coup[5 + d, site]
            if sign is not None:
                value = value * sign
            high, low = split(value)
            h_hi[site, d] = high
            h_lo[site, d] = low

    loop(0, sites, prepare_matrices)

    def self_part(field):
        acc[...] = jnp.zeros_like(acc)

        def body(site):
            value = field[site]
            out_all = product(m_hi[site], m_lo[site], stacked(value, times_i(value)))
            for d, out in enumerate(outs_of(site)):
                acc[out] += out_all[d * nc:(d + 1) * nc]

        loop(0, sites, body)

    def prepare_vectors(site):
        turned = vec[site]
        high, low = split(turned.T)
        wk_hi[site] = high
        wk_lo[site] = low
        high, low = split(turned)
        wt_hi[site, :, 0:nv] = high[0:nc]
        wt_hi[site, :, nv:2 * nv] = high[nc:2 * nc]
        wt_lo[site, :, 0:nv] = low[0:nc]
        wt_lo[site, :, nv:2 * nv] = low[nc:2 * nc]

    def halo_part(it, out):
        last = it + 1 == ITERS

        def body(site):
            total = acc[site]
            for slot in range(4):
                copy = [t for t in targets if t[0] == slot][0]
                halo_copy(it, site, slot, copy[1]).wait_recv()
                value = halo[it, slot, site]
                total = total + product(h_hi[site, slot], h_lo[site, slot], stacked(value, times_i(value)))
            residual = src[site] - total
            out[site] = residual
            if last:
                r1_copy(site).start()
            part[it] += product(wk_hi[site], wk_lo[site], stacked(residual, -times_i(residual)))

        part[it] = jnp.zeros((nv, width), F32)
        loop(0, sites, body)

    def member(q):
        return {"groups": me_g, "space": lax.rem(q, pairs) * 2 + parity, "tm": q // pairs}

    my_rows = pl.multiple_of(parity * half, 8)
    other_rows = pl.multiple_of((1 - parity) * half, 8)
    piece = lax.rem(rank, pieces)
    block = rank - piece
    piece_row = pl.multiple_of(my_rows + piece * rows, 8)

    def core_copy(it):
        return pltpu.make_async_remote_copy(
            src_ref=part.at[it, pl.ds(other_rows, half)],
            dst_ref=core_in.at[it],
            send_sem=core_send.at[it],
            recv_sem=core_recv.at[it],
            device_id=partner,
            device_id_type=MESH,
        )

    def rs_copy(it, o):
        q = lax.rem(rank + o, members)
        row = pl.multiple_of(lax.rem(q, pieces) * rows, 8)
        return pltpu.make_async_remote_copy(
            src_ref=mine.at[it, pl.ds(row, rows)],
            dst_ref=rs_in.at[it, o],
            send_sem=rs_send.at[it, o],
            recv_sem=rs_recv.at[it, o],
            device_id=member(q),
            device_id_type=MESH,
        )

    def ag_copy(it, o):
        q = block + lax.rem(piece + o, pieces)
        return pltpu.make_async_remote_copy(
            src_ref=dfull.at[it, pl.ds(piece_row, rows)],
            dst_ref=dfull.at[it, pl.ds(piece_row, rows)],
            send_sem=ag_send.at[it, o],
            recv_sem=ag_recv.at[it, o],
            device_id=member(q),
            device_id_type=MESH,
        )

    def row_of(o):
        return pl.multiple_of(my_rows + lax.rem(piece + pieces - o, pieces) * rows, 8)

    def relay_copy(it, o):
        return pltpu.make_async_remote_copy(
            src_ref=dfull.at[it, pl.ds(row_of(o), rows)],
            dst_ref=dfull.at[it, pl.ds(row_of(o), rows)],
            send_sem=re_send.at[it, o],
            recv_sem=re_recv.at[it, o],
            device_id=partner,
            device_id_type=MESH,
        )

    def y_copy(o):
        return pltpu.make_async_remote_copy(
            src_ref=dfull.at[ITERS - 1, pl.ds(row_of(o), rows)],
            dst_ref=dother.at[pl.ds(row_of(o), rows)],
            send_sem=y_send.at[o],
            recv_sem=y_recv.at[o],
            device_id=other_group,
            device_id_type=MESH,
        )

    def relay_other(o):
        return pltpu.make_async_remote_copy(
            src_ref=dother.at[pl.ds(row_of(o), rows)],
            dst_ref=dother.at[pl.ds(row_of(o), rows)],
            send_sem=r2_send.at[o],
            recv_sem=r2_recv.at[o],
            device_id=partner,
            device_id_type=MESH,
        )

    def fill(slot, value):
        dst[slot] = stacked(value, times_i(value))

    def reduce_coefficients(it):
        last = it + 1 == ITERS
        core_copy(it).start()
        core_copy(it).wait_recv()
        mine[it] = part[it, pl.ds(my_rows, half), :] + core_in[it]
        loop(1, members, lambda o: rs_copy(it, o).start())
        own = mine[it, pl.ds(pl.multiple_of(piece * rows, 8), rows), :]

        def gather(o, total):
            rs_copy(it, o).wait_recv()
            return total + rs_in[it, o]

        coef = lax.fori_loop(1, members, gather, own)
        eigen = eig_t[pl.ds(piece_row, rows), :]
        dfull[it, pl.ds(piece_row, rows), :] = eigen[:, 0:1] * coef + eigen[:, 1:2] * times_i(coef)
        loop(1, pieces, lambda o: ag_copy(it, o).start())
        relay_copy(it, 0).start()
        if last:
            y_copy(0).start()

        def forward(o):
            ag_copy(it, o).wait_recv()
            relay_copy(it, o).start()
            if last:
                y_copy(o).start()

        loop(1, pieces, forward)
        loop(0, pieces, lambda o: relay_copy(it, o).wait_recv())
        fill(0, dfull[it])

    def expand(first, group, slot):
        a_hi = wt_hi[pl.ds(first, group)].reshape(group * nc, 2 * nv)
        a_lo = wt_lo[pl.ds(first, group)].reshape(group * nc, 2 * nv)
        return product(a_hi, a_lo, dst[slot]).reshape(group, nc, width)

    group = 4 if sites % 4 == 0 else 1

    self_part(x0)
    loads[2].wait()

    def half_source(site):
        src[site, :, 0:width] = take_half(src[site])

    loads[3].wait()
    eig_t[...] = jnp.concatenate([eig[...]] * 4, axis=0).T
    loads[4].wait()
    loop(0, sites, prepare_vectors)

    srch = src
    loop(0, sites, half_source)
    src = srch.at[:, :, 0:width]

    halo_part(0, r0)
    reduce_coefficients(0)

    def update(g):
        first = g * group
        now = pl.ds(first, group)
        x1[now] = x0[now] + expand(first, group, 0) + 0.5 * r0[now]

        def send(site):
            send_halo(1, site)
            x1_copy(site).start()

        loop(first, first + group, send)

    loop(0, sites // group, update)
    self_part(x1)
    halo_part(1, r1)
    reduce_coefficients(1)

    def finish_own(g):
        first = g * group
        now = pl.ds(first, group)
        acc[now] = x1[now] + expand(first, group, 0) + 0.5 * r1[now]

    loop(0, sites // group, finish_own)

    def pass_on(o):
        y_copy(o).wait_recv()
        relay_other(o).start()

    loop(0, pieces, pass_on)

    def join_residual(site):
        x1_copy(site).wait_recv()
        r1_copy(site).wait_recv()
        res[site] = join(r1[site], r1o[site])

    loop(0, sites, join_residual)
    loop(0, pieces, lambda o: relay_other(o).wait_recv())
    fill(1, dother[...])

    def finish_other(g):
        first = g * group
        now = pl.ds(first, group)
        other = x1o[now] + expand(first, group, 1) + 0.5 * r1o[now]
        for i in range(group):
            sol[first + i] = join(acc[first + i], other[i])

    loop(0, sites // group, finish_other)

    for it in range(ITERS):
        core_copy(it).wait_send()
        loop(1, members, lambda o: rs_copy(it, o).wait_send())
        loop(1, pieces, lambda o: ag_copy(it, o).wait_send())
        loop(0, pieces, lambda o: relay_copy(it, o).wait_send())

        def drain(site):
            for slot, target in targets:
                halo_copy(it, site, slot, target).wait_send()

        loop(0, sites, drain)

    def drain_y(o):
        y_copy(o).wait_send()
        relay_other(o).wait_send()

    loop(0, pieces, drain_y)

    def drain_fields(site):
        x1_copy(site).wait_send()
        r1_copy(site).wait_send()

    loop(0, sites, drain_fields)


def solve(mesh, couplings, source, initial, vectors, inverse_eigen):
    nine, _, _, ly, lx, nc, _ = couplings.shape
    full = source.shape[-1]
    nv = vectors.shape[0]
    D = Dims(mesh, ly, lx, nc, full, nv)
    sites, width = D.sites, D.width
    field = (sites, nc, full)
    mine = (sites, nc, width)
    vecs = vectors.reshape(nv, sites, 2 * nc).transpose(1, 2, 0)
    any_spec = pl.BlockSpec(memory_space=pl.ANY)
    vmem = pl.BlockSpec(memory_space=pltpu.VMEM)
    dma = pltpu.SemaphoreType.DMA
    out = jax.ShapeDtypeStruct(field, F32)
    x, r = pl.pallas_call(
        functools.partial(kernel, D),
        out_shape=(out, out),
        in_specs=[any_spec] * 5,
        out_specs=(vmem, vmem),
        scratch_shapes=[
            pltpu.VMEM((nine, sites, nc, 2 * nc), F32),
            pltpu.VMEM(field, F32),
            pltpu.VMEM(field, F32),
            pltpu.VMEM((sites, 2 * nc, nv), F32),
            pltpu.VMEM((2, nv), F32),
            dma((5,)),
        ]
        + [pltpu.VMEM(mine, F32)] * 6
        + [
            pltpu.VMEM((sites, 4 * nc, 2 * nc), BF16),
            pltpu.VMEM((sites, 4 * nc, 2 * nc), BF16),
            pltpu.VMEM((sites, 4, nc, 2 * nc), BF16),
            pltpu.VMEM((sites, 4, nc, 2 * nc), BF16),
            pltpu.VMEM((sites, nv, 2 * nc), BF16),
            pltpu.VMEM((sites, nv, 2 * nc), BF16),
            pltpu.VMEM((sites, nc, 2 * nv), BF16),
            pltpu.VMEM((sites, nc, 2 * nv), BF16),
            pltpu.VMEM(mine, F32),
            pltpu.VMEM((2, 2 * nv, 2 * width), BF16),
            pltpu.VMEM((ITERS, 4) + mine, F32),
            pltpu.VMEM((ITERS, nv, width), F32),
            pltpu.VMEM((ITERS, D.half, width), F32),
            pltpu.VMEM((ITERS, D.half, width), F32),
            pltpu.VMEM((ITERS, D.members, D.rows, width), F32),
            pltpu.VMEM((ITERS, nv, width), F32),
            pltpu.VMEM((nv, width), F32),
            pltpu.VMEM((nv, 8), F32),
            dma((ITERS, 4, sites)),
            dma((ITERS, 4, sites)),
            dma((ITERS,)),
            dma((ITERS,)),
            dma((ITERS, D.members)),
            dma((ITERS, D.members)),
            dma((ITERS, D.pieces)),
            dma((ITERS, D.pieces)),
            dma((ITERS, D.pieces)),
            dma((ITERS, D.pieces)),
            dma((D.pieces,)),
            dma((D.pieces,)),
            dma((sites,)),
            dma((sites,)),
            dma((sites,)),
            dma((sites,)),
            dma((D.pieces,)),
            dma((D.pieces,)),
        ],
        compiler_params=pltpu.CompilerParams(
            collective_id=0, has_side_effects=True, vmem_limit_bytes=56 * 1024 * 1024
        ),
    )(
        couplings.reshape(nine, sites, nc, 2 * nc),
        source.reshape(field),
        initial.reshape(field),
        vecs,
        inverse_eigen,
    )
    return x.reshape(source.shape), r.reshape(source.shape)


def solution(mesh):
    in_specs = (
        P(None, "tm", "space", None, None, None, None),
        P("tm", "space", None, None, None, None),
        P("tm", "space", None, None, None, None),
        P(None, "tm", "space", None, None, None),
        P(),
    )
    out_specs = (
        P(("groups", "tm"), "space", None, None, None, None),
        P(("groups", "tm"), "space", None, None, None, None),
    )
    return jax.shard_map(
        functools.partial(solve, mesh), mesh=mesh, in_specs=in_specs, out_specs=out_specs, check_vma=False
    )
```

```python
import functools

import jax
import jax.numpy as jnp
from jax import lax
from jax.experimental import pallas as pl
from jax.experimental.pallas import tpu as pltpu
from jax.sharding import PartitionSpec as P

ITERS = 2
MESH = pl.DeviceIdType.MESH
F32 = jnp.float32
BF16 = jnp.bfloat16


def split(value):
    high = value.astype(BF16)
    low = (value - high.astype(F32)).astype(BF16)
    return high, low


def dot(a, b):
    return jnp.dot(a, b, preferred_element_type=F32)


class Dims:
    def __init__(self, mesh, ly, lx, nc, full, nv):
        self.ng, self.ns, self.nt = mesh.shape["groups"], mesh.shape["space"], mesh.shape["tm"]
        self.ly, self.lx, self.nc, self.full, self.nv = ly, lx, nc, full, nv
        assert self.ng == 2 and ly == 2 and lx % 2 == 0
        self.width = full // 2
        self.sites = ly * lx
        self.members = self.ns // 2 * self.nt
        self.packed = nv // 2
        self.half = self.packed // 2
        self.pieces = min(self.members, self.half // 8)
        self.rows = self.half // self.pieces


CHUNKS = 2


def kernel(
    D, coup_h, src_h, x0_h, vec_h, eig_h, sol, res,
    coup, srcf, x0f, vec, eig, local_sem,
    x0, x1, r0, r1, src, x1o, r1o, acc, early,
    m_loc, m_halo, wk, wt, rhs_loc, rhs_halo, rhs_res, dst, proj,
    halo, part, core_in, mine, rs_in, dfull, dother, eig_t,
    halo_send, halo_recv, core_send, core_recv, rs_send, rs_recv, ag_send, ag_recv, re_send, re_recv,
    y_send, y_recv, yx_send, yx_recv, yr_send, yr_recv, r2_send, r2_recv,
):
    ns, nt, sites, nc, lx, ly = D.ns, D.nt, D.sites, D.nc, D.lx, D.ly
    nv, packed, half, rows, pieces, members = D.nv, D.packed, D.half, D.rows, D.pieces, D.members
    width, full = D.width, D.full
    quarter = width // 4
    me_g, me_s, me_t = lax.axis_index("groups"), lax.axis_index("space"), lax.axis_index("tm")
    parity = lax.rem(me_s, 2)
    pairs = ns // 2
    rank = me_t * pairs + me_s // 2
    partner = {"groups": me_g, "space": me_s + 1 - 2 * parity, "tm": me_t}
    other_group = {"groups": 1 - me_g, "space": me_s, "tm": me_t}
    last = ITERS - 1
    block_k = ly * 2 * nc

    loads = [
        pltpu.make_async_copy(x0_h, x0f, local_sem.at[0]),
        pltpu.make_async_copy(coup_h, coup, local_sem.at[1]),
        pltpu.make_async_copy(src_h, srcf, local_sem.at[2]),
        pltpu.make_async_copy(eig_h, eig, local_sem.at[3]),
        pltpu.make_async_copy(vec_h, vec, local_sem.at[4]),
    ]
    for load in loads:
        load.start()

    barrier = pltpu.get_barrier_semaphore()
    total = ns * nt
    flat = me_t * ns + me_s

    def greet(o, carry):
        other = lax.rem(flat + o, total)
        pl.semaphore_signal(
            barrier, inc=1,
            device_id={"groups": me_g, "space": lax.rem(other, ns), "tm": other // ns}, device_id_type=MESH,
        )
        return carry

    lax.fori_loop(1, total, greet, 0)
    pl.semaphore_signal(barrier, inc=1, device_id=other_group, device_id_type=MESH)

    def lane(shape):
        return lax.broadcasted_iota(jnp.int32, shape, 1)

    def turn(v):
        return pltpu.roll(v, width // 2, 1)

    def later(v):
        return pltpu.roll(v, quarter, 1)

    def sooner(v):
        return pltpu.roll(v, width - quarter, 1)

    def real_lanes(v):
        return lane(v.shape) < width // 2

    def first_lanes(v):
        return lax.rem(lane(v.shape), width // 2) < quarter

    def times_i(v):
        turned = turn(v)
        return jnp.where(real_lanes(v), -turned, turned)

    def pack(even, odd):
        return jnp.where(first_lanes(even), even, later(odd)), jnp.where(first_lanes(even), sooner(even), odd)

    def take(c, value):
        re, im = value[:, 0:width], value[:, width:full]
        if c == 0:
            return jnp.where(real_lanes(re), re, turn(im))
        return jnp.where(real_lanes(re), turn(re), im)

    def take_pair(c, x, ref):
        of_g0, of_g1 = pack(take(c, ref[x]), take(c, ref[lx + x]))
        return jnp.where(me_g == 0, of_g0, of_g1)

    def groups_of(own, other):
        return pack(jnp.where(me_g == 0, own, other), jnp.where(me_g == 0, other, own))

    def join(c0, c1):
        return jnp.concatenate(
            [jnp.where(real_lanes(c0), c0, turn(c1)), jnp.where(real_lanes(c0), turn(c0), c1)], axis=1
        )

    def stacked(value, turned):
        high, low = split(value)
        t_high, t_low = split(turned)
        return jnp.concatenate(
            [jnp.concatenate([high, t_high], axis=0), jnp.concatenate([low, t_low], axis=0)], axis=1
        )

    keep = jnp.where(lax.rem(lane((2 * nc, 2 * width)), width // 2) < quarter, 1.0, 0.0).astype(BF16)

    def masked(value, turned):
        both = stacked(value, turned)
        even = both * keep
        return jnp.concatenate([even, both - even], axis=0)

    def fold(out, count):
        top, bottom = out[0:count], out[count:2 * count]
        return (top[:, 0:width] + top[:, width:2 * width]) + (bottom[:, 0:width] + bottom[:, width:2 * width])

    up_s, down_s = lax.rem(me_s + 1, ns), lax.rem(me_s + ns - 1, ns)
    up_t, down_t = lax.rem(me_t + 1, nt), lax.rem(me_t + nt - 1, nt)
    targets = (
        (2, {"groups": me_g, "space": me_s, "tm": down_t}),
        (3, {"groups": me_g, "space": me_s, "tm": up_t}),
        (0, {"groups": me_g, "space": down_s, "tm": me_t}),
        (1, {"groups": me_g, "space": up_s, "tm": me_t}),
    )
    target_of = dict(targets)

    def index(it, c):
        return it * CHUNKS + c

    def halo_copy(it, c, x, slot):
        source = x0 if it == 0 else x1
        u = index(it, c)
        return pltpu.make_async_remote_copy(
            src_ref=source.at[c, x],
            dst_ref=halo.at[u, slot, x],
            send_sem=halo_send.at[u, slot, x],
            recv_sem=halo_recv.at[u, slot, x],
            device_id=target_of[slot],
            device_id_type=MESH,
        )

    def send_halo(it, c, x):
        for slot, _ in targets:
            halo_copy(it, c, x, slot).start()

    def x1_copy(c, x):
        return pltpu.make_async_remote_copy(
            src_ref=x1.at[c, x], dst_ref=x1o.at[c, x], send_sem=yx_send.at[c, x], recv_sem=yx_recv.at[c, x],
            device_id=other_group, device_id_type=MESH,
        )

    def r1_copy(c, x):
        return pltpu.make_async_remote_copy(
            src_ref=r1.at[c, x], dst_ref=r1o.at[c, x], send_sem=yr_send.at[c, x], recv_sem=yr_recv.at[c, x],
            device_id=other_group, device_id_type=MESH,
        )

    def loop(start, stop, action):
        def body(o, carry):
            action(o)
            return carry

        lax.fori_loop(start, stop, body, 0)

    sign_up = jnp.where(me_t == nt - 1, -1.0, 1.0).astype(F32)
    sign_down = jnp.where(me_t == 0, -1.0, 1.0).astype(F32)

    def prepare_matrices(x):
        def both(value_of):
            high, low = split(jnp.concatenate([value_of(x), value_of(lx + x)], axis=1))
            return jnp.concatenate([high, low], axis=0)

        for d in range(3):
            m_loc[x, :, d * block_k:(d + 1) * block_k] = both(lambda site: coup[d, site])
        m_loc[x, :, 3 * block_k:4 * block_k] = both(lambda site: coup[3, site] + coup[4, site])
        for d, sign in enumerate((None, None, sign_up, sign_down)):
            m_halo[x, :, d * block_k:(d + 1) * block_k] = both(
                lambda site: coup[5 + d, site] if sign is None else coup[5 + d, site] * sign
            )

    def prepare_vectors(x):
        even, odd = vec[x], vec[lx + x]
        high, low = split(jnp.concatenate([even, odd], axis=0).T)
        where = x // 2, lax.rem(x, 2)
        wk[where[0], where[1], 0:nv, :] = high
        wk[where[0], where[1], nv:2 * nv, :] = low
        for y, value in enumerate((even, odd)):
            high, low = split(value)
            wt[x, y, 0:nc, 0:nv] = high[0:nc]
            wt[x, y, 0:nc, nv:2 * nv] = high[nc:2 * nc]
            wt[x, y, nc:2 * nc, 0:nv] = low[0:nc]
            wt[x, y, nc:2 * nc, nv:2 * nv] = low[nc:2 * nc]

    def local_part(it, c):
        field = x0 if it == 0 else x1

        def place(x):
            value = field[c, x]
            mine = masked(value, times_i(value))
            rhs_loc[x, 0:block_k, :] = mine
            rhs_loc[lax.rem(x + lx - 1, lx), block_k:2 * block_k, :] = mine
            rhs_loc[lax.rem(x + 1, lx), 2 * block_k:3 * block_k, :] = mine
            other = jnp.where(first_lanes(value), sooner(value), later(value))
            rhs_loc[x, 3 * block_k:4 * block_k, :] = masked(other, times_i(other))

        loop(0, lx, place)

        def multiply(x):
            acc[c, x] = src[c, x] - fold(dot(m_loc[x], rhs_loc[x]), nc)

        loop(0, lx, multiply)

    def halo_part(it, c, part_of):
        out = r0 if it == 0 else r1

        def body(j):
            x = part_of * (lx // 2) + j
            for slot in range(4):
                halo_copy(it, c, x, slot).wait_recv()
                value = halo[index(it, c), slot, x]
                rhs_halo[slot * block_k:(slot + 1) * block_k, :] = masked(value, times_i(value))
            residual = acc[c, x] - fold(dot(m_halo[x], rhs_halo[...]), nc)
            out[c, x] = residual
            if it == last:
                r1_copy(c, x).start()
            rhs_res[pl.ds(pl.multiple_of(j * block_k, 16), block_k), :] = masked(residual, -times_i(residual))

        loop(0, lx // 2, body)
        total = None
        for j in range(lx // 2):
            x = part_of * (lx // 2) + j
            value = fold(dot(wk[x // 2, x % 2], rhs_res[j * block_k:(j + 1) * block_k, :]), nv)
            total = value if total is None else total + value
        if part_of == 0:
            proj[...] = total
        else:
            total = total + proj[...]
            top, bottom = total[0:packed], total[packed:nv]
            part[index(it, c)] = jnp.where(first_lanes(top), top + sooner(top), bottom + later(bottom))

    def member(q):
        return {"groups": me_g, "space": lax.rem(q, pairs) * 2 + parity, "tm": q // pairs}

    my_rows = pl.multiple_of(parity * half, 8)
    other_rows = pl.multiple_of((1 - parity) * half, 8)
    piece = lax.rem(rank, pieces)
    block = rank - piece
    piece_row = pl.multiple_of(my_rows + piece * rows, 8)

    def core_copy(u):
        return pltpu.make_async_remote_copy(
            src_ref=part.at[u, pl.ds(other_rows, half)],
            dst_ref=core_in.at[u],
            send_sem=core_send.at[u],
            recv_sem=core_recv.at[u],
            device_id=partner,
            device_id_type=MESH,
        )

    def rs_copy(u, o):
        q = lax.rem(rank + o, members)
        row = pl.multiple_of(lax.rem(q, pieces) * rows, 8)
        return pltpu.make_async_remote_copy(
            src_ref=mine.at[u, pl.ds(row, rows)],
            dst_ref=rs_in.at[u, o],
            send_sem=rs_send.at[u, o],
            recv_sem=rs_recv.at[u, o],
            device_id=member(q),
            device_id_type=MESH,
        )

    def ag_copy(u, o):
        q = block + lax.rem(piece + o, pieces)
        return pltpu.make_async_remote_copy(
            src_ref=dfull.at[u, pl.ds(piece_row, rows)],
            dst_ref=dfull.at[u, pl.ds(piece_row, rows)],
            send_sem=ag_send.at[u, o],
            recv_sem=ag_recv.at[u, o],
            device_id=member(q),
            device_id_type=MESH,
        )

    def row_of(o):
        return pl.multiple_of(my_rows + lax.rem(piece + pieces - o, pieces) * rows, 8)

    def relay_copy(u, o):
        return pltpu.make_async_remote_copy(
            src_ref=dfull.at[u, pl.ds(row_of(o), rows)],
            dst_ref=dfull.at[u, pl.ds(row_of(o), rows)],
            send_sem=re_send.at[u, o],
            recv_sem=re_recv.at[u, o],
            device_id=partner,
            device_id_type=MESH,
        )

    def y_copy(c, o):
        return pltpu.make_async_remote_copy(
            src_ref=dfull.at[index(last, c), pl.ds(row_of(o), rows)],
            dst_ref=dother.at[c, pl.ds(row_of(o), rows)],
            send_sem=y_send.at[c, o],
            recv_sem=y_recv.at[c, o],
            device_id=other_group,
            device_id_type=MESH,
        )

    def relay_other(c, o):
        return pltpu.make_async_remote_copy(
            src_ref=dother.at[c, pl.ds(row_of(o), rows)],
            dst_ref=dother.at[c, pl.ds(row_of(o), rows)],
            send_sem=r2_send.at[c, o],
            recv_sem=r2_recv.at[c, o],
            device_id=partner,
            device_id_type=MESH,
        )

    def send_core(it, c):
        core_copy(index(it, c)).start()

    def send_sums(it, c):
        u = index(it, c)
        core_copy(u).wait_recv()
        mine[u] = part[u, pl.ds(my_rows, half), :] + core_in[u]
        loop(1, members, lambda o: rs_copy(u, o).start())

    def send_scaled(it, c):
        u = index(it, c)
        own = mine[u, pl.ds(pl.multiple_of(piece * rows, 8), rows), :]

        def gather(o, total):
            rs_copy(u, o).wait_recv()
            return total + rs_in[u, o]

        coef = lax.fori_loop(1, members, gather, own)
        eigen = eig_t[pl.ds(piece_row, rows), :]
        first = first_lanes(coef)
        real = jnp.where(first, eigen[:, 0:1], eigen[:, 2:3])
        imag = jnp.where(first, eigen[:, 1:2], eigen[:, 3:4])
        dfull[u, pl.ds(piece_row, rows), :] = real * coef + imag * times_i(coef)
        loop(1, pieces, lambda o: ag_copy(u, o).start())
        relay_copy(u, 0).start()
        if it == last:
            y_copy(c, 0).start()

    def relay(it, c):
        u = index(it, c)

        def forward(o):
            ag_copy(u, o).wait_recv()
            relay_copy(u, o).start()
            if it == last:
                y_copy(c, o).start()

        loop(1, pieces, forward)

    def gathered(it, c):
        loop(0, pieces, lambda o: relay_copy(index(it, c), o).wait_recv())

    def fill(even, odd):
        upper = jnp.where(first_lanes(even), even, later(odd))
        lower = jnp.where(first_lanes(even), sooner(even), odd)
        value = jnp.concatenate([upper, lower], axis=0)
        dst[...] = stacked(value, times_i(value))

    def expand(x, y):
        return fold(dot(wt[x, y], dst[...]), nc)

    def update(c):
        u = index(0, c)
        fill(dfull[u], dfull[u])

        def body(x):
            even, odd = expand(x, 0), expand(x, 1)
            x1[c, x] = x0[c, x] + jnp.where(first_lanes(even), even, odd) + 0.5 * r0[c, x]
            send_halo(1, c, x)
            x1_copy(c, x).start()

        loop(0, lx, body)

    def pass_on(c):
        def body(o):
            y_copy(c, o).wait_recv()
            relay_other(c, o).start()

        loop(0, pieces, body)

    def bases(c):
        def body(x):
            x1_copy(c, x).wait_recv()
            r1_copy(c, x).wait_recv()
            own_r, other_r = r1[c, x], r1o[c, x]
            one = groups_of(x1[c, x] + 0.5 * own_r, x1o[c, x] + 0.5 * other_r)
            two = groups_of(own_r, other_r)
            for y in range(2):
                early[c, y * lx + x] = one[y]
                if c == 0:
                    res[y * lx + x, :, 0:width] = two[y]
                else:
                    res[y * lx + x] = join(res[y * lx + x, :, 0:width], two[y])

        loop(0, lx, body)

    def finish(c):
        u = index(last, c)
        loop(0, pieces, lambda o: relay_other(c, o).wait_recv())
        own, other = dfull[u], dother[c]
        fill(jnp.where(me_g == 0, own, other), jnp.where(me_g == 0, other, own))

        def body(x):
            for y in range(2):
                site = y * lx + x
                value = early[c, site] + expand(x, y)
                if c == 0:
                    early[c, site] = value
                else:
                    sol[site] = join(early[0, site], value)

        loop(0, lx, body)

    def begin(c):
        def body(x):
            x0[c, x] = take_pair(c, x, x0f)

        loop(0, lx, body)

    loads[0].wait()
    begin(0)
    pl.semaphore_wait(barrier, total)
    loop(0, lx, lambda x: send_halo(0, 0, x))
    begin(1)
    loop(0, lx, lambda x: send_halo(0, 1, x))

    loads[1].wait()
    loop(0, lx, prepare_matrices)
    loads[2].wait()

    def take_source(x):
        for c in range(CHUNKS):
            src[c, x] = take_pair(c, x, srcf)

    loop(0, lx, take_source)
    local_part(0, 0)
    loads[3].wait()
    rows_of_eigen = jnp.concatenate([eig[:, 0:packed], eig[:, packed:nv]], axis=0)
    eig_t[...] = jnp.concatenate([rows_of_eigen, rows_of_eigen], axis=0).T
    loads[4].wait()
    loop(0, lx, prepare_vectors)
    local_part(0, 1)

    halo_part(0, 0, 0)
    halo_part(0, 0, 1)
    send_core(0, 0)
    send_sums(0, 0)
    halo_part(0, 1, 0)
    send_scaled(0, 0)
    halo_part(0, 1, 1)
    send_core(0, 1)
    relay(0, 0)
    gathered(0, 0)
    update(0)
    send_sums(0, 1)
    local_part(1, 0)
    send_scaled(0, 1)
    relay(0, 1)
    gathered(0, 1)
    update(1)
    local_part(1, 1)
    halo_part(1, 0, 0)
    halo_part(1, 0, 1)
    send_core(1, 0)
    send_sums(1, 0)
    halo_part(1, 1, 0)
    send_scaled(1, 0)
    halo_part(1, 1, 1)
    send_core(1, 1)
    relay(1, 0)
    send_sums(1, 1)
    gathered(1, 0)
    pass_on(0)
    bases(0)
    finish(0)
    send_scaled(1, 1)
    bases(1)
    relay(1, 1)
    gathered(1, 1)
    pass_on(1)
    finish(1)

    for it in range(ITERS):
        for c in range(CHUNKS):
            u = index(it, c)
            core_copy(u).wait_send()
            loop(1, members, lambda o: rs_copy(u, o).wait_send())
            loop(1, pieces, lambda o: ag_copy(u, o).wait_send())
            loop(0, pieces, lambda o: relay_copy(u, o).wait_send())

            def drain(x):
                for slot in range(4):
                    halo_copy(it, c, x, slot).wait_send()
                if it == last:
                    x1_copy(c, x).wait_send()
                    r1_copy(c, x).wait_send()

            loop(0, lx, drain)

    for c in range(CHUNKS):
        def drain_y(o):
            y_copy(c, o).wait_send()
            relay_other(c, o).wait_send()

        loop(0, pieces, drain_y)


def solve(mesh, couplings, source, initial, vectors, inverse_eigen):
    nine, _, _, ly, lx, nc, _ = couplings.shape
    full = source.shape[-1]
    nv = vectors.shape[0]
    D = Dims(mesh, ly, lx, nc, full, nv)
    sites, width = D.sites, D.width
    field = (sites, nc, full)
    mine = (CHUNKS, lx, nc, width)
    units = ITERS * CHUNKS
    block_k = ly * 2 * nc
    vecs = vectors.reshape(nv, sites, 2 * nc).transpose(1, 2, 0)
    any_spec = pl.BlockSpec(memory_space=pl.ANY)
    vmem = pl.BlockSpec(memory_space=pltpu.VMEM)
    dma = pltpu.SemaphoreType.DMA
    out = jax.ShapeDtypeStruct(field, F32)
    x, r = pl.pallas_call(
        functools.partial(kernel, D),
        out_shape=(out, out),
        in_specs=[any_spec] * 5,
        out_specs=(vmem, vmem),
        scratch_shapes=[
            pltpu.VMEM((nine, sites, nc, 2 * nc), F32),
            pltpu.VMEM(field, F32),
            pltpu.VMEM(field, F32),
            pltpu.VMEM((sites, 2 * nc, nv), F32),
            pltpu.VMEM((2, nv), F32),
            dma((5,)),
        ]
        + [pltpu.VMEM(mine, F32)] * 8
        + [
            pltpu.VMEM((CHUNKS, sites, nc, width), F32),
            pltpu.VMEM((lx, 2 * nc, 4 * block_k), BF16),
            pltpu.VMEM((lx, 2 * nc, 4 * block_k), BF16),
            pltpu.VMEM((lx // 2, 2, 2 * nv, block_k), BF16),
            pltpu.VMEM((lx, ly, 2 * nc, 2 * nv), BF16),
            pltpu.VMEM((lx, 4 * block_k, 2 * width), BF16),
            pltpu.VMEM((4 * block_k, 2 * width), BF16),
            pltpu.VMEM((lx // 2 * block_k, 2 * width), BF16),
            pltpu.VMEM((2 * nv, 2 * width), BF16),
            pltpu.VMEM((nv, width), F32),
            pltpu.VMEM((units, 4, lx, nc, width), F32),
            pltpu.VMEM((units, D.packed, width), F32),
            pltpu.VMEM((units, D.half, width), F32),
            pltpu.VMEM((units, D.half, width), F32),
            pltpu.VMEM((units, D.members, D.rows, width), F32),
            pltpu.VMEM((units, D.packed, width), F32),
            pltpu.VMEM((CHUNKS, D.packed, width), F32),
            pltpu.VMEM((D.packed, 8), F32),
            dma((units, 4, lx)),
            dma((units, 4, lx)),
            dma((units,)),
            dma((units,)),
            dma((units, D.members)),
            dma((units, D.members)),
            dma((units, D.pieces)),
            dma((units, D.pieces)),
            dma((units, D.pieces)),
            dma((units, D.pieces)),
            dma((CHUNKS, D.pieces)),
            dma((CHUNKS, D.pieces)),
            dma((CHUNKS, lx)),
            dma((CHUNKS, lx)),
            dma((CHUNKS, lx)),
            dma((CHUNKS, lx)),
            dma((CHUNKS, D.pieces)),
            dma((CHUNKS, D.pieces)),
        ],
        compiler_params=pltpu.CompilerParams(
            collective_id=0, has_side_effects=True, vmem_limit_bytes=56 * 1024 * 1024
        ),
    )(
        couplings.reshape(nine, sites, nc, 2 * nc),
        source.reshape(field),
        initial.reshape(field),
        vecs,
        inverse_eigen,
    )
    return x.reshape(source.shape), r.reshape(source.shape)


def solution(mesh):
    in_specs = (
        P(None, "tm", "space", None, None, None, None),
        P("tm", "space", None, None, None, None),
        P("tm", "space", None, None, None, None),
        P(None, "tm", "space", None, None, None),
        P(),
    )
    out_specs = (
        P(("groups", "tm"), "space", None, None, None, None),
        P(("groups", "tm"), "space", None, None, None, None),
    )
    return jax.shard_map(
        functools.partial(solve, mesh), mesh=mesh, in_specs=in_specs, out_specs=out_specs, check_vma=False
    )
```

```python
import functools

import jax
import jax.numpy as jnp
from jax import lax
from jax.experimental import pallas as pl
from jax.experimental.pallas import tpu as pltpu
from jax.sharding import PartitionSpec as P

ITERS = 2
MESH = pl.DeviceIdType.MESH
F32 = jnp.float32
BF16 = jnp.bfloat16


def split(value):
    high = value.astype(BF16)
    low = (value - high.astype(F32)).astype(BF16)
    return high, low


def dot(a, b):
    return jnp.dot(a, b, preferred_element_type=F32)


class Dims:
    def __init__(self, mesh, ly, lx, nc, full, nv):
        self.ng, self.ns, self.nt = mesh.shape["groups"], mesh.shape["space"], mesh.shape["tm"]
        self.ly, self.lx, self.nc, self.full, self.nv = ly, lx, nc, full, nv
        assert self.ng == 2 and ly == 2 and lx % 2 == 0
        self.width = full // 2
        self.sites = ly * lx
        self.members = self.ns // 2 * self.nt
        self.packed = nv // 2
        self.half = self.packed // 2
        self.pieces = min(self.members, self.half // 8)
        self.rows = self.half // self.pieces


CHUNKS = 2


def kernel(
    D, coup_h, src_h, x0_h, vec_h, eig_h, sol, res,
    coup, srcf, x0f, vec, eig, local_sem,
    x0, x1, r0, r1, src, x1o, r1o, acc, early,
    m_loc, m_halo, wk, wt, rhs_loc, rhs_halo, rhs_res, dst, proj,
    halo, part, core_in, mine, rs_in, dfull, dother, eig_t,
    halo_send, halo_recv, core_send, core_recv, rs_send, rs_recv, ag_send, ag_recv, re_send, re_recv,
    y_send, y_recv, yx_send, yx_recv, yr_send, yr_recv, r2_send, r2_recv,
):
    ns, nt, sites, nc, lx, ly = D.ns, D.nt, D.sites, D.nc, D.lx, D.ly
    nv, packed, half, rows, pieces, members = D.nv, D.packed, D.half, D.rows, D.pieces, D.members
    width, full = D.width, D.full
    quarter = width // 4
    me_g, me_s, me_t = lax.axis_index("groups"), lax.axis_index("space"), lax.axis_index("tm")
    parity = lax.rem(me_s, 2)
    pairs = ns // 2
    rank = me_t * pairs + me_s // 2
    partner = {"groups": me_g, "space": me_s + 1 - 2 * parity, "tm": me_t}
    other_group = {"groups": 1 - me_g, "space": me_s, "tm": me_t}
    last = ITERS - 1
    block_k = ly * 2 * nc

    loads = [
        pltpu.make_async_copy(x0_h, x0f, local_sem.at[0]),
        pltpu.make_async_copy(coup_h, coup, local_sem.at[1]),
        pltpu.make_async_copy(src_h, srcf, local_sem.at[2]),
        pltpu.make_async_copy(eig_h, eig, local_sem.at[3]),
        pltpu.make_async_copy(vec_h, vec, local_sem.at[4]),
    ]
    for load in loads:
        load.start()

    barrier = pltpu.get_barrier_semaphore()
    total = ns * nt
    flat = me_t * ns + me_s

    def greet(o, carry):
        other = lax.rem(flat + o, total)
        pl.semaphore_signal(
            barrier, inc=1,
            device_id={"groups": me_g, "space": lax.rem(other, ns), "tm": other // ns}, device_id_type=MESH,
        )
        return carry

    lax.fori_loop(1, total, greet, 0)
    pl.semaphore_signal(barrier, inc=1, device_id=other_group, device_id_type=MESH)

    def lane(shape):
        return lax.broadcasted_iota(jnp.int32, shape, 1)

    def turn(v):
        return pltpu.roll(v, width // 2, 1)

    def later(v):
        return pltpu.roll(v, quarter, 1)

    def sooner(v):
        return pltpu.roll(v, width - quarter, 1)

    def real_lanes(v):
        return lane(v.shape) < width // 2

    def first_lanes(v):
        return lax.rem(lane(v.shape), width // 2) < quarter

    def times_i(v):
        turned = turn(v)
        return jnp.where(real_lanes(v), -turned, turned)

    def pack(even, odd):
        return jnp.where(first_lanes(even), even, later(odd)), jnp.where(first_lanes(even), sooner(even), odd)

    def take(c, value):
        re, im = value[:, 0:width], value[:, width:full]
        if c == 0:
            return jnp.where(real_lanes(re), re, turn(im))
        return jnp.where(real_lanes(re), turn(re), im)

    def take_pair(c, x, ref):
        of_g0, of_g1 = pack(take(c, ref[x]), take(c, ref[lx + x]))
        return jnp.where(me_g == 0, of_g0, of_g1)

    def groups_of(own, other):
        return pack(jnp.where(me_g == 0, own, other), jnp.where(me_g == 0, other, own))

    def join(c0, c1):
        return jnp.concatenate(
            [jnp.where(real_lanes(c0), c0, turn(c1)), jnp.where(real_lanes(c0), turn(c0), c1)], axis=1
        )

    def stacked(value, turned):
        high, low = split(value)
        t_high, t_low = split(turned)
        return jnp.concatenate(
            [jnp.concatenate([high, t_high], axis=0), jnp.concatenate([low, t_low], axis=0)], axis=1
        )

    keep = jnp.where(lax.rem(lane((2 * nc, 2 * width)), width // 2) < quarter, 1.0, 0.0).astype(BF16)

    def masked(value, turned):
        both = stacked(value, turned)
        even = both * keep
        return jnp.concatenate([even, both - even], axis=0)

    def fold(out, count):
        top, bottom = out[0:count], out[count:2 * count]
        return (top[:, 0:width] + top[:, width:2 * width]) + (bottom[:, 0:width] + bottom[:, width:2 * width])

    up_s, down_s = lax.rem(me_s + 1, ns), lax.rem(me_s + ns - 1, ns)
    up_t, down_t = lax.rem(me_t + 1, nt), lax.rem(me_t + nt - 1, nt)
    targets = (
        (2, {"groups": me_g, "space": me_s, "tm": down_t}),
        (3, {"groups": me_g, "space": me_s, "tm": up_t}),
        (0, {"groups": me_g, "space": down_s, "tm": me_t}),
        (1, {"groups": me_g, "space": up_s, "tm": me_t}),
    )
    target_of = dict(targets)

    def index(it, c):
        return it * CHUNKS + c

    def halo_copy(it, c, x, slot):
        source = x0 if it == 0 else x1
        u = index(it, c)
        return pltpu.make_async_remote_copy(
            src_ref=source.at[c, x],
            dst_ref=halo.at[u, slot, x],
            send_sem=halo_send.at[u, slot, x],
            recv_sem=halo_recv.at[u, slot, x],
            device_id=target_of[slot],
            device_id_type=MESH,
        )

    def send_halo(it, c, x):
        for slot, _ in targets:
            halo_copy(it, c, x, slot).start()

    def x1_copy(c, x):
        return pltpu.make_async_remote_copy(
            src_ref=x1.at[c, x], dst_ref=x1o.at[c, x], send_sem=yx_send.at[c, x], recv_sem=yx_recv.at[c, x],
            device_id=other_group, device_id_type=MESH,
        )

    def r1_copy(c, x):
        return pltpu.make_async_remote_copy(
            src_ref=r1.at[c, x], dst_ref=r1o.at[c, x], send_sem=yr_send.at[c, x], recv_sem=yr_recv.at[c, x],
            device_id=other_group, device_id_type=MESH,
        )

    def loop(start, stop, action):
        def body(o, carry):
            action(o)
            return carry

        lax.fori_loop(start, stop, body, 0)

    sign_up = jnp.where(me_t == nt - 1, -1.0, 1.0).astype(F32)
    sign_down = jnp.where(me_t == 0, -1.0, 1.0).astype(F32)

    def prepare_matrices(x):
        def both(value_of):
            high, low = split(jnp.concatenate([value_of(x), value_of(lx + x)], axis=1))
            return jnp.concatenate([high, low], axis=0)

        for d in range(3):
            m_loc[x, :, d * block_k:(d + 1) * block_k] = both(lambda site: coup[d, site])
        m_loc[x, :, 3 * block_k:4 * block_k] = both(lambda site: coup[3, site] + coup[4, site])
        for d, sign in enumerate((None, None, sign_up, sign_down)):
            m_halo[x, :, d * block_k:(d + 1) * block_k] = both(
                lambda site: coup[5 + d, site] if sign is None else coup[5 + d, site] * sign
            )

    def prepare_vectors(x):
        even, odd = vec[x], vec[lx + x]
        high, low = split(jnp.concatenate([even, odd], axis=0).T)
        where = x // 2, lax.rem(x, 2)
        wk[where[0], where[1], 0:nv, :] = high
        wk[where[0], where[1], nv:2 * nv, :] = low
        for y, value in enumerate((even, odd)):
            high, low = split(value)
            wt[x, y, 0:nc, 0:nv] = high[0:nc]
            wt[x, y, 0:nc, nv:2 * nv] = high[nc:2 * nc]
            wt[x, y, nc:2 * nc, 0:nv] = low[0:nc]
            wt[x, y, nc:2 * nc, nv:2 * nv] = low[nc:2 * nc]

    def local_part(it, c):
        field = x0 if it == 0 else x1

        def place(x):
            value = field[c, x]
            mine = masked(value, times_i(value))
            rhs_loc[x, 0:block_k, :] = mine
            rhs_loc[lax.rem(x + lx - 1, lx), block_k:2 * block_k, :] = mine
            rhs_loc[lax.rem(x + 1, lx), 2 * block_k:3 * block_k, :] = mine
            other = jnp.where(first_lanes(value), sooner(value), later(value))
            rhs_loc[x, 3 * block_k:4 * block_k, :] = masked(other, times_i(other))

        loop(0, lx, place)

        def multiply(x):
            acc[c, x] = src[c, x] - fold(dot(m_loc[x], rhs_loc[x]), nc)

        loop(0, lx, multiply)

    def halo_part(it, c, part_of):
        out = r0 if it == 0 else r1

        def body(j):
            x = part_of * (lx // 2) + j
            for slot in range(4):
                halo_copy(it, c, x, slot).wait_recv()
                value = halo[index(it, c), slot, x]
                rhs_halo[slot * block_k:(slot + 1) * block_k, :] = masked(value, times_i(value))
            residual = acc[c, x] - fold(dot(m_halo[x], rhs_halo[...]), nc)
            out[c, x] = residual
            if it == last:
                r1_copy(c, x).start()
            rhs_res[pl.ds(pl.multiple_of(j * block_k, 16), block_k), :] = masked(residual, -times_i(residual))

        loop(0, lx // 2, body)
        total = None
        for j in range(lx // 2):
            x = part_of * (lx // 2) + j
            value = fold(dot(wk[x // 2, x % 2], rhs_res[j * block_k:(j + 1) * block_k, :]), nv)
            total = value if total is None else total + value
        if part_of == 0:
            proj[...] = total
        else:
            total = total + proj[...]
            top, bottom = total[0:packed], total[packed:nv]
            part[index(it, c)] = jnp.where(first_lanes(top), top + sooner(top), bottom + later(bottom))

    def member(q):
        return {"groups": me_g, "space": lax.rem(q, pairs) * 2 + parity, "tm": q // pairs}

    my_rows = pl.multiple_of(parity * half, 8)
    other_rows = pl.multiple_of((1 - parity) * half, 8)
    piece = lax.rem(rank, pieces)
    block = rank - piece
    piece_row = pl.multiple_of(my_rows + piece * rows, 8)

    def core_copy(u):
        return pltpu.make_async_remote_copy(
            src_ref=part.at[u, pl.ds(other_rows, half)],
            dst_ref=core_in.at[u],
            send_sem=core_send.at[u],
            recv_sem=core_recv.at[u],
            device_id=partner,
            device_id_type=MESH,
        )

    def rs_copy(u, o):
        q = lax.rem(rank + o, members)
        row = pl.multiple_of(lax.rem(q, pieces) * rows, 8)
        return pltpu.make_async_remote_copy(
            src_ref=mine.at[u, pl.ds(row, rows)],
            dst_ref=rs_in.at[u, o],
            send_sem=rs_send.at[u, o],
            recv_sem=rs_recv.at[u, o],
            device_id=member(q),
            device_id_type=MESH,
        )

    def ag_copy(u, o):
        q = block + lax.rem(piece + o, pieces)
        return pltpu.make_async_remote_copy(
            src_ref=dfull.at[u, pl.ds(piece_row, rows)],
            dst_ref=dfull.at[u, pl.ds(piece_row, rows)],
            send_sem=ag_send.at[u, o],
            recv_sem=ag_recv.at[u, o],
            device_id=member(q),
            device_id_type=MESH,
        )

    def row_of(o):
        return pl.multiple_of(my_rows + lax.rem(piece + pieces - o, pieces) * rows, 8)

    def relay_copy(u, o):
        return pltpu.make_async_remote_copy(
            src_ref=dfull.at[u, pl.ds(row_of(o), rows)],
            dst_ref=dfull.at[u, pl.ds(row_of(o), rows)],
            send_sem=re_send.at[u, o],
            recv_sem=re_recv.at[u, o],
            device_id=partner,
            device_id_type=MESH,
        )

    def y_copy(c, o):
        return pltpu.make_async_remote_copy(
            src_ref=dfull.at[index(last, c), pl.ds(row_of(o), rows)],
            dst_ref=dother.at[c, pl.ds(row_of(o), rows)],
            send_sem=y_send.at[c, o],
            recv_sem=y_recv.at[c, o],
            device_id=other_group,
            device_id_type=MESH,
        )

    def relay_other(c, o):
        return pltpu.make_async_remote_copy(
            src_ref=dother.at[c, pl.ds(row_of(o), rows)],
            dst_ref=dother.at[c, pl.ds(row_of(o), rows)],
            send_sem=r2_send.at[c, o],
            recv_sem=r2_recv.at[c, o],
            device_id=partner,
            device_id_type=MESH,
        )

    def send_core(it, c):
        core_copy(index(it, c)).start()

    def send_sums(it, c):
        u = index(it, c)
        core_copy(u).wait_recv()
        mine[u] = part[u, pl.ds(my_rows, half), :] + core_in[u]
        loop(1, members, lambda o: rs_copy(u, o).start())

    def send_scaled(it, c):
        u = index(it, c)
        own = mine[u, pl.ds(pl.multiple_of(piece * rows, 8), rows), :]

        def gather(o, total):
            rs_copy(u, o).wait_recv()
            return total + rs_in[u, o]

        coef = lax.fori_loop(1, members, gather, own)
        eigen = eig_t[pl.ds(piece_row, rows), :]
        first = first_lanes(coef)
        real = jnp.where(first, eigen[:, 0:1], eigen[:, 2:3])
        imag = jnp.where(first, eigen[:, 1:2], eigen[:, 3:4])
        dfull[u, pl.ds(piece_row, rows), :] = real * coef + imag * times_i(coef)
        loop(1, pieces, lambda o: ag_copy(u, o).start())
        relay_copy(u, 0).start()
        if it == last:
            y_copy(c, 0).start()

    def relay(it, c):
        u = index(it, c)

        def forward(o):
            ag_copy(u, o).wait_recv()
            relay_copy(u, o).start()
            if it == last:
                y_copy(c, o).start()

        loop(1, pieces, forward)

    def gathered(it, c):
        loop(0, pieces, lambda o: relay_copy(index(it, c), o).wait_recv())

    def fill(even, odd):
        upper = jnp.where(first_lanes(even), even, later(odd))
        lower = jnp.where(first_lanes(even), sooner(even), odd)
        value = jnp.concatenate([upper, lower], axis=0)
        dst[...] = stacked(value, times_i(value))

    def expand(x, y):
        return fold(dot(wt[x, y], dst[...]), nc)

    def update(c):
        u = index(0, c)
        fill(dfull[u], dfull[u])

        def body(x):
            even, odd = expand(x, 0), expand(x, 1)
            x1[c, x] = x0[c, x] + jnp.where(first_lanes(even), even, odd) + 0.5 * r0[c, x]
            x1_copy(c, x).start()

        def first(x):
            body(x)
            send_halo(1, c, x)

        loop(0, lx // 2, first)
        loop(lx // 2, lx, body)

    def pass_on(c):
        def body(o):
            y_copy(c, o).wait_recv()
            relay_other(c, o).start()

        loop(0, pieces, body)

    def bases(c):
        def body(x):
            x1_copy(c, x).wait_recv()
            r1_copy(c, x).wait_recv()
            own_r, other_r = r1[c, x], r1o[c, x]
            one = groups_of(x1[c, x] + 0.5 * own_r, x1o[c, x] + 0.5 * other_r)
            two = groups_of(own_r, other_r)
            for y in range(2):
                early[c, y * lx + x] = one[y]
                if c == 0:
                    res[y * lx + x, :, 0:width] = two[y]
                else:
                    res[y * lx + x] = join(res[y * lx + x, :, 0:width], two[y])

        loop(0, lx, body)

    def finish(c):
        u = index(last, c)
        loop(0, pieces, lambda o: relay_other(c, o).wait_recv())
        own, other = dfull[u], dother[c]
        fill(jnp.where(me_g == 0, own, other), jnp.where(me_g == 0, other, own))

        def body(x):
            for y in range(2):
                site = y * lx + x
                value = early[c, site] + expand(x, y)
                if c == 0:
                    early[c, site] = value
                else:
                    sol[site] = join(early[0, site], value)

        loop(0, lx, body)

    def begin(c):
        def body(x):
            x0[c, x] = take_pair(c, x, x0f)

        loop(0, lx, body)

    def send_pairs(it, c, start, stop):
        loop(start, stop, lambda x: send_halo(it, c, x))

    some = lx // 2
    loads[0].wait()
    begin(0)
    pl.semaphore_wait(barrier, total)
    send_pairs(0, 0, 0, lx)
    begin(1)
    send_pairs(0, 1, 0, some)

    loads[1].wait()
    loop(0, lx, prepare_matrices)
    loads[2].wait()

    def take_source(x):
        for c in range(CHUNKS):
            src[c, x] = take_pair(c, x, srcf)

    loop(0, lx, take_source)
    local_part(0, 0)
    loads[3].wait()
    rows_of_eigen = jnp.concatenate([eig[:, 0:packed], eig[:, packed:nv]], axis=0)
    eig_t[...] = jnp.concatenate([rows_of_eigen, rows_of_eigen], axis=0).T
    loads[4].wait()
    loop(0, lx, prepare_vectors)
    local_part(0, 1)

    halo_part(0, 0, 0)
    halo_part(0, 0, 1)
    send_core(0, 0)
    send_sums(0, 0)
    send_pairs(0, 1, some, lx)
    halo_part(0, 1, 0)
    send_scaled(0, 0)
    halo_part(0, 1, 1)
    send_core(0, 1)
    relay(0, 0)
    send_sums(0, 1)
    gathered(0, 0)
    update(0)
    local_part(1, 0)
    send_scaled(0, 1)
    send_pairs(1, 0, some, lx)
    halo_part(1, 0, 0)
    relay(0, 1)
    gathered(0, 1)
    update(1)
    local_part(1, 1)
    halo_part(1, 0, 1)
    send_core(1, 0)
    send_sums(1, 0)
    send_pairs(1, 1, some, lx)
    halo_part(1, 1, 0)
    send_scaled(1, 0)
    halo_part(1, 1, 1)
    send_core(1, 1)
    relay(1, 0)
    send_sums(1, 1)
    gathered(1, 0)
    pass_on(0)
    bases(0)
    finish(0)
    send_scaled(1, 1)
    bases(1)
    relay(1, 1)
    gathered(1, 1)
    pass_on(1)
    finish(1)

    for it in range(ITERS):
        for c in range(CHUNKS):
            u = index(it, c)
            core_copy(u).wait_send()
            loop(1, members, lambda o: rs_copy(u, o).wait_send())
            loop(1, pieces, lambda o: ag_copy(u, o).wait_send())
            loop(0, pieces, lambda o: relay_copy(u, o).wait_send())

            def drain(x):
                for slot in range(4):
                    halo_copy(it, c, x, slot).wait_send()
                if it == last:
                    x1_copy(c, x).wait_send()
                    r1_copy(c, x).wait_send()

            loop(0, lx, drain)

    for c in range(CHUNKS):
        def drain_y(o):
            y_copy(c, o).wait_send()
            relay_other(c, o).wait_send()

        loop(0, pieces, drain_y)


def solve(mesh, couplings, source, initial, vectors, inverse_eigen):
    nine, _, _, ly, lx, nc, _ = couplings.shape
    full = source.shape[-1]
    nv = vectors.shape[0]
    D = Dims(mesh, ly, lx, nc, full, nv)
    sites, width = D.sites, D.width
    field = (sites, nc, full)
    mine = (CHUNKS, lx, nc, width)
    units = ITERS * CHUNKS
    block_k = ly * 2 * nc
    vecs = vectors.reshape(nv, sites, 2 * nc).transpose(1, 2, 0)
    any_spec = pl.BlockSpec(memory_space=pl.ANY)
    vmem = pl.BlockSpec(memory_space=pltpu.VMEM)
    dma = pltpu.SemaphoreType.DMA
    out = jax.ShapeDtypeStruct(field, F32)
    x, r = pl.pallas_call(
        functools.partial(kernel, D),
        out_shape=(out, out),
        in_specs=[any_spec] * 5,
        out_specs=(vmem, vmem),
        scratch_shapes=[
            pltpu.VMEM((nine, sites, nc, 2 * nc), F32),
            pltpu.VMEM(field, F32),
            pltpu.VMEM(field, F32),
            pltpu.VMEM((sites, 2 * nc, nv), F32),
            pltpu.VMEM((2, nv), F32),
            dma((5,)),
        ]
        + [pltpu.VMEM(mine, F32)] * 8
        + [
            pltpu.VMEM((CHUNKS, sites, nc, width), F32),
            pltpu.VMEM((lx, 2 * nc, 4 * block_k), BF16),
            pltpu.VMEM((lx, 2 * nc, 4 * block_k), BF16),
            pltpu.VMEM((lx // 2, 2, 2 * nv, block_k), BF16),
            pltpu.VMEM((lx, ly, 2 * nc, 2 * nv), BF16),
            pltpu.VMEM((lx, 4 * block_k, 2 * width), BF16),
            pltpu.VMEM((4 * block_k, 2 * width), BF16),
            pltpu.VMEM((lx // 2 * block_k, 2 * width), BF16),
            pltpu.VMEM((2 * nv, 2 * width), BF16),
            pltpu.VMEM((nv, width), F32),
            pltpu.VMEM((units, 4, lx, nc, width), F32),
            pltpu.VMEM((units, D.packed, width), F32),
            pltpu.VMEM((units, D.half, width), F32),
            pltpu.VMEM((units, D.half, width), F32),
            pltpu.VMEM((units, D.members, D.rows, width), F32),
            pltpu.VMEM((units, D.packed, width), F32),
            pltpu.VMEM((CHUNKS, D.packed, width), F32),
            pltpu.VMEM((D.packed, 8), F32),
            dma((units, 4, lx)),
            dma((units, 4, lx)),
            dma((units,)),
            dma((units,)),
            dma((units, D.members)),
            dma((units, D.members)),
            dma((units, D.pieces)),
            dma((units, D.pieces)),
            dma((units, D.pieces)),
            dma((units, D.pieces)),
            dma((CHUNKS, D.pieces)),
            dma((CHUNKS, D.pieces)),
            dma((CHUNKS, lx)),
            dma((CHUNKS, lx)),
            dma((CHUNKS, lx)),
            dma((CHUNKS, lx)),
            dma((CHUNKS, D.pieces)),
            dma((CHUNKS, D.pieces)),
        ],
        compiler_params=pltpu.CompilerParams(
            collective_id=0, has_side_effects=True, vmem_limit_bytes=52 * 1024 * 1024
        ),
    )(
        couplings.reshape(nine, sites, nc, 2 * nc),
        source.reshape(field),
        initial.reshape(field),
        vecs,
        inverse_eigen,
    )
    return x.reshape(source.shape), r.reshape(source.shape)


def solution(mesh):
    in_specs = (
        P(None, "tm", "space", None, None, None, None),
        P("tm", "space", None, None, None, None),
        P("tm", "space", None, None, None, None),
        P(None, "tm", "space", None, None, None),
        P(),
    )
    out_specs = (
        P(("groups", "tm"), "space", None, None, None, None),
        P(("groups", "tm"), "space", None, None, None, None),
    )
    return jax.shard_map(
        functools.partial(solve, mesh), mesh=mesh, in_specs=in_specs, out_specs=out_specs, check_vma=False
    )
```

```python
import functools

import jax
import jax.numpy as jnp
from jax import lax
from jax.experimental import pallas as pl
from jax.experimental.pallas import tpu as pltpu
from jax.sharding import PartitionSpec as P

ITERS = 2
MESH = pl.DeviceIdType.MESH
F32 = jnp.float32
BF16 = jnp.bfloat16


def split(value):
    high = value.astype(BF16)
    low = (value - high.astype(F32)).astype(BF16)
    return high, low


def dot(a, b):
    return jnp.dot(a, b, preferred_element_type=F32)


class Dims:
    def __init__(self, mesh, ly, lx, nc, full, nv):
        self.ng, self.ns, self.nt = mesh.shape["groups"], mesh.shape["space"], mesh.shape["tm"]
        self.ly, self.lx, self.nc, self.full, self.nv = ly, lx, nc, full, nv
        assert self.ng == 2 and ly == 2 and lx % 2 == 0
        self.width = full // 2
        self.sites = ly * lx
        self.members = self.ns // 2 * self.nt
        self.packed = nv // 2
        self.half = self.packed // 2
        self.pieces = min(self.members, self.half // 8)
        self.rows = self.half // self.pieces


CHUNKS = 2


def kernel(
    D, coup_h, src_h, x0_h, vec_h, eig_h, sol, res,
    coup, srcf, x0f, vec, eig, local_sem,
    x0, x1, r0, r1, src, x1o, r1o, acc, early,
    m_loc, m_halo, wk, wt, rhs_loc, rhs_halo, rhs_res, dst, proj,
    halo, part, core_in, mine, rs_in, dfull, dother, eig_t,
    halo_send, halo_recv, core_send, core_recv, rs_send, rs_recv, ag_send, ag_recv, re_send, re_recv,
    y_send, y_recv, yx_send, yx_recv, yr_send, yr_recv, r2_send, r2_recv,
):
    ns, nt, sites, nc, lx, ly = D.ns, D.nt, D.sites, D.nc, D.lx, D.ly
    nv, packed, half, rows, pieces, members = D.nv, D.packed, D.half, D.rows, D.pieces, D.members
    width, full = D.width, D.full
    quarter = width // 4
    me_g, me_s, me_t = lax.axis_index("groups"), lax.axis_index("space"), lax.axis_index("tm")
    parity = lax.rem(me_s, 2)
    pairs = ns // 2
    rank = me_t * pairs + me_s // 2
    partner = {"groups": me_g, "space": me_s + 1 - 2 * parity, "tm": me_t}
    other_group = {"groups": 1 - me_g, "space": me_s, "tm": me_t}
    last = ITERS - 1
    block_k = ly * 2 * nc

    loads = [
        pltpu.make_async_copy(x0_h, x0f, local_sem.at[0]),
        pltpu.make_async_copy(coup_h, coup, local_sem.at[1]),
        pltpu.make_async_copy(src_h, srcf, local_sem.at[2]),
        pltpu.make_async_copy(eig_h, eig, local_sem.at[3]),
        pltpu.make_async_copy(vec_h, vec, local_sem.at[4]),
    ]
    for load in loads:
        load.start()

    barrier = pltpu.get_barrier_semaphore()
    total = ns * nt
    flat = me_t * ns + me_s

    def greet(o, carry):
        other = lax.rem(flat + o, total)
        pl.semaphore_signal(
            barrier, inc=1,
            device_id={"groups": me_g, "space": lax.rem(other, ns), "tm": other // ns}, device_id_type=MESH,
        )
        return carry

    lax.fori_loop(1, total, greet, 0)
    pl.semaphore_signal(barrier, inc=1, device_id=other_group, device_id_type=MESH)

    def lane(shape):
        return lax.broadcasted_iota(jnp.int32, shape, 1)

    def turn(v):
        return pltpu.roll(v, width // 2, 1)

    def later(v):
        return pltpu.roll(v, quarter, 1)

    def sooner(v):
        return pltpu.roll(v, width - quarter, 1)

    def real_lanes(v):
        return lane(v.shape) < width // 2

    def first_lanes(v):
        return lax.rem(lane(v.shape), width // 2) < quarter

    def times_i(v):
        turned = turn(v)
        return jnp.where(real_lanes(v), -turned, turned)

    def pack(even, odd):
        return jnp.where(first_lanes(even), even, later(odd)), jnp.where(first_lanes(even), sooner(even), odd)

    def take(c, value):
        re, im = value[:, 0:width], value[:, width:full]
        if c == 0:
            return jnp.where(real_lanes(re), re, turn(im))
        return jnp.where(real_lanes(re), turn(re), im)

    def take_pair(c, x, ref):
        of_g0, of_g1 = pack(take(c, ref[x]), take(c, ref[lx + x]))
        return jnp.where(me_g == 0, of_g0, of_g1)

    def groups_of(own, other):
        return pack(jnp.where(me_g == 0, own, other), jnp.where(me_g == 0, other, own))

    def join(c0, c1):
        return jnp.concatenate(
            [jnp.where(real_lanes(c0), c0, turn(c1)), jnp.where(real_lanes(c0), turn(c0), c1)], axis=1
        )

    def stacked(value, turned):
        high, low = split(value)
        t_high, t_low = split(turned)
        return jnp.concatenate(
            [jnp.concatenate([high, t_high], axis=0), jnp.concatenate([low, t_low], axis=0)], axis=1
        )

    keep = jnp.where(lax.rem(lane((2 * nc, 2 * width)), width // 2) < quarter, 1.0, 0.0).astype(BF16)

    def masked(value, turned):
        both = stacked(value, turned)
        even = both * keep
        return jnp.concatenate([even, both - even], axis=0)

    def fold(out, count):
        top, bottom = out[0:count], out[count:2 * count]
        return (top[:, 0:width] + top[:, width:2 * width]) + (bottom[:, 0:width] + bottom[:, width:2 * width])

    up_s, down_s = lax.rem(me_s + 1, ns), lax.rem(me_s + ns - 1, ns)
    up_t, down_t = lax.rem(me_t + 1, nt), lax.rem(me_t + nt - 1, nt)
    targets = (
        (2, {"groups": me_g, "space": me_s, "tm": down_t}),
        (3, {"groups": me_g, "space": me_s, "tm": up_t}),
        (0, {"groups": me_g, "space": down_s, "tm": me_t}),
        (1, {"groups": me_g, "space": up_s, "tm": me_t}),
    )
    target_of = dict(targets)

    def index(it, c):
        return it * CHUNKS + c

    def halo_copy(it, c, x, slot):
        source = x0 if it == 0 else x1
        u = index(it, c)
        return pltpu.make_async_remote_copy(
            src_ref=source.at[c, x],
            dst_ref=halo.at[u, slot, x],
            send_sem=halo_send.at[u, slot, x],
            recv_sem=halo_recv.at[u, slot, x],
            device_id=target_of[slot],
            device_id_type=MESH,
        )

    def send_halo(it, c, x):
        for slot, _ in targets:
            halo_copy(it, c, x, slot).start()

    def x1_copy(c, x):
        return pltpu.make_async_remote_copy(
            src_ref=x1.at[c, x], dst_ref=x1o.at[c, x], send_sem=yx_send.at[c, x], recv_sem=yx_recv.at[c, x],
            device_id=other_group, device_id_type=MESH,
        )

    def r1_copy(c, x):
        return pltpu.make_async_remote_copy(
            src_ref=r1.at[c, x], dst_ref=r1o.at[c, x], send_sem=yr_send.at[c, x], recv_sem=yr_recv.at[c, x],
            device_id=other_group, device_id_type=MESH,
        )

    def loop(start, stop, action):
        def body(o, carry):
            action(o)
            return carry

        lax.fori_loop(start, stop, body, 0)

    sign_up = jnp.where(me_t == nt - 1, -1.0, 1.0).astype(F32)
    sign_down = jnp.where(me_t == 0, -1.0, 1.0).astype(F32)

    def prepare_matrices(x):
        def both(value_of):
            high, low = split(jnp.concatenate([value_of(x), value_of(lx + x)], axis=1))
            return jnp.concatenate([high, low], axis=0)

        for d in range(3):
            m_loc[x, :, d * block_k:(d + 1) * block_k] = both(lambda site: coup[d, site])
        m_loc[x, :, 3 * block_k:4 * block_k] = both(lambda site: coup[3, site] + coup[4, site])
        for d, sign in enumerate((None, None, sign_up, sign_down)):
            m_halo[x, :, d * block_k:(d + 1) * block_k] = both(
                lambda site: coup[5 + d, site] if sign is None else coup[5 + d, site] * sign
            )

    def prepare_vectors(x):
        even, odd = vec[x], vec[lx + x]
        high, low = split(jnp.concatenate([even, odd], axis=0).T)
        where = x // 2, lax.rem(x, 2)
        wk[where[0], where[1], 0:nv, :] = high
        wk[where[0], where[1], nv:2 * nv, :] = low
        for y, value in enumerate((even, odd)):
            high, low = split(value)
            wt[x, y, 0:nc, 0:nv] = high[0:nc]
            wt[x, y, 0:nc, nv:2 * nv] = high[nc:2 * nc]
            wt[x, y, nc:2 * nc, 0:nv] = low[0:nc]
            wt[x, y, nc:2 * nc, nv:2 * nv] = low[nc:2 * nc]

    def local_part(it, c):
        field = x0 if it == 0 else x1

        def place(x):
            value = field[c, x]
            mine = masked(value, times_i(value))
            rhs_loc[x, 0:block_k, :] = mine
            rhs_loc[lax.rem(x + lx - 1, lx), block_k:2 * block_k, :] = mine
            rhs_loc[lax.rem(x + 1, lx), 2 * block_k:3 * block_k, :] = mine
            other = jnp.where(first_lanes(value), sooner(value), later(value))
            rhs_loc[x, 3 * block_k:4 * block_k, :] = masked(other, times_i(other))

        loop(0, lx, place)

        def multiply(x):
            acc[c, x] = src[c, x] - fold(dot(m_loc[x], rhs_loc[x]), nc)

        loop(0, lx, multiply)

    def halo_part(it, c, part_of):
        out = r0 if it == 0 else r1

        def body(j):
            x = part_of * (lx // 2) + j
            for slot in range(4):
                halo_copy(it, c, x, slot).wait_recv()
                value = halo[index(it, c), slot, x]
                rhs_halo[slot * block_k:(slot + 1) * block_k, :] = masked(value, times_i(value))
            residual = acc[c, x] - fold(dot(m_halo[x], rhs_halo[...]), nc)
            out[c, x] = residual
            if it == last:
                r1_copy(c, x).start()
            rhs_res[pl.ds(pl.multiple_of(j * block_k, 16), block_k), :] = masked(residual, -times_i(residual))

        loop(0, lx // 2, body)
        total = None
        for j in range(lx // 2):
            x = part_of * (lx // 2) + j
            value = fold(dot(wk[x // 2, x % 2], rhs_res[j * block_k:(j + 1) * block_k, :]), nv)
            total = value if total is None else total + value
        if part_of == 0:
            proj[...] = total
        else:
            total = total + proj[...]
            top, bottom = total[0:packed], total[packed:nv]
            part[index(it, c)] = jnp.where(first_lanes(top), top + sooner(top), bottom + later(bottom))

    def member(q):
        return {"groups": me_g, "space": lax.rem(q, pairs) * 2 + parity, "tm": q // pairs}

    my_rows = pl.multiple_of(parity * half, 8)
    other_rows = pl.multiple_of((1 - parity) * half, 8)
    piece = lax.rem(rank, pieces)
    block = rank - piece
    piece_row = pl.multiple_of(my_rows + piece * rows, 8)

    def core_copy(u):
        return pltpu.make_async_remote_copy(
            src_ref=part.at[u, pl.ds(other_rows, half)],
            dst_ref=core_in.at[u],
            send_sem=core_send.at[u],
            recv_sem=core_recv.at[u],
            device_id=partner,
            device_id_type=MESH,
        )

    def rs_copy(u, o):
        q = lax.rem(rank + o, members)
        row = pl.multiple_of(lax.rem(q, pieces) * rows, 8)
        return pltpu.make_async_remote_copy(
            src_ref=mine.at[u, pl.ds(row, rows)],
            dst_ref=rs_in.at[u, o],
            send_sem=rs_send.at[u, o],
            recv_sem=rs_recv.at[u, o],
            device_id=member(q),
            device_id_type=MESH,
        )

    def ag_copy(u, o):
        q = block + lax.rem(piece + o, pieces)
        return pltpu.make_async_remote_copy(
            src_ref=dfull.at[u, pl.ds(piece_row, rows)],
            dst_ref=dfull.at[u, pl.ds(piece_row, rows)],
            send_sem=ag_send.at[u, o],
            recv_sem=ag_recv.at[u, o],
            device_id=member(q),
            device_id_type=MESH,
        )

    def row_of(o):
        return pl.multiple_of(my_rows + lax.rem(piece + pieces - o, pieces) * rows, 8)

    def relay_copy(u, o):
        return pltpu.make_async_remote_copy(
            src_ref=dfull.at[u, pl.ds(row_of(o), rows)],
            dst_ref=dfull.at[u, pl.ds(row_of(o), rows)],
            send_sem=re_send.at[u, o],
            recv_sem=re_recv.at[u, o],
            device_id=partner,
            device_id_type=MESH,
        )

    def y_copy(c, o):
        return pltpu.make_async_remote_copy(
            src_ref=dfull.at[index(last, c), pl.ds(row_of(o), rows)],
            dst_ref=dother.at[c, pl.ds(row_of(o), rows)],
            send_sem=y_send.at[c, o],
            recv_sem=y_recv.at[c, o],
            device_id=other_group,
            device_id_type=MESH,
        )

    def relay_other(c, o):
        return pltpu.make_async_remote_copy(
            src_ref=dother.at[c, pl.ds(row_of(o), rows)],
            dst_ref=dother.at[c, pl.ds(row_of(o), rows)],
            send_sem=r2_send.at[c, o],
            recv_sem=r2_recv.at[c, o],
            device_id=partner,
            device_id_type=MESH,
        )

    def send_core(it, c):
        core_copy(index(it, c)).start()

    def send_sums(it, c):
        u = index(it, c)
        core_copy(u).wait_recv()
        mine[u] = part[u, pl.ds(my_rows, half), :] + core_in[u]
        loop(1, members, lambda o: rs_copy(u, o).start())

    def send_scaled(it, c):
        u = index(it, c)
        own = mine[u, pl.ds(pl.multiple_of(piece * rows, 8), rows), :]

        def gather(o, total):
            rs_copy(u, o).wait_recv()
            return total + rs_in[u, o]

        coef = lax.fori_loop(1, members, gather, own)
        eigen = eig_t[pl.ds(piece_row, rows), :]
        first = first_lanes(coef)
        real = jnp.where(first, eigen[:, 0:1], eigen[:, 2:3])
        imag = jnp.where(first, eigen[:, 1:2], eigen[:, 3:4])
        dfull[u, pl.ds(piece_row, rows), :] = real * coef + imag * times_i(coef)
        loop(1, pieces, lambda o: ag_copy(u, o).start())
        relay_copy(u, 0).start()
        if it == last:
            y_copy(c, 0).start()

    def relay(it, c):
        u = index(it, c)

        def forward(o):
            ag_copy(u, o).wait_recv()
            relay_copy(u, o).start()
            if it == last:
                y_copy(c, o).start()

        loop(1, pieces, forward)

    def gathered(it, c):
        loop(0, pieces, lambda o: relay_copy(index(it, c), o).wait_recv())

    group = 2

    def fill(even, odd):
        upper = jnp.where(first_lanes(even), even, later(odd))
        lower = jnp.where(first_lanes(even), sooner(even), odd)
        value = jnp.concatenate([upper, lower], axis=0)
        dst[...] = stacked(value, times_i(value))

    def expand(start, count):
        lhs = wt[pl.ds(start, count)].reshape(count * ly * 2 * nc, 2 * nv)
        out = dot(lhs, dst[...]).reshape(count, ly, 2 * nc, 2 * width)
        return [[fold(out[i, y], nc) for y in range(ly)] for i in range(count)]

    def update(c, pairs_now):
        u = index(0, c)
        fill(dfull[u], dfull[u])

        def body(j):
            outs = expand(j * group, group)
            for i in range(group):
                x = j * group + i
                even, odd = outs[i]
                x1[c, x] = x0[c, x] + jnp.where(first_lanes(even), even, odd) + 0.5 * r0[c, x]

                @pl.when(x < pairs_now)
                def _():
                    send_halo(1, c, x)

                x1_copy(c, x).start()

        loop(0, lx // group, body)

    def pass_on(c):
        def body(o):
            y_copy(c, o).wait_recv()
            relay_other(c, o).start()

        loop(0, pieces, body)

    def bases(c):
        def body(x):
            x1_copy(c, x).wait_recv()
            r1_copy(c, x).wait_recv()
            own_r, other_r = r1[c, x], r1o[c, x]
            one = groups_of(x1[c, x] + 0.5 * own_r, x1o[c, x] + 0.5 * other_r)
            two = groups_of(own_r, other_r)
            for y in range(2):
                early[c, y * lx + x] = one[y]
                if c == 0:
                    res[y * lx + x, :, 0:width] = two[y]
                else:
                    res[y * lx + x] = join(res[y * lx + x, :, 0:width], two[y])

        loop(0, lx, body)

    def finish(c):
        u = index(last, c)
        loop(0, pieces, lambda o: relay_other(c, o).wait_recv())
        own, other = dfull[u], dother[c]
        fill(jnp.where(me_g == 0, own, other), jnp.where(me_g == 0, other, own))

        def body(j):
            outs = expand(j * group, group)
            for i in range(group):
                for y in range(2):
                    site = y * lx + j * group + i
                    value = early[c, site] + outs[i][y]
                    if c == 0:
                        early[c, site] = value
                    else:
                        sol[site] = join(early[0, site], value)

        loop(0, lx // group, body)

    def begin(c):
        def body(x):
            x0[c, x] = take_pair(c, x, x0f)

        loop(0, lx, body)

    def send_pairs(it, c, start, stop):
        loop(start, stop, lambda x: send_halo(it, c, x))

    early_pairs, mid_pairs, late_pairs = 2, 2, 3
    loads[0].wait()
    begin(0)
    pl.semaphore_wait(barrier, total)
    send_pairs(0, 0, 0, lx)
    begin(1)
    send_pairs(0, 1, 0, early_pairs)

    loads[1].wait()
    loop(0, lx, prepare_matrices)
    loads[2].wait()

    def take_source(x):
        for c in range(CHUNKS):
            src[c, x] = take_pair(c, x, srcf)

    loop(0, lx, take_source)
    local_part(0, 0)
    loads[3].wait()
    rows_of_eigen = jnp.concatenate([eig[:, 0:packed], eig[:, packed:nv]], axis=0)
    eig_t[...] = jnp.concatenate([rows_of_eigen, rows_of_eigen], axis=0).T
    loads[4].wait()
    loop(0, lx, prepare_vectors)
    local_part(0, 1)

    halo_part(0, 0, 0)
    halo_part(0, 0, 1)
    send_core(0, 0)
    send_sums(0, 0)
    send_pairs(0, 1, early_pairs, lx)
    halo_part(0, 1, 0)
    send_scaled(0, 0)
    halo_part(0, 1, 1)
    send_core(0, 1)
    relay(0, 0)
    send_sums(0, 1)
    gathered(0, 0)
    update(0, mid_pairs)
    local_part(1, 0)
    send_scaled(0, 1)
    send_pairs(1, 0, mid_pairs, lx)
    halo_part(1, 0, 0)
    relay(0, 1)
    gathered(0, 1)
    update(1, late_pairs)
    local_part(1, 1)
    halo_part(1, 0, 1)
    send_core(1, 0)
    send_sums(1, 0)
    send_pairs(1, 1, late_pairs, lx)
    halo_part(1, 1, 0)
    send_scaled(1, 0)
    halo_part(1, 1, 1)
    send_core(1, 1)
    relay(1, 0)
    send_sums(1, 1)
    gathered(1, 0)
    pass_on(0)
    bases(0)
    finish(0)
    send_scaled(1, 1)
    bases(1)
    relay(1, 1)
    gathered(1, 1)
    pass_on(1)
    finish(1)

    for it in range(ITERS):
        for c in range(CHUNKS):
            u = index(it, c)
            core_copy(u).wait_send()
            loop(1, members, lambda o: rs_copy(u, o).wait_send())
            loop(1, pieces, lambda o: ag_copy(u, o).wait_send())
            loop(0, pieces, lambda o: relay_copy(u, o).wait_send())

            def drain(x):
                for slot in range(4):
                    halo_copy(it, c, x, slot).wait_send()
                if it == last:
                    x1_copy(c, x).wait_send()
                    r1_copy(c, x).wait_send()

            loop(0, lx, drain)

    for c in range(CHUNKS):
        def drain_y(o):
            y_copy(c, o).wait_send()
            relay_other(c, o).wait_send()

        loop(0, pieces, drain_y)


def solve(mesh, couplings, source, initial, vectors, inverse_eigen):
    nine, _, _, ly, lx, nc, _ = couplings.shape
    full = source.shape[-1]
    nv = vectors.shape[0]
    D = Dims(mesh, ly, lx, nc, full, nv)
    sites, width = D.sites, D.width
    field = (sites, nc, full)
    mine = (CHUNKS, lx, nc, width)
    units = ITERS * CHUNKS
    block_k = ly * 2 * nc
    vecs = vectors.reshape(nv, sites, 2 * nc).transpose(1, 2, 0)
    any_spec = pl.BlockSpec(memory_space=pl.ANY)
    vmem = pl.BlockSpec(memory_space=pltpu.VMEM)
    dma = pltpu.SemaphoreType.DMA
    out = jax.ShapeDtypeStruct(field, F32)
    x, r = pl.pallas_call(
        functools.partial(kernel, D),
        out_shape=(out, out),
        in_specs=[any_spec] * 5,
        out_specs=(vmem, vmem),
        scratch_shapes=[
            pltpu.VMEM((nine, sites, nc, 2 * nc), F32),
            pltpu.VMEM(field, F32),
            pltpu.VMEM(field, F32),
            pltpu.VMEM((sites, 2 * nc, nv), F32),
            pltpu.VMEM((2, nv), F32),
            dma((5,)),
        ]
        + [pltpu.VMEM(mine, F32)] * 8
        + [
            pltpu.VMEM((CHUNKS, sites, nc, width), F32),
            pltpu.VMEM((lx, 2 * nc, 4 * block_k), BF16),
            pltpu.VMEM((lx, 2 * nc, 4 * block_k), BF16),
            pltpu.VMEM((lx // 2, 2, 2 * nv, block_k), BF16),
            pltpu.VMEM((lx, ly, 2 * nc, 2 * nv), BF16),
            pltpu.VMEM((lx, 4 * block_k, 2 * width), BF16),
            pltpu.VMEM((4 * block_k, 2 * width), BF16),
            pltpu.VMEM((lx // 2 * block_k, 2 * width), BF16),
            pltpu.VMEM((2 * nv, 2 * width), BF16),
            pltpu.VMEM((nv, width), F32),
            pltpu.VMEM((units, 4, lx, nc, width), F32),
            pltpu.VMEM((units, D.packed, width), F32),
            pltpu.VMEM((units, D.half, width), F32),
            pltpu.VMEM((units, D.half, width), F32),
            pltpu.VMEM((units, D.members, D.rows, width), F32),
            pltpu.VMEM((units, D.packed, width), F32),
            pltpu.VMEM((CHUNKS, D.packed, width), F32),
            pltpu.VMEM((D.packed, 8), F32),
            dma((units, 4, lx)),
            dma((units, 4, lx)),
            dma((units,)),
            dma((units,)),
            dma((units, D.members)),
            dma((units, D.members)),
            dma((units, D.pieces)),
            dma((units, D.pieces)),
            dma((units, D.pieces)),
            dma((units, D.pieces)),
            dma((CHUNKS, D.pieces)),
            dma((CHUNKS, D.pieces)),
            dma((CHUNKS, lx)),
            dma((CHUNKS, lx)),
            dma((CHUNKS, lx)),
            dma((CHUNKS, lx)),
            dma((CHUNKS, D.pieces)),
            dma((CHUNKS, D.pieces)),
        ],
        compiler_params=pltpu.CompilerParams(
            collective_id=0, has_side_effects=True, vmem_limit_bytes=52 * 1024 * 1024
        ),
    )(
        couplings.reshape(nine, sites, nc, 2 * nc),
        source.reshape(field),
        initial.reshape(field),
        vecs,
        inverse_eigen,
    )
    return x.reshape(source.shape), r.reshape(source.shape)


def solution(mesh):
    in_specs = (
        P(None, "tm", "space", None, None, None, None),
        P("tm", "space", None, None, None, None),
        P("tm", "space", None, None, None, None),
        P(None, "tm", "space", None, None, None),
        P(),
    )
    out_specs = (
        P(("groups", "tm"), "space", None, None, None, None),
        P(("groups", "tm"), "space", None, None, None, None),
    )
    return jax.shard_map(
        functools.partial(solve, mesh), mesh=mesh, in_specs=in_specs, out_specs=out_specs, check_vma=False
    )
```

```python
import functools

import jax
import jax.numpy as jnp
from jax import lax
from jax.experimental import pallas as pl
from jax.experimental.pallas import tpu as pltpu
from jax.sharding import PartitionSpec as P

ITERS = 2
MESH = pl.DeviceIdType.MESH
F32 = jnp.float32
BF16 = jnp.bfloat16


def split(value):
    high = value.astype(BF16)
    low = (value - high.astype(F32)).astype(BF16)
    return high, low


def dot(a, b):
    return jnp.dot(a, b, preferred_element_type=F32)


class Dims:
    def __init__(self, mesh, ly, lx, nc, full, nv):
        self.ng, self.ns, self.nt = mesh.shape["groups"], mesh.shape["space"], mesh.shape["tm"]
        self.ly, self.lx, self.nc, self.full, self.nv = ly, lx, nc, full, nv
        assert self.ng == 2 and ly == 2 and lx % 4 == 0
        self.width = full // 2
        self.sites = ly * lx
        self.members = self.ns // 2 * self.nt
        self.packed = nv // 2
        self.half = self.packed // 2
        self.pieces = min(self.members, self.half // 8)
        self.rows = self.half // self.pieces


CHUNKS = 2


def kernel(
    D, coup_h, src_h, x0_h, vec_h, eig_h, sol, res,
    coup, srcf, x0f, vec, eig, local_sem,
    x0, x1, r0, r1, src, x1o, r1o, acc, early,
    m_loc, m_halo, wk, wt, rhs_loc, rhs_halo, rhs_res, dst, proj,
    halo, part, core_in, mine, rs_in, dfull, dother, eig_t,
    halo_send, halo_recv, core_send, core_recv, rs_send, rs_recv, ag_send, ag_recv, re_send, re_recv,
    y_send, y_recv, yx_send, yx_recv, yr_send, yr_recv, r2_send, r2_recv,
):
    ns, nt, sites, nc, lx, ly = D.ns, D.nt, D.sites, D.nc, D.lx, D.ly
    nv, packed, half, rows, pieces, members = D.nv, D.packed, D.half, D.rows, D.pieces, D.members
    width, full = D.width, D.full
    quarter = width // 4
    me_g, me_s, me_t = lax.axis_index("groups"), lax.axis_index("space"), lax.axis_index("tm")
    parity = lax.rem(me_s, 2)
    pairs = ns // 2
    rank = me_t * pairs + me_s // 2
    partner = {"groups": me_g, "space": me_s + 1 - 2 * parity, "tm": me_t}
    other_group = {"groups": 1 - me_g, "space": me_s, "tm": me_t}
    last = ITERS - 1
    block_k = ly * 2 * nc

    loads = [
        pltpu.make_async_copy(x0_h, x0f, local_sem.at[0]),
        pltpu.make_async_copy(coup_h, coup, local_sem.at[1]),
        pltpu.make_async_copy(src_h, srcf, local_sem.at[2]),
        pltpu.make_async_copy(eig_h, eig, local_sem.at[3]),
        pltpu.make_async_copy(vec_h, vec, local_sem.at[4]),
    ]
    for load in loads:
        load.start()

    barrier = pltpu.get_barrier_semaphore()
    total = ns * nt
    flat = me_t * ns + me_s

    def greet(o, carry):
        other = lax.rem(flat + o, total)
        pl.semaphore_signal(
            barrier, inc=1,
            device_id={"groups": me_g, "space": lax.rem(other, ns), "tm": other // ns}, device_id_type=MESH,
        )
        return carry

    lax.fori_loop(1, total, greet, 0)
    pl.semaphore_signal(barrier, inc=1, device_id=other_group, device_id_type=MESH)

    def lane(shape):
        return lax.broadcasted_iota(jnp.int32, shape, 1)

    def turn(v):
        return pltpu.roll(v, width // 2, 1)

    def later(v):
        return pltpu.roll(v, quarter, 1)

    def sooner(v):
        return pltpu.roll(v, width - quarter, 1)

    def real_lanes(v):
        return lane(v.shape) < width // 2

    def first_lanes(v):
        return lax.rem(lane(v.shape), width // 2) < quarter

    def times_i(v):
        turned = turn(v)
        return jnp.where(real_lanes(v), -turned, turned)

    def pack(even, odd):
        return jnp.where(first_lanes(even), even, later(odd)), jnp.where(first_lanes(even), sooner(even), odd)

    def take(c, value):
        re, im = value[:, 0:width], value[:, width:full]
        if c == 0:
            return jnp.where(real_lanes(re), re, turn(im))
        return jnp.where(real_lanes(re), turn(re), im)

    def take_pair(c, x, ref):
        of_g0, of_g1 = pack(take(c, ref[x]), take(c, ref[lx + x]))
        return jnp.where(me_g == 0, of_g0, of_g1)

    def groups_of(own, other):
        return pack(jnp.where(me_g == 0, own, other), jnp.where(me_g == 0, other, own))

    def join(c0, c1):
        return jnp.concatenate(
            [jnp.where(real_lanes(c0), c0, turn(c1)), jnp.where(real_lanes(c0), turn(c0), c1)], axis=1
        )

    def stacked(value, turned):
        high, low = split(value)
        t_high, t_low = split(turned)
        return jnp.concatenate(
            [jnp.concatenate([high, t_high], axis=0), jnp.concatenate([low, t_low], axis=0)], axis=1
        )

    keep = jnp.where(lax.rem(lane((2 * nc, 2 * width)), width // 2) < quarter, 1.0, 0.0).astype(BF16)

    def masked(value, turned):
        both = stacked(value, turned)
        even = both * keep
        return jnp.concatenate([even, both - even], axis=0)

    def fold(out, count):
        top, bottom = out[0:count], out[count:2 * count]
        return (top[:, 0:width] + top[:, width:2 * width]) + (bottom[:, 0:width] + bottom[:, width:2 * width])

    up_s, down_s = lax.rem(me_s + 1, ns), lax.rem(me_s + ns - 1, ns)
    up_t, down_t = lax.rem(me_t + 1, nt), lax.rem(me_t + nt - 1, nt)
    targets = (
        (2, {"groups": me_g, "space": me_s, "tm": down_t}),
        (3, {"groups": me_g, "space": me_s, "tm": up_t}),
        (0, {"groups": me_g, "space": down_s, "tm": me_t}),
        (1, {"groups": me_g, "space": up_s, "tm": me_t}),
    )
    target_of = dict(targets)

    def index(it, c):
        return it * CHUNKS + c

    def halo_copy(it, c, x, slot):
        source = x0 if it == 0 else x1
        u = index(it, c)
        return pltpu.make_async_remote_copy(
            src_ref=source.at[c, x],
            dst_ref=halo.at[u, slot, x],
            send_sem=halo_send.at[u, slot, x],
            recv_sem=halo_recv.at[u, slot, x],
            device_id=target_of[slot],
            device_id_type=MESH,
        )

    def send_halo(it, c, x):
        for slot, _ in targets:
            halo_copy(it, c, x, slot).start()

    def x1_copy(c, x):
        return pltpu.make_async_remote_copy(
            src_ref=x1.at[c, x], dst_ref=x1o.at[c, x], send_sem=yx_send.at[c, x], recv_sem=yx_recv.at[c, x],
            device_id=other_group, device_id_type=MESH,
        )

    def r1_copy(c, x):
        return pltpu.make_async_remote_copy(
            src_ref=r1.at[c, x], dst_ref=r1o.at[c, x], send_sem=yr_send.at[c, x], recv_sem=yr_recv.at[c, x],
            device_id=other_group, device_id_type=MESH,
        )

    def loop(start, stop, action):
        def body(o, carry):
            action(o)
            return carry

        lax.fori_loop(start, stop, body, 0)

    sign_up = jnp.where(me_t == nt - 1, -1.0, 1.0).astype(F32)
    sign_down = jnp.where(me_t == 0, -1.0, 1.0).astype(F32)

    def prepare_matrices(x):
        def both(value_of):
            high, low = split(jnp.concatenate([value_of(x), value_of(lx + x)], axis=1))
            return jnp.concatenate([high, low], axis=0)

        for d in range(3):
            m_loc[x, :, d * block_k:(d + 1) * block_k] = both(lambda site: coup[d, site])
        m_loc[x, :, 3 * block_k:4 * block_k] = both(lambda site: coup[3, site] + coup[4, site])
        for d, sign in enumerate((None, None, sign_up, sign_down)):
            m_halo[x, :, d * block_k:(d + 1) * block_k] = both(
                lambda site: coup[5 + d, site] if sign is None else coup[5 + d, site] * sign
            )

    def prepare_vectors(h):
        for i in range(2):
            x = 2 * h + i
            even, odd = vec[x], vec[lx + x]
            high, low = split(jnp.concatenate([even, odd], axis=0).T)
            wk[h, 0:nv, i * block_k:(i + 1) * block_k] = high
            wk[h, nv:2 * nv, i * block_k:(i + 1) * block_k] = low
            for y, value in enumerate((even, odd)):
                high, low = split(value)
                wt[x, y, 0:nc, 0:nv] = high[0:nc]
                wt[x, y, 0:nc, nv:2 * nv] = high[nc:2 * nc]
                wt[x, y, nc:2 * nc, 0:nv] = low[0:nc]
                wt[x, y, nc:2 * nc, nv:2 * nv] = low[nc:2 * nc]

    def local_part(it, c):
        field = x0 if it == 0 else x1

        def place(x):
            value = field[c, x]
            mine = masked(value, times_i(value))
            rhs_loc[x, 0:block_k, :] = mine
            rhs_loc[lax.rem(x + lx - 1, lx), block_k:2 * block_k, :] = mine
            rhs_loc[lax.rem(x + 1, lx), 2 * block_k:3 * block_k, :] = mine
            other = jnp.where(first_lanes(value), sooner(value), later(value))
            rhs_loc[x, 3 * block_k:4 * block_k, :] = masked(other, times_i(other))

        loop(0, lx, place)

        def multiply(x):
            acc[c, x] = src[c, x] - fold(dot(m_loc[x], rhs_loc[x]), nc)

        loop(0, lx, multiply)

    def halo_part(it, c, part_of):
        out = r0 if it == 0 else r1

        def body(j):
            x = part_of * (lx // 2) + j
            for slot in range(4):
                halo_copy(it, c, x, slot).wait_recv()
                value = halo[index(it, c), slot, x]
                rhs_halo[slot * block_k:(slot + 1) * block_k, :] = masked(value, times_i(value))
            residual = acc[c, x] - fold(dot(m_halo[x], rhs_halo[...]), nc)
            out[c, x] = residual
            if it == last:
                r1_copy(c, x).start()
            rhs_res[pl.ds(pl.multiple_of(j * block_k, 16), block_k), :] = masked(residual, -times_i(residual))

        loop(0, lx // 2, body)
        total = None
        for h in range(lx // 4):
            value = fold(dot(wk[part_of * (lx // 4) + h], rhs_res[2 * h * block_k:2 * (h + 1) * block_k, :]), nv)
            total = value if total is None else total + value
        if part_of == 0:
            proj[...] = total
        else:
            total = total + proj[...]
            top, bottom = total[0:packed], total[packed:nv]
            part[index(it, c)] = jnp.where(first_lanes(top), top + sooner(top), bottom + later(bottom))

    def member(q):
        return {"groups": me_g, "space": lax.rem(q, pairs) * 2 + parity, "tm": q // pairs}

    my_rows = pl.multiple_of(parity * half, 8)
    other_rows = pl.multiple_of((1 - parity) * half, 8)
    piece = lax.rem(rank, pieces)
    block = rank - piece
    piece_row = pl.multiple_of(my_rows + piece * rows, 8)

    def core_copy(u):
        return pltpu.make_async_remote_copy(
            src_ref=part.at[u, pl.ds(other_rows, half)],
            dst_ref=core_in.at[u],
            send_sem=core_send.at[u],
            recv_sem=core_recv.at[u],
            device_id=partner,
            device_id_type=MESH,
        )

    def rs_copy(u, o):
        q = lax.rem(rank + o, members)
        row = pl.multiple_of(lax.rem(q, pieces) * rows, 8)
        return pltpu.make_async_remote_copy(
            src_ref=mine.at[u, pl.ds(row, rows)],
            dst_ref=rs_in.at[u, o],
            send_sem=rs_send.at[u, o],
            recv_sem=rs_recv.at[u, o],
            device_id=member(q),
            device_id_type=MESH,
        )

    def ag_copy(u, o):
        q = block + lax.rem(piece + o, pieces)
        return pltpu.make_async_remote_copy(
            src_ref=dfull.at[u, pl.ds(piece_row, rows)],
            dst_ref=dfull.at[u, pl.ds(piece_row, rows)],
            send_sem=ag_send.at[u, o],
            recv_sem=ag_recv.at[u, o],
            device_id=member(q),
            device_id_type=MESH,
        )

    def row_of(o):
        return pl.multiple_of(my_rows + lax.rem(piece + pieces - o, pieces) * rows, 8)

    def relay_copy(u, o):
        return pltpu.make_async_remote_copy(
            src_ref=dfull.at[u, pl.ds(row_of(o), rows)],
            dst_ref=dfull.at[u, pl.ds(row_of(o), rows)],
            send_sem=re_send.at[u, o],
            recv_sem=re_recv.at[u, o],
            device_id=partner,
            device_id_type=MESH,
        )

    def y_copy(c, o):
        return pltpu.make_async_remote_copy(
            src_ref=dfull.at[index(last, c), pl.ds(row_of(o), rows)],
            dst_ref=dother.at[c, pl.ds(row_of(o), rows)],
            send_sem=y_send.at[c, o],
            recv_sem=y_recv.at[c, o],
            device_id=other_group,
            device_id_type=MESH,
        )

    def relay_other(c, o):
        return pltpu.make_async_remote_copy(
            src_ref=dother.at[c, pl.ds(row_of(o), rows)],
            dst_ref=dother.at[c, pl.ds(row_of(o), rows)],
            send_sem=r2_send.at[c, o],
            recv_sem=r2_recv.at[c, o],
            device_id=partner,
            device_id_type=MESH,
        )

    def send_core(it, c):
        core_copy(index(it, c)).start()

    def send_sums(it, c):
        u = index(it, c)
        core_copy(u).wait_recv()
        mine[u] = part[u, pl.ds(my_rows, half), :] + core_in[u]
        loop(1, members, lambda o: rs_copy(u, o).start())

    def send_scaled(it, c):
        u = index(it, c)
        own = mine[u, pl.ds(pl.multiple_of(piece * rows, 8), rows), :]

        def gather(o, total):
            rs_copy(u, o).wait_recv()
            return total + rs_in[u, o]

        coef = lax.fori_loop(1, members, gather, own)
        eigen = eig_t[pl.ds(piece_row, rows), :]
        first = first_lanes(coef)
        real = jnp.where(first, eigen[:, 0:1], eigen[:, 2:3])
        imag = jnp.where(first, eigen[:, 1:2], eigen[:, 3:4])
        dfull[u, pl.ds(piece_row, rows), :] = real * coef + imag * times_i(coef)
        loop(1, pieces, lambda o: ag_copy(u, o).start())
        relay_copy(u, 0).start()
        if it == last:
            y_copy(c, 0).start()

    def relay(it, c):
        u = index(it, c)

        def forward(o):
            ag_copy(u, o).wait_recv()
            relay_copy(u, o).start()
            if it == last:
                y_copy(c, o).start()

        loop(1, pieces, forward)

    def gathered(it, c):
        loop(0, pieces, lambda o: relay_copy(index(it, c), o).wait_recv())

    group = 2

    def fill(even, odd):
        upper = jnp.where(first_lanes(even), even, later(odd))
        lower = jnp.where(first_lanes(even), sooner(even), odd)
        value = jnp.concatenate([upper, lower], axis=0)
        dst[...] = stacked(value, times_i(value))

    def expand(start, count):
        lhs = wt[pl.ds(start, count)].reshape(count * ly * 2 * nc, 2 * nv)
        out = dot(lhs, dst[...]).reshape(count, ly, 2 * nc, 2 * width)
        return [[fold(out[i, y], nc) for y in range(ly)] for i in range(count)]

    def update(c, pairs_now):
        u = index(0, c)
        fill(dfull[u], dfull[u])

        def body(j):
            outs = expand(j * group, group)
            for i in range(group):
                x = j * group + i
                even, odd = outs[i]
                x1[c, x] = x0[c, x] + jnp.where(first_lanes(even), even, odd) + 0.5 * r0[c, x]

                @pl.when(x < pairs_now)
                def _():
                    send_halo(1, c, x)

                x1_copy(c, x).start()

        loop(0, lx // group, body)

    def pass_on(c):
        def body(o):
            y_copy(c, o).wait_recv()
            relay_other(c, o).start()

        loop(0, pieces, body)

    def bases(c):
        def body(x):
            x1_copy(c, x).wait_recv()
            r1_copy(c, x).wait_recv()
            own_r, other_r = r1[c, x], r1o[c, x]
            one = groups_of(x1[c, x] + 0.5 * own_r, x1o[c, x] + 0.5 * other_r)
            two = groups_of(own_r, other_r)
            for y in range(2):
                early[c, y * lx + x] = one[y]
                if c == 0:
                    res[y * lx + x, :, 0:width] = two[y]
                else:
                    res[y * lx + x] = join(res[y * lx + x, :, 0:width], two[y])

        loop(0, lx, body)

    def finish(c):
        u = index(last, c)
        loop(0, pieces, lambda o: relay_other(c, o).wait_recv())
        own, other = dfull[u], dother[c]
        fill(jnp.where(me_g == 0, own, other), jnp.where(me_g == 0, other, own))

        def body(j):
            outs = expand(j * group, group)
            for i in range(group):
                for y in range(2):
                    site = y * lx + j * group + i
                    value = early[c, site] + outs[i][y]
                    if c == 0:
                        early[c, site] = value
                    else:
                        sol[site] = join(early[0, site], value)

        loop(0, lx // group, body)

    def drain_fields(it, c):
        u = index(it, c)
        core_copy(u).wait_send()
        loop(1, members, lambda o: rs_copy(u, o).wait_send())

        def body(x):
            for slot in range(4):
                halo_copy(it, c, x, slot).wait_send()
            if it == last:
                x1_copy(c, x).wait_send()
                r1_copy(c, x).wait_send()

        loop(0, lx, body)

    def drain_coefficients(it, c):
        u = index(it, c)
        loop(1, pieces, lambda o: ag_copy(u, o).wait_send())
        loop(0, pieces, lambda o: relay_copy(u, o).wait_send())
        if it == last:
            loop(0, pieces, lambda o: y_copy(c, o).wait_send())
            loop(0, pieces, lambda o: relay_other(c, o).wait_send())

    def begin(c):
        def body(x):
            x0[c, x] = take_pair(c, x, x0f)

        loop(0, lx, body)

    def send_pairs(it, c, start, stop):
        loop(start, stop, lambda x: send_halo(it, c, x))

    early_pairs, mid_pairs, late_pairs = 2, 2, 3
    loads[0].wait()
    begin(0)
    pl.semaphore_wait(barrier, total)
    send_pairs(0, 0, 0, lx)
    begin(1)
    send_pairs(0, 1, 0, early_pairs)

    loads[1].wait()
    loop(0, lx, prepare_matrices)
    loads[2].wait()

    def take_source(x):
        for c in range(CHUNKS):
            src[c, x] = take_pair(c, x, srcf)

    loop(0, lx, take_source)
    local_part(0, 0)
    loads[3].wait()
    rows_of_eigen = jnp.concatenate([eig[:, 0:packed], eig[:, packed:nv]], axis=0)
    eig_t[...] = jnp.concatenate([rows_of_eigen, rows_of_eigen], axis=0).T
    loads[4].wait()
    loop(0, lx // 2, prepare_vectors)
    local_part(0, 1)

    halo_part(0, 0, 0)
    halo_part(0, 0, 1)
    send_core(0, 0)
    send_sums(0, 0)
    send_pairs(0, 1, early_pairs, lx)
    halo_part(0, 1, 0)
    send_scaled(0, 0)
    halo_part(0, 1, 1)
    send_core(0, 1)
    relay(0, 0)
    send_sums(0, 1)
    gathered(0, 0)
    update(0, mid_pairs)
    local_part(1, 0)
    send_scaled(0, 1)
    send_pairs(1, 0, mid_pairs, lx)
    halo_part(1, 0, 0)
    relay(0, 1)
    gathered(0, 1)
    update(1, late_pairs)
    local_part(1, 1)
    halo_part(1, 0, 1)
    send_core(1, 0)
    send_sums(1, 0)
    send_pairs(1, 1, late_pairs, lx)
    halo_part(1, 1, 0)
    send_scaled(1, 0)
    for c in range(CHUNKS):
        drain_fields(0, c)
        drain_coefficients(0, c)
    halo_part(1, 1, 1)
    send_core(1, 1)
    relay(1, 0)
    send_sums(1, 1)
    gathered(1, 0)
    pass_on(0)
    bases(0)
    send_scaled(1, 1)
    finish(0)
    bases(1)
    drain_fields(1, 0)
    drain_coefficients(1, 0)
    drain_fields(1, 1)
    relay(1, 1)
    gathered(1, 1)
    pass_on(1)
    finish(1)

    drain_coefficients(1, 1)


def solve(mesh, couplings, source, initial, vectors, inverse_eigen):
    nine, _, _, ly, lx, nc, _ = couplings.shape
    full = source.shape[-1]
    nv = vectors.shape[0]
    D = Dims(mesh, ly, lx, nc, full, nv)
    sites, width = D.sites, D.width
    field = (sites, nc, full)
    mine = (CHUNKS, lx, nc, width)
    units = ITERS * CHUNKS
    block_k = ly * 2 * nc
    vecs = vectors.reshape(nv, sites, 2 * nc).transpose(1, 2, 0)
    any_spec = pl.BlockSpec(memory_space=pl.ANY)
    vmem = pl.BlockSpec(memory_space=pltpu.VMEM)
    dma = pltpu.SemaphoreType.DMA
    out = jax.ShapeDtypeStruct(field, F32)
    x, r = pl.pallas_call(
        functools.partial(kernel, D),
        out_shape=(out, out),
        in_specs=[any_spec] * 5,
        out_specs=(vmem, vmem),
        scratch_shapes=[
            pltpu.VMEM((nine, sites, nc, 2 * nc), F32),
            pltpu.VMEM(field, F32),
            pltpu.VMEM(field, F32),
            pltpu.VMEM((sites, 2 * nc, nv), F32),
            pltpu.VMEM((2, nv), F32),
            dma((5,)),
        ]
        + [pltpu.VMEM(mine, F32)] * 8
        + [
            pltpu.VMEM((CHUNKS, sites, nc, width), F32),
            pltpu.VMEM((lx, 2 * nc, 4 * block_k), BF16),
            pltpu.VMEM((lx, 2 * nc, 4 * block_k), BF16),
            pltpu.VMEM((lx // 2, 2 * nv, 2 * block_k), BF16),
            pltpu.VMEM((lx, ly, 2 * nc, 2 * nv), BF16),
            pltpu.VMEM((lx, 4 * block_k, 2 * width), BF16),
            pltpu.VMEM((4 * block_k, 2 * width), BF16),
            pltpu.VMEM((lx // 2 * block_k, 2 * width), BF16),
            pltpu.VMEM((2 * nv, 2 * width), BF16),
            pltpu.VMEM((nv, width), F32),
            pltpu.VMEM((units, 4, lx, nc, width), F32),
            pltpu.VMEM((units, D.packed, width), F32),
            pltpu.VMEM((units, D.half, width), F32),
            pltpu.VMEM((units, D.half, width), F32),
            pltpu.VMEM((units, D.members, D.rows, width), F32),
            pltpu.VMEM((units, D.packed, width), F32),
            pltpu.VMEM((CHUNKS, D.packed, width), F32),
            pltpu.VMEM((D.packed, 8), F32),
            dma((units, 4, lx)),
            dma((units, 4, lx)),
            dma((units,)),
            dma((units,)),
            dma((units, D.members)),
            dma((units, D.members)),
            dma((units, D.pieces)),
            dma((units, D.pieces)),
            dma((units, D.pieces)),
            dma((units, D.pieces)),
            dma((CHUNKS, D.pieces)),
            dma((CHUNKS, D.pieces)),
            dma((CHUNKS, lx)),
            dma((CHUNKS, lx)),
            dma((CHUNKS, lx)),
            dma((CHUNKS, lx)),
            dma((CHUNKS, D.pieces)),
            dma((CHUNKS, D.pieces)),
        ],
        compiler_params=pltpu.CompilerParams(
            collective_id=0, has_side_effects=True, vmem_limit_bytes=52 * 1024 * 1024
        ),
    )(
        couplings.reshape(nine, sites, nc, 2 * nc),
        source.reshape(field),
        initial.reshape(field),
        vecs,
        inverse_eigen,
    )
    return x.reshape(source.shape), r.reshape(source.shape)


def solution(mesh):
    in_specs = (
        P(None, "tm", "space", None, None, None, None),
        P("tm", "space", None, None, None, None),
        P("tm", "space", None, None, None, None),
        P(None, "tm", "space", None, None, None),
        P(),
    )
    out_specs = (
        P(("groups", "tm"), "space", None, None, None, None),
        P(("groups", "tm"), "space", None, None, None, None),
    )
    return jax.shard_map(
        functools.partial(solve, mesh), mesh=mesh, in_specs=in_specs, out_specs=out_specs, check_vma=False
    )
```

```python
import functools

import jax
import jax.numpy as jnp
from jax import lax
from jax.experimental import pallas as pl
from jax.experimental.pallas import tpu as pltpu
from jax.sharding import PartitionSpec as P

ITERS = 2
MESH = pl.DeviceIdType.MESH
F32 = jnp.float32
BF16 = jnp.bfloat16


def split(value):
    high = value.astype(BF16)
    low = (value - high.astype(F32)).astype(BF16)
    return high, low


def dot(a, b):
    return jnp.dot(a, b, preferred_element_type=F32)


def join(c0, c1):
    width = c0.shape[1]
    real = lax.broadcasted_iota(jnp.int32, c0.shape, 1) < width // 2
    turned0, turned1 = pltpu.roll(c0, width // 2, 1), pltpu.roll(c1, width // 2, 1)
    return jnp.concatenate([jnp.where(real, c0, turned1), jnp.where(real, turned0, c1)], axis=1)


def fold(out, count):
    top, bottom = out[0:count], out[count:2 * count]
    width = out.shape[1] // 2
    return (top[:, 0:width] + top[:, width:2 * width]) + (bottom[:, 0:width] + bottom[:, width:2 * width])


def expansion(D, matrices, rhs):
    count = matrices.shape[0]
    out = dot(matrices.reshape(count * D.ly * 2 * D.nc, 2 * D.nv), rhs)
    out = out.reshape(count, D.ly, 2 * D.nc, 2 * D.width)
    return [[fold(out[i, y], D.nc) for y in range(D.ly)] for i in range(count)]


class Dims:
    def __init__(self, mesh, ly, lx, nc, full, nv):
        self.ng, self.ns, self.nt = mesh.shape["groups"], mesh.shape["space"], mesh.shape["tm"]
        self.ly, self.lx, self.nc, self.full, self.nv = ly, lx, nc, full, nv
        assert self.ng == 2 and ly == 2 and lx % 4 == 0
        self.width = full // 2
        self.sites = ly * lx
        self.members = self.ns // 2 * self.nt
        self.packed = nv // 2
        self.half = self.packed // 2
        self.pieces = min(self.members, self.half // 8)
        self.rows = self.half // self.pieces


CHUNKS = 2


def kernel(
    D, coup_h, src_h, x0_h, vec_h, eig_h, res, early, dst, wt,
    coup, srcf, x0f, vec, eig, local_sem,
    x0, x1, r0, r1, src, x1o, r1o, acc,
    m_loc, m_halo, wk, rhs_loc, rhs_halo, rhs_res, proj,
    halo, part, core_in, mine, rs_in, dfull, dother, eig_t,
    halo_send, halo_recv, core_send, core_recv, rs_send, rs_recv, ag_send, ag_recv, re_send, re_recv,
    y_send, y_recv, yx_send, yx_recv, yr_send, yr_recv, r2_send, r2_recv,
):
    ns, nt, sites, nc, lx, ly = D.ns, D.nt, D.sites, D.nc, D.lx, D.ly
    nv, packed, half, rows, pieces, members = D.nv, D.packed, D.half, D.rows, D.pieces, D.members
    width, full = D.width, D.full
    quarter = width // 4
    me_g, me_s, me_t = lax.axis_index("groups"), lax.axis_index("space"), lax.axis_index("tm")
    parity = lax.rem(me_s, 2)
    pairs = ns // 2
    rank = me_t * pairs + me_s // 2
    partner = {"groups": me_g, "space": me_s + 1 - 2 * parity, "tm": me_t}
    other_group = {"groups": 1 - me_g, "space": me_s, "tm": me_t}
    last = ITERS - 1
    block_k = ly * 2 * nc

    loads = [
        pltpu.make_async_copy(x0_h, x0f, local_sem.at[0]),
        pltpu.make_async_copy(coup_h, coup, local_sem.at[1]),
        pltpu.make_async_copy(src_h, srcf, local_sem.at[2]),
        pltpu.make_async_copy(eig_h, eig, local_sem.at[3]),
        pltpu.make_async_copy(vec_h, vec, local_sem.at[4]),
    ]
    for load in loads:
        load.start()

    barrier = pltpu.get_barrier_semaphore()
    total = ns * nt
    flat = me_t * ns + me_s

    def greet(o, carry):
        other = lax.rem(flat + o, total)
        pl.semaphore_signal(
            barrier, inc=1,
            device_id={"groups": me_g, "space": lax.rem(other, ns), "tm": other // ns}, device_id_type=MESH,
        )
        return carry

    lax.fori_loop(1, total, greet, 0)
    pl.semaphore_signal(barrier, inc=1, device_id=other_group, device_id_type=MESH)

    def lane(shape):
        return lax.broadcasted_iota(jnp.int32, shape, 1)

    def turn(v):
        return pltpu.roll(v, width // 2, 1)

    def later(v):
        return pltpu.roll(v, quarter, 1)

    def sooner(v):
        return pltpu.roll(v, width - quarter, 1)

    def real_lanes(v):
        return lane(v.shape) < width // 2

    def first_lanes(v):
        return lax.rem(lane(v.shape), width // 2) < quarter

    def times_i(v):
        turned = turn(v)
        return jnp.where(real_lanes(v), -turned, turned)

    def pack(even, odd):
        return jnp.where(first_lanes(even), even, later(odd)), jnp.where(first_lanes(even), sooner(even), odd)

    def take(c, value):
        re, im = value[:, 0:width], value[:, width:full]
        if c == 0:
            return jnp.where(real_lanes(re), re, turn(im))
        return jnp.where(real_lanes(re), turn(re), im)

    def take_pair(c, x, ref):
        of_g0, of_g1 = pack(take(c, ref[x]), take(c, ref[lx + x]))
        return jnp.where(me_g == 0, of_g0, of_g1)

    def groups_of(own, other):
        return pack(jnp.where(me_g == 0, own, other), jnp.where(me_g == 0, other, own))

    def stacked(value, turned):
        high, low = split(value)
        t_high, t_low = split(turned)
        return jnp.concatenate(
            [jnp.concatenate([high, t_high], axis=0), jnp.concatenate([low, t_low], axis=0)], axis=1
        )

    keep = jnp.where(lax.rem(lane((2 * nc, 2 * width)), width // 2) < quarter, 1.0, 0.0).astype(BF16)

    def masked(value, turned):
        both = stacked(value, turned)
        even = both * keep
        return jnp.concatenate([even, both - even], axis=0)

    up_s, down_s = lax.rem(me_s + 1, ns), lax.rem(me_s + ns - 1, ns)
    up_t, down_t = lax.rem(me_t + 1, nt), lax.rem(me_t + nt - 1, nt)
    targets = (
        (2, {"groups": me_g, "space": me_s, "tm": down_t}),
        (3, {"groups": me_g, "space": me_s, "tm": up_t}),
        (0, {"groups": me_g, "space": down_s, "tm": me_t}),
        (1, {"groups": me_g, "space": up_s, "tm": me_t}),
    )
    target_of = dict(targets)

    def index(it, c):
        return it * CHUNKS + c

    def halo_copy(it, c, x, slot):
        source = x0 if it == 0 else x1
        u = index(it, c)
        return pltpu.make_async_remote_copy(
            src_ref=source.at[c, x],
            dst_ref=halo.at[u, slot, x],
            send_sem=halo_send.at[u, slot, x],
            recv_sem=halo_recv.at[u, slot, x],
            device_id=target_of[slot],
            device_id_type=MESH,
        )

    def send_halo(it, c, x):
        for slot, _ in targets:
            halo_copy(it, c, x, slot).start()

    def x1_copy(c, x):
        return pltpu.make_async_remote_copy(
            src_ref=x1.at[c, x], dst_ref=x1o.at[c, x], send_sem=yx_send.at[c, x], recv_sem=yx_recv.at[c, x],
            device_id=other_group, device_id_type=MESH,
        )

    def r1_copy(c, x):
        return pltpu.make_async_remote_copy(
            src_ref=r1.at[c, x], dst_ref=r1o.at[c, x], send_sem=yr_send.at[c, x], recv_sem=yr_recv.at[c, x],
            device_id=other_group, device_id_type=MESH,
        )

    def loop(start, stop, action):
        def body(o, carry):
            action(o)
            return carry

        lax.fori_loop(start, stop, body, 0)

    sign_up = jnp.where(me_t == nt - 1, -1.0, 1.0).astype(F32)
    sign_down = jnp.where(me_t == 0, -1.0, 1.0).astype(F32)

    def prepare_matrices(x):
        def both(value_of):
            high, low = split(jnp.concatenate([value_of(x), value_of(lx + x)], axis=1))
            return jnp.concatenate([high, low], axis=0)

        for d in range(3):
            m_loc[x, :, d * block_k:(d + 1) * block_k] = both(lambda site: coup[d, site])
        m_loc[x, :, 3 * block_k:4 * block_k] = both(lambda site: coup[3, site] + coup[4, site])
        for d, sign in enumerate((None, None, sign_up, sign_down)):
            m_halo[x, :, d * block_k:(d + 1) * block_k] = both(
                lambda site: coup[5 + d, site] if sign is None else coup[5 + d, site] * sign
            )

    def prepare_vectors(h):
        for i in range(2):
            x = 2 * h + i
            even, odd = vec[x], vec[lx + x]
            high, low = split(jnp.concatenate([even, odd], axis=0).T)
            wk[h, 0:nv, i * block_k:(i + 1) * block_k] = high
            wk[h, nv:2 * nv, i * block_k:(i + 1) * block_k] = low
            for y, value in enumerate((even, odd)):
                high, low = split(value)
                wt[x, y, 0:nc, 0:nv] = high[0:nc]
                wt[x, y, 0:nc, nv:2 * nv] = high[nc:2 * nc]
                wt[x, y, nc:2 * nc, 0:nv] = low[0:nc]
                wt[x, y, nc:2 * nc, nv:2 * nv] = low[nc:2 * nc]

    def local_part(it, c):
        field = x0 if it == 0 else x1

        def place(x):
            value = field[c, x]
            mine = masked(value, times_i(value))
            rhs_loc[x, 0:block_k, :] = mine
            rhs_loc[lax.rem(x + lx - 1, lx), block_k:2 * block_k, :] = mine
            rhs_loc[lax.rem(x + 1, lx), 2 * block_k:3 * block_k, :] = mine
            other = jnp.where(first_lanes(value), sooner(value), later(value))
            rhs_loc[x, 3 * block_k:4 * block_k, :] = masked(other, times_i(other))

        loop(0, lx, place)

        def multiply(x):
            acc[c, x] = src[c, x] - fold(dot(m_loc[x], rhs_loc[x]), nc)

        loop(0, lx, multiply)

    def halo_part(it, c, part_of):
        out = r0 if it == 0 else r1

        def body(j):
            x = part_of * (lx // 2) + j
            for slot in range(4):
                halo_copy(it, c, x, slot).wait_recv()
                value = halo[index(it, c), slot, x]
                rhs_halo[slot * block_k:(slot + 1) * block_k, :] = masked(value, times_i(value))
            residual = acc[c, x] - fold(dot(m_halo[x], rhs_halo[...]), nc)
            out[c, x] = residual
            if it == last:
                r1_copy(c, x).start()
            rhs_res[pl.ds(pl.multiple_of(j * block_k, 16), block_k), :] = masked(residual, -times_i(residual))

        loop(0, lx // 2, body)
        total = None
        for h in range(lx // 4):
            value = fold(dot(wk[part_of * (lx // 4) + h], rhs_res[2 * h * block_k:2 * (h + 1) * block_k, :]), nv)
            total = value if total is None else total + value
        if part_of == 0:
            proj[...] = total
        else:
            total = total + proj[...]
            top, bottom = total[0:packed], total[packed:nv]
            part[index(it, c)] = jnp.where(first_lanes(top), top + sooner(top), bottom + later(bottom))

    def member(q):
        return {"groups": me_g, "space": lax.rem(q, pairs) * 2 + parity, "tm": q // pairs}

    my_rows = pl.multiple_of(parity * half, 8)
    other_rows = pl.multiple_of((1 - parity) * half, 8)
    piece = lax.rem(rank, pieces)
    block = rank - piece
    piece_row = pl.multiple_of(my_rows + piece * rows, 8)

    def core_copy(u):
        return pltpu.make_async_remote_copy(
            src_ref=part.at[u, pl.ds(other_rows, half)],
            dst_ref=core_in.at[u],
            send_sem=core_send.at[u],
            recv_sem=core_recv.at[u],
            device_id=partner,
            device_id_type=MESH,
        )

    def rs_copy(u, o):
        q = lax.rem(rank + o, members)
        row = pl.multiple_of(lax.rem(q, pieces) * rows, 8)
        return pltpu.make_async_remote_copy(
            src_ref=mine.at[u, pl.ds(row, rows)],
            dst_ref=rs_in.at[u, o],
            send_sem=rs_send.at[u, o],
            recv_sem=rs_recv.at[u, o],
            device_id=member(q),
            device_id_type=MESH,
        )

    def ag_copy(u, o):
        q = block + lax.rem(piece + o, pieces)
        return pltpu.make_async_remote_copy(
            src_ref=dfull.at[u, pl.ds(piece_row, rows)],
            dst_ref=dfull.at[u, pl.ds(piece_row, rows)],
            send_sem=ag_send.at[u, o],
            recv_sem=ag_recv.at[u, o],
            device_id=member(q),
            device_id_type=MESH,
        )

    def row_of(o):
        return pl.multiple_of(my_rows + lax.rem(piece + pieces - o, pieces) * rows, 8)

    def relay_copy(u, o):
        return pltpu.make_async_remote_copy(
            src_ref=dfull.at[u, pl.ds(row_of(o), rows)],
            dst_ref=dfull.at[u, pl.ds(row_of(o), rows)],
            send_sem=re_send.at[u, o],
            recv_sem=re_recv.at[u, o],
            device_id=partner,
            device_id_type=MESH,
        )

    def y_copy(c, o):
        return pltpu.make_async_remote_copy(
            src_ref=dfull.at[index(last, c), pl.ds(row_of(o), rows)],
            dst_ref=dother.at[c, pl.ds(row_of(o), rows)],
            send_sem=y_send.at[c, o],
            recv_sem=y_recv.at[c, o],
            device_id=other_group,
            device_id_type=MESH,
        )

    def relay_other(c, o):
        return pltpu.make_async_remote_copy(
            src_ref=dother.at[c, pl.ds(row_of(o), rows)],
            dst_ref=dother.at[c, pl.ds(row_of(o), rows)],
            send_sem=r2_send.at[c, o],
            recv_sem=r2_recv.at[c, o],
            device_id=partner,
            device_id_type=MESH,
        )

    def send_core(it, c):
        core_copy(index(it, c)).start()

    def send_sums(it, c):
        u = index(it, c)
        core_copy(u).wait_recv()
        mine[u] = part[u, pl.ds(my_rows, half), :] + core_in[u]
        loop(1, members, lambda o: rs_copy(u, o).start())

    def send_scaled(it, c):
        u = index(it, c)
        own = mine[u, pl.ds(pl.multiple_of(piece * rows, 8), rows), :]

        def gather(o, total):
            rs_copy(u, o).wait_recv()
            return total + rs_in[u, o]

        coef = lax.fori_loop(1, members, gather, own)
        eigen = eig_t[pl.ds(piece_row, rows), :]
        first = first_lanes(coef)
        real = jnp.where(first, eigen[:, 0:1], eigen[:, 2:3])
        imag = jnp.where(first, eigen[:, 1:2], eigen[:, 3:4])
        dfull[u, pl.ds(piece_row, rows), :] = real * coef + imag * times_i(coef)
        loop(1, pieces, lambda o: ag_copy(u, o).start())
        relay_copy(u, 0).start()
        if it == last:
            y_copy(c, 0).start()

    def relay(it, c):
        u = index(it, c)

        def forward(o):
            ag_copy(u, o).wait_recv()
            relay_copy(u, o).start()
            if it == last:
                y_copy(c, o).start()

        loop(1, pieces, forward)

    def gathered(it, c):
        loop(0, pieces, lambda o: relay_copy(index(it, c), o).wait_recv())

    group = 2

    def fill(even, odd):
        upper = jnp.where(first_lanes(even), even, later(odd))
        lower = jnp.where(first_lanes(even), sooner(even), odd)
        value = jnp.concatenate([upper, lower], axis=0)
        dst[...] = stacked(value, times_i(value))

    def expand(start, count):
        return expansion(D, wt[pl.ds(start, count)], dst[...])

    def update(c, pairs_now):
        u = index(0, c)
        fill(dfull[u], dfull[u])

        def body(j):
            outs = expand(j * group, group)
            for i in range(group):
                x = j * group + i
                even, odd = outs[i]
                x1[c, x] = x0[c, x] + jnp.where(first_lanes(even), even, odd) + 0.5 * r0[c, x]

                @pl.when(x < pairs_now)
                def _():
                    send_halo(1, c, x)

                x1_copy(c, x).start()

        loop(0, lx // group, body)

    def pass_on(c):
        def body(o):
            y_copy(c, o).wait_recv()
            relay_other(c, o).start()

        loop(0, pieces, body)

    def bases(c):
        def body(x):
            x1_copy(c, x).wait_recv()
            r1_copy(c, x).wait_recv()
            own_r, other_r = r1[c, x], r1o[c, x]
            one = groups_of(x1[c, x] + 0.5 * own_r, x1o[c, x] + 0.5 * other_r)
            two = groups_of(own_r, other_r)
            for y in range(2):
                early[c, y * lx + x] = one[y]
                if c == 0:
                    res[y * lx + x, :, 0:width] = two[y]
                else:
                    res[y * lx + x] = join(res[y * lx + x, :, 0:width], two[y])

        loop(0, lx, body)

    def finish(c):
        u = index(last, c)
        loop(0, pieces, lambda o: relay_other(c, o).wait_recv())
        own, other = dfull[u], dother[c]
        fill(jnp.where(me_g == 0, own, other), jnp.where(me_g == 0, other, own))

        def body(j):
            outs = expand(j * group, group)
            for i in range(group):
                for y in range(2):
                    early[c, y * lx + j * group + i] += outs[i][y]

        if c == 0:
            loop(0, lx // group, body)

    def drain_fields(it, c):
        u = index(it, c)
        core_copy(u).wait_send()
        loop(1, members, lambda o: rs_copy(u, o).wait_send())

        def body(x):
            for slot in range(4):
                halo_copy(it, c, x, slot).wait_send()
            if it == last:
                x1_copy(c, x).wait_send()
                r1_copy(c, x).wait_send()

        loop(0, lx, body)

    def drain_coefficients(it, c):
        u = index(it, c)
        loop(1, pieces, lambda o: ag_copy(u, o).wait_send())
        loop(0, pieces, lambda o: relay_copy(u, o).wait_send())
        if it == last:
            loop(0, pieces, lambda o: y_copy(c, o).wait_send())
            loop(0, pieces, lambda o: relay_other(c, o).wait_send())

    def begin(c):
        def body(x):
            x0[c, x] = take_pair(c, x, x0f)

        loop(0, lx, body)

    def send_pairs(it, c, start, stop):
        loop(start, stop, lambda x: send_halo(it, c, x))

    early_pairs, mid_pairs, late_pairs = 2, 2, 3
    loads[0].wait()
    begin(0)
    pl.semaphore_wait(barrier, total)
    send_pairs(0, 0, 0, lx)
    begin(1)
    send_pairs(0, 1, 0, early_pairs)

    loads[1].wait()
    loop(0, lx, prepare_matrices)
    loads[2].wait()

    def take_source(x):
        for c in range(CHUNKS):
            src[c, x] = take_pair(c, x, srcf)

    loop(0, lx, take_source)
    local_part(0, 0)
    loads[3].wait()
    rows_of_eigen = jnp.concatenate([eig[:, 0:packed], eig[:, packed:nv]], axis=0)
    eig_t[...] = jnp.concatenate([rows_of_eigen, rows_of_eigen], axis=0).T
    loads[4].wait()
    loop(0, lx // 2, prepare_vectors)
    local_part(0, 1)

    halo_part(0, 0, 0)
    halo_part(0, 0, 1)
    send_core(0, 0)
    send_sums(0, 0)
    send_pairs(0, 1, early_pairs, lx)
    halo_part(0, 1, 0)
    send_scaled(0, 0)
    halo_part(0, 1, 1)
    send_core(0, 1)
    relay(0, 0)
    send_sums(0, 1)
    gathered(0, 0)
    update(0, mid_pairs)
    local_part(1, 0)
    send_scaled(0, 1)
    send_pairs(1, 0, mid_pairs, lx)
    halo_part(1, 0, 0)
    relay(0, 1)
    gathered(0, 1)
    update(1, late_pairs)
    local_part(1, 1)
    halo_part(1, 0, 1)
    send_core(1, 0)
    send_sums(1, 0)
    send_pairs(1, 1, late_pairs, lx)
    halo_part(1, 1, 0)
    send_scaled(1, 0)
    for c in range(CHUNKS):
        drain_fields(0, c)
        drain_coefficients(0, c)
    halo_part(1, 1, 1)
    send_core(1, 1)
    send_sums(1, 1)
    relay(1, 0)
    gathered(1, 0)
    pass_on(0)
    bases(0)
    send_scaled(1, 1)
    finish(0)
    bases(1)
    drain_fields(1, 0)
    drain_coefficients(1, 0)
    drain_fields(1, 1)
    relay(1, 1)
    gathered(1, 1)
    pass_on(1)
    finish(1)

    drain_coefficients(1, 1)


def finish_kernel(D, res, early, dst, wt, sol_out, res_out, sol, sol_sem, res_sem):
    copies = [pltpu.make_async_copy(res, res_out, res_sem)]
    copies[0].start()
    group = 2
    for start in range(0, D.lx, group):
        outs = expansion(D, wt[start:start + group], dst[...])
        for i in range(group):
            for y in range(D.ly):
                site = y * D.lx + start + i
                sol[site] = join(early[0, site], early[1, site] + outs[i][y])
                copies.append(pltpu.make_async_copy(sol.at[site], sol_out.at[site], sol_sem.at[site]))
                copies[-1].start()
    for copy in copies:
        copy.wait()


def solve(mesh, couplings, source, initial, vectors, inverse_eigen):
    nine, _, _, ly, lx, nc, _ = couplings.shape
    full = source.shape[-1]
    nv = vectors.shape[0]
    D = Dims(mesh, ly, lx, nc, full, nv)
    sites, width = D.sites, D.width
    field = (sites, nc, full)
    mine = (CHUNKS, lx, nc, width)
    units = ITERS * CHUNKS
    block_k = ly * 2 * nc
    vecs = vectors.reshape(nv, sites, 2 * nc).transpose(1, 2, 0)
    any_spec = pl.BlockSpec(memory_space=pl.ANY)
    vmem = pl.BlockSpec(memory_space=pltpu.VMEM)
    dma = pltpu.SemaphoreType.DMA
    out = jax.ShapeDtypeStruct(field, F32)
    between = (
        out,
        jax.ShapeDtypeStruct((CHUNKS, sites, nc, width), F32),
        jax.ShapeDtypeStruct((2 * nv, 2 * width), BF16),
        jax.ShapeDtypeStruct((lx, ly, 2 * nc, 2 * nv), BF16),
    )
    held = pl.pallas_call(
        functools.partial(kernel, D),
        out_shape=between,
        in_specs=[any_spec] * 5,
        out_specs=(vmem,) * 4,
        scratch_shapes=[
            pltpu.VMEM((nine, sites, nc, 2 * nc), F32),
            pltpu.VMEM(field, F32),
            pltpu.VMEM(field, F32),
            pltpu.VMEM((sites, 2 * nc, nv), F32),
            pltpu.VMEM((2, nv), F32),
            dma((5,)),
        ]
        + [pltpu.VMEM(mine, F32)] * 8
        + [
            pltpu.VMEM((lx, 2 * nc, 4 * block_k), BF16),
            pltpu.VMEM((lx, 2 * nc, 4 * block_k), BF16),
            pltpu.VMEM((lx // 2, 2 * nv, 2 * block_k), BF16),
            pltpu.VMEM((lx, 4 * block_k, 2 * width), BF16),
            pltpu.VMEM((4 * block_k, 2 * width), BF16),
            pltpu.VMEM((lx // 2 * block_k, 2 * width), BF16),
            pltpu.VMEM((nv, width), F32),
            pltpu.VMEM((units, 4, lx, nc, width), F32),
            pltpu.VMEM((units, D.packed, width), F32),
            pltpu.VMEM((units, D.half, width), F32),
            pltpu.VMEM((units, D.half, width), F32),
            pltpu.VMEM((units, D.members, D.rows, width), F32),
            pltpu.VMEM((units, D.packed, width), F32),
            pltpu.VMEM((CHUNKS, D.packed, width), F32),
            pltpu.VMEM((D.packed, 8), F32),
            dma((units, 4, lx)),
            dma((units, 4, lx)),
            dma((units,)),
            dma((units,)),
            dma((units, D.members)),
            dma((units, D.members)),
            dma((units, D.pieces)),
            dma((units, D.pieces)),
            dma((units, D.pieces)),
            dma((units, D.pieces)),
            dma((CHUNKS, D.pieces)),
            dma((CHUNKS, D.pieces)),
            dma((CHUNKS, lx)),
            dma((CHUNKS, lx)),
            dma((CHUNKS, lx)),
            dma((CHUNKS, lx)),
            dma((CHUNKS, D.pieces)),
            dma((CHUNKS, D.pieces)),
        ],
        compiler_params=pltpu.CompilerParams(
            collective_id=0, has_side_effects=True, vmem_limit_bytes=44 * 1024 * 1024
        ),
    )(
        pltpu.with_memory_space_constraint(couplings.reshape(nine, sites, nc, 2 * nc), pltpu.HBM),
        pltpu.with_memory_space_constraint(source.reshape(field), pltpu.HBM),
        pltpu.with_memory_space_constraint(initial.reshape(field), pltpu.HBM),
        pltpu.with_memory_space_constraint(vecs, pltpu.HBM),
        pltpu.with_memory_space_constraint(inverse_eigen, pltpu.HBM),
    )
    held = [pltpu.with_memory_space_constraint(value, pltpu.VMEM) for value in held]
    x, r = pl.pallas_call(
        functools.partial(finish_kernel, D),
        out_shape=(out, out),
        in_specs=[vmem] * 4,
        out_specs=(any_spec, any_spec),
        scratch_shapes=[pltpu.VMEM(field, F32), dma((sites,)), dma],
        compiler_params=pltpu.CompilerParams(vmem_limit_bytes=16 * 1024 * 1024),
    )(*held)
    return x.reshape(source.shape), r.reshape(source.shape)


def solution(mesh):
    in_specs = (
        P(None, "tm", "space", None, None, None, None),
        P("tm", "space", None, None, None, None),
        P("tm", "space", None, None, None, None),
        P(None, "tm", "space", None, None, None),
        P(),
    )
    out_specs = (
        P(("groups", "tm"), "space", None, None, None, None),
        P(("groups", "tm"), "space", None, None, None, None),
    )
    return jax.shard_map(
        functools.partial(solve, mesh), mesh=mesh, in_specs=in_specs, out_specs=out_specs, check_vma=False
    )
```

```python
import functools

import jax
import jax.numpy as jnp
from jax import lax
from jax.experimental import pallas as pl
from jax.experimental.pallas import tpu as pltpu
from jax.sharding import PartitionSpec as P

ITERS = 2
MESH = pl.DeviceIdType.MESH
F32 = jnp.float32
BF16 = jnp.bfloat16


def split(value):
    high = value.astype(BF16)
    low = (value - high.astype(F32)).astype(BF16)
    return high, low


def dot(a, b):
    return jnp.dot(a, b, preferred_element_type=F32)


def join(c0, c1):
    width = c0.shape[1]
    real = lax.broadcasted_iota(jnp.int32, c0.shape, 1) < width // 2
    turned0, turned1 = pltpu.roll(c0, width // 2, 1), pltpu.roll(c1, width // 2, 1)
    return jnp.concatenate([jnp.where(real, c0, turned1), jnp.where(real, turned0, c1)], axis=1)


def fold(out, count):
    top, bottom = out[0:count], out[count:2 * count]
    width = out.shape[1] // 2
    return (top[:, 0:width] + top[:, width:2 * width]) + (bottom[:, 0:width] + bottom[:, width:2 * width])


def expansion(D, matrices, rhs):
    count = matrices.shape[0]
    out = dot(matrices.reshape(count * D.ly * 2 * D.nc, 2 * D.nv), rhs)
    out = out.reshape(count, D.ly, 2 * D.nc, 2 * D.width)
    return [[fold(out[i, y], D.nc) for y in range(D.ly)] for i in range(count)]


class Dims:
    def __init__(self, mesh, ly, lx, nc, full, nv):
        self.ng, self.ns, self.nt = mesh.shape["groups"], mesh.shape["space"], mesh.shape["tm"]
        self.ly, self.lx, self.nc, self.full, self.nv = ly, lx, nc, full, nv
        assert self.ng == 2 and ly == 2 and lx % 4 == 0
        self.width = full // 2
        self.sites = ly * lx
        self.members = self.ns // 2 * self.nt
        self.packed = nv // 2
        self.half = self.packed // 2
        self.pieces = min(self.members, self.half // 8)
        self.rows = self.half // self.pieces


CHUNKS = 2


def kernel(
    D, coup_h, src_h, x0_h, vec_h, eig_h, res, early, dst, wt,
    coup, srcf, x0f, vec, eig, local_sem,
    x0, x1, r0, r1, src, x1o, r1o, acc,
    m_loc, m_halo, wk, rhs_loc, rhs_halo, rhs_res, proj,
    halo, part, core_in, mine, rs_in, dfull, dother, eig_t,
    halo_send, halo_recv, core_send, core_recv, rs_send, rs_recv, ag_send, ag_recv, re_send, re_recv,
    y_send, y_recv, yx_send, yx_recv, yr_send, yr_recv, r2_send, r2_recv,
):
    ns, nt, sites, nc, lx, ly = D.ns, D.nt, D.sites, D.nc, D.lx, D.ly
    nv, packed, half, rows, pieces, members = D.nv, D.packed, D.half, D.rows, D.pieces, D.members
    width, full = D.width, D.full
    quarter = width // 4
    me_g, me_s, me_t = lax.axis_index("groups"), lax.axis_index("space"), lax.axis_index("tm")
    parity = lax.rem(me_s, 2)
    pairs = ns // 2
    rank = me_t * pairs + me_s // 2
    partner = {"groups": me_g, "space": me_s + 1 - 2 * parity, "tm": me_t}
    other_group = {"groups": 1 - me_g, "space": me_s, "tm": me_t}
    last = ITERS - 1
    block_k = ly * 2 * nc

    loads = [
        pltpu.make_async_copy(x0_h, x0f, local_sem.at[0]),
        pltpu.make_async_copy(coup_h, coup, local_sem.at[1]),
        pltpu.make_async_copy(src_h, srcf, local_sem.at[2]),
        pltpu.make_async_copy(eig_h, eig, local_sem.at[3]),
        pltpu.make_async_copy(vec_h, vec, local_sem.at[4]),
    ]
    for load in loads:
        load.start()

    barrier = pltpu.get_barrier_semaphore()
    total = ns * nt
    flat = me_t * ns + me_s

    def greet(o, carry):
        other = lax.rem(flat + o, total)
        pl.semaphore_signal(
            barrier, inc=1,
            device_id={"groups": me_g, "space": lax.rem(other, ns), "tm": other // ns}, device_id_type=MESH,
        )
        return carry

    lax.fori_loop(1, total, greet, 0)
    pl.semaphore_signal(barrier, inc=1, device_id=other_group, device_id_type=MESH)

    def lane(shape):
        return lax.broadcasted_iota(jnp.int32, shape, 1)

    def turn(v):
        return pltpu.roll(v, width // 2, 1)

    def later(v):
        return pltpu.roll(v, quarter, 1)

    def sooner(v):
        return pltpu.roll(v, width - quarter, 1)

    def real_lanes(v):
        return lane(v.shape) < width // 2

    def first_lanes(v):
        return lax.rem(lane(v.shape), width // 2) < quarter

    def times_i(v):
        turned = turn(v)
        return jnp.where(real_lanes(v), -turned, turned)

    def pack(even, odd):
        return jnp.where(first_lanes(even), even, later(odd)), jnp.where(first_lanes(even), sooner(even), odd)

    def take(c, value):
        re, im = value[:, 0:width], value[:, width:full]
        if c == 0:
            return jnp.where(real_lanes(re), re, turn(im))
        return jnp.where(real_lanes(re), turn(re), im)

    def take_pair(c, x, ref):
        of_g0, of_g1 = pack(take(c, ref[x]), take(c, ref[lx + x]))
        return jnp.where(me_g == 0, of_g0, of_g1)

    def groups_of(own, other):
        return pack(jnp.where(me_g == 0, own, other), jnp.where(me_g == 0, other, own))

    def stacked(value, turned):
        high, low = split(value)
        t_high, t_low = split(turned)
        return jnp.concatenate(
            [jnp.concatenate([high, t_high], axis=0), jnp.concatenate([low, t_low], axis=0)], axis=1
        )

    keep = jnp.where(lax.rem(lane((2 * nc, 2 * width)), width // 2) < quarter, 1.0, 0.0).astype(BF16)

    def masked(value, turned):
        both = stacked(value, turned)
        even = both * keep
        return jnp.concatenate([even, both - even], axis=0)

    up_s, down_s = lax.rem(me_s + 1, ns), lax.rem(me_s + ns - 1, ns)
    up_t, down_t = lax.rem(me_t + 1, nt), lax.rem(me_t + nt - 1, nt)
    targets = (
        (2, {"groups": me_g, "space": me_s, "tm": down_t}),
        (3, {"groups": me_g, "space": me_s, "tm": up_t}),
        (0, {"groups": me_g, "space": down_s, "tm": me_t}),
        (1, {"groups": me_g, "space": up_s, "tm": me_t}),
    )
    target_of = dict(targets)

    def index(it, c):
        return it * CHUNKS + c

    def halo_copy(it, c, x, slot):
        source = x0 if it == 0 else x1
        u = index(it, c)
        return pltpu.make_async_remote_copy(
            src_ref=source.at[c, x],
            dst_ref=halo.at[u, slot, x],
            send_sem=halo_send.at[u, slot, x],
            recv_sem=halo_recv.at[u, slot, x],
            device_id=target_of[slot],
            device_id_type=MESH,
        )

    def send_halo(it, c, x):
        for slot, _ in targets:
            halo_copy(it, c, x, slot).start()

    def x1_copy(c, x):
        return pltpu.make_async_remote_copy(
            src_ref=x1.at[c, x], dst_ref=x1o.at[c, x], send_sem=yx_send.at[c, x], recv_sem=yx_recv.at[c, x],
            device_id=other_group, device_id_type=MESH,
        )

    def r1_copy(c, x):
        return pltpu.make_async_remote_copy(
            src_ref=r1.at[c, x], dst_ref=r1o.at[c, x], send_sem=yr_send.at[c, x], recv_sem=yr_recv.at[c, x],
            device_id=other_group, device_id_type=MESH,
        )

    def loop(start, stop, action):
        def body(o, carry):
            action(o)
            return carry

        lax.fori_loop(start, stop, body, 0)

    sign_up = jnp.where(me_t == nt - 1, -1.0, 1.0).astype(F32)
    sign_down = jnp.where(me_t == 0, -1.0, 1.0).astype(F32)

    def prepare_matrices(x):
        def both(value_of):
            high, low = split(jnp.concatenate([value_of(x), value_of(lx + x)], axis=1))
            return jnp.concatenate([high, low], axis=0)

        for d in range(3):
            m_loc[x, :, d * block_k:(d + 1) * block_k] = both(lambda site: coup[d, site])
        m_loc[x, :, 3 * block_k:4 * block_k] = both(lambda site: coup[3, site] + coup[4, site])
        for d, sign in enumerate((None, None, sign_up, sign_down)):
            m_halo[x, :, d * block_k:(d + 1) * block_k] = both(
                lambda site: coup[5 + d, site] if sign is None else coup[5 + d, site] * sign
            )

    def prepare_vectors(h):
        for i in range(2):
            x = 2 * h + i
            even, odd = vec[x], vec[lx + x]
            high, low = split(jnp.concatenate([even, odd], axis=0).T)
            wk[h, 0:nv, i * block_k:(i + 1) * block_k] = high
            wk[h, nv:2 * nv, i * block_k:(i + 1) * block_k] = low
            for y, value in enumerate((even, odd)):
                high, low = split(value)
                wt[x, y, 0:nc, 0:nv] = high[0:nc]
                wt[x, y, 0:nc, nv:2 * nv] = high[nc:2 * nc]
                wt[x, y, nc:2 * nc, 0:nv] = low[0:nc]
                wt[x, y, nc:2 * nc, nv:2 * nv] = low[nc:2 * nc]

    def local_part(it, c):
        field = x0 if it == 0 else x1

        def place(x):
            value = field[c, x]
            mine = masked(value, times_i(value))
            rhs_loc[x, 0:block_k, :] = mine
            rhs_loc[lax.rem(x + lx - 1, lx), block_k:2 * block_k, :] = mine
            rhs_loc[lax.rem(x + 1, lx), 2 * block_k:3 * block_k, :] = mine
            other = jnp.where(first_lanes(value), sooner(value), later(value))
            rhs_loc[x, 3 * block_k:4 * block_k, :] = masked(other, times_i(other))

        loop(0, lx, place)

        def multiply(x):
            acc[c, x] = src[c, x] - fold(dot(m_loc[x], rhs_loc[x]), nc)

        loop(0, lx, multiply)

    def halo_part(it, c, part_of):
        out = r0 if it == 0 else r1

        def body(j):
            x = part_of * (lx // 2) + j
            for slot in range(4):
                halo_copy(it, c, x, slot).wait_recv()
                value = halo[index(it, c), slot, x]
                rhs_halo[slot * block_k:(slot + 1) * block_k, :] = masked(value, times_i(value))
            residual = acc[c, x] - fold(dot(m_halo[x], rhs_halo[...]), nc)
            out[c, x] = residual
            if it == last:
                r1_copy(c, x).start()
            rhs_res[pl.ds(pl.multiple_of(j * block_k, 16), block_k), :] = masked(residual, -times_i(residual))

        loop(0, lx // 2, body)
        total = None
        for h in range(lx // 4):
            value = fold(dot(wk[part_of * (lx // 4) + h], rhs_res[2 * h * block_k:2 * (h + 1) * block_k, :]), nv)
            total = value if total is None else total + value
        if part_of == 0:
            proj[...] = total
        else:
            total = total + proj[...]
            top, bottom = total[0:packed], total[packed:nv]
            part[index(it, c)] = jnp.where(first_lanes(top), top + sooner(top), bottom + later(bottom))

    def member(q):
        return {"groups": me_g, "space": lax.rem(q, pairs) * 2 + parity, "tm": q // pairs}

    my_rows = pl.multiple_of(parity * half, 8)
    other_rows = pl.multiple_of((1 - parity) * half, 8)
    piece = lax.rem(rank, pieces)
    block = rank - piece
    piece_row = pl.multiple_of(my_rows + piece * rows, 8)

    def core_copy(u):
        return pltpu.make_async_remote_copy(
            src_ref=part.at[u, pl.ds(other_rows, half)],
            dst_ref=core_in.at[u],
            send_sem=core_send.at[u],
            recv_sem=core_recv.at[u],
            device_id=partner,
            device_id_type=MESH,
        )

    def rs_copy(u, o):
        q = lax.rem(rank + o, members)
        row = pl.multiple_of(lax.rem(q, pieces) * rows, 8)
        return pltpu.make_async_remote_copy(
            src_ref=mine.at[u, pl.ds(row, rows)],
            dst_ref=rs_in.at[u, o],
            send_sem=rs_send.at[u, o],
            recv_sem=rs_recv.at[u, o],
            device_id=member(q),
            device_id_type=MESH,
        )

    def ag_copy(u, o):
        q = block + lax.rem(piece + o, pieces)
        return pltpu.make_async_remote_copy(
            src_ref=dfull.at[u, pl.ds(piece_row, rows)],
            dst_ref=dfull.at[u, pl.ds(piece_row, rows)],
            send_sem=ag_send.at[u, o],
            recv_sem=ag_recv.at[u, o],
            device_id=member(q),
            device_id_type=MESH,
        )

    def row_of(o):
        return pl.multiple_of(my_rows + lax.rem(piece + pieces - o, pieces) * rows, 8)

    def relay_copy(u, o):
        return pltpu.make_async_remote_copy(
            src_ref=dfull.at[u, pl.ds(row_of(o), rows)],
            dst_ref=dfull.at[u, pl.ds(row_of(o), rows)],
            send_sem=re_send.at[u, o],
            recv_sem=re_recv.at[u, o],
            device_id=partner,
            device_id_type=MESH,
        )

    def y_copy(c, o):
        return pltpu.make_async_remote_copy(
            src_ref=dfull.at[index(last, c), pl.ds(row_of(o), rows)],
            dst_ref=dother.at[c, pl.ds(row_of(o), rows)],
            send_sem=y_send.at[c, o],
            recv_sem=y_recv.at[c, o],
            device_id=other_group,
            device_id_type=MESH,
        )

    def relay_other(c, o):
        return pltpu.make_async_remote_copy(
            src_ref=dother.at[c, pl.ds(row_of(o), rows)],
            dst_ref=dother.at[c, pl.ds(row_of(o), rows)],
            send_sem=r2_send.at[c, o],
            recv_sem=r2_recv.at[c, o],
            device_id=partner,
            device_id_type=MESH,
        )

    def send_core(it, c):
        core_copy(index(it, c)).start()

    def send_sums(it, c):
        u = index(it, c)
        core_copy(u).wait_recv()
        mine[u] = part[u, pl.ds(my_rows, half), :] + core_in[u]
        loop(1, members, lambda o: rs_copy(u, o).start())

    def send_scaled(it, c):
        u = index(it, c)
        own = mine[u, pl.ds(pl.multiple_of(piece * rows, 8), rows), :]

        def gather(o, total):
            rs_copy(u, o).wait_recv()
            return total + rs_in[u, o]

        coef = lax.fori_loop(1, members, gather, own)
        eigen = eig_t[pl.ds(piece_row, rows), :]
        first = first_lanes(coef)
        real = jnp.where(first, eigen[:, 0:1], eigen[:, 2:3])
        imag = jnp.where(first, eigen[:, 1:2], eigen[:, 3:4])
        dfull[u, pl.ds(piece_row, rows), :] = real * coef + imag * times_i(coef)
        loop(1, pieces, lambda o: ag_copy(u, o).start())
        relay_copy(u, 0).start()
        if it == last:
            y_copy(c, 0).start()

    def relay(it, c):
        u = index(it, c)

        def forward(o):
            ag_copy(u, o).wait_recv()
            relay_copy(u, o).start()
            if it == last:
                y_copy(c, o).start()

        loop(1, pieces, forward)

    def gathered(it, c):
        loop(0, pieces, lambda o: relay_copy(index(it, c), o).wait_recv())

    group = 2

    def fill(even, odd):
        upper = jnp.where(first_lanes(even), even, later(odd))
        lower = jnp.where(first_lanes(even), sooner(even), odd)
        value = jnp.concatenate([upper, lower], axis=0)
        dst[...] = stacked(value, times_i(value))

    def expand(start, count):
        return expansion(D, wt[pl.ds(start, count)], dst[...])

    def update(c, pairs_now):
        group = 1
        u = index(0, c)
        fill(dfull[u], dfull[u])

        def body(j):
            outs = expand(j * group, group)
            for i in range(group):
                x = j * group + i
                even, odd = outs[i]
                x1[c, x] = x0[c, x] + jnp.where(first_lanes(even), even, odd) + 0.5 * r0[c, x]

                @pl.when(x < pairs_now)
                def _():
                    send_halo(1, c, x)

                x1_copy(c, x).start()

        loop(0, lx // group, body)

    def pass_on(c):
        def body(o):
            y_copy(c, o).wait_recv()
            relay_other(c, o).start()

        loop(0, pieces, body)

    def bases(c):
        def body(x):
            x1_copy(c, x).wait_recv()
            r1_copy(c, x).wait_recv()
            own_r, other_r = r1[c, x], r1o[c, x]
            one = groups_of(x1[c, x] + 0.5 * own_r, x1o[c, x] + 0.5 * other_r)
            two = groups_of(own_r, other_r)
            for y in range(2):
                early[c, y * lx + x] = one[y]
                if c == 0:
                    res[y * lx + x, :, 0:width] = two[y]
                else:
                    res[y * lx + x] = join(res[y * lx + x, :, 0:width], two[y])

        loop(0, lx, body)

    def finish(c):
        u = index(last, c)
        loop(0, pieces, lambda o: relay_other(c, o).wait_recv())
        own, other = dfull[u], dother[c]
        fill(jnp.where(me_g == 0, own, other), jnp.where(me_g == 0, other, own))

        def body(j):
            outs = expand(j * group, group)
            for i in range(group):
                for y in range(2):
                    early[c, y * lx + j * group + i] += outs[i][y]

        if c == 0:
            loop(0, lx // group, body)

    def drain_fields(it, c):
        u = index(it, c)
        core_copy(u).wait_send()
        loop(1, members, lambda o: rs_copy(u, o).wait_send())

        def body(x):
            for slot in range(4):
                halo_copy(it, c, x, slot).wait_send()
            if it == last:
                x1_copy(c, x).wait_send()
                r1_copy(c, x).wait_send()

        loop(0, lx, body)

    def drain_coefficients(it, c):
        u = index(it, c)
        loop(1, pieces, lambda o: ag_copy(u, o).wait_send())
        loop(0, pieces, lambda o: relay_copy(u, o).wait_send())
        if it == last:
            loop(0, pieces, lambda o: y_copy(c, o).wait_send())
            loop(0, pieces, lambda o: relay_other(c, o).wait_send())

    def begin(c):
        def body(x):
            x0[c, x] = take_pair(c, x, x0f)

        loop(0, lx, body)

    def send_pairs(it, c, start, stop):
        loop(start, stop, lambda x: send_halo(it, c, x))

    early_pairs, mid_pairs, late_pairs = 2, 2, 3
    loads[0].wait()
    begin(0)
    pl.semaphore_wait(barrier, total)
    send_pairs(0, 0, 0, lx)
    begin(1)
    send_pairs(0, 1, 0, early_pairs)

    loads[1].wait()
    loop(0, lx, prepare_matrices)
    loads[2].wait()

    def take_source(x):
        for c in range(CHUNKS):
            src[c, x] = take_pair(c, x, srcf)

    loop(0, lx, take_source)
    local_part(0, 0)
    loads[3].wait()
    rows_of_eigen = jnp.concatenate([eig[:, 0:packed], eig[:, packed:nv]], axis=0)
    eig_t[...] = jnp.concatenate([rows_of_eigen, rows_of_eigen], axis=0).T
    loads[4].wait()
    loop(0, lx // 2, prepare_vectors)
    local_part(0, 1)

    halo_part(0, 0, 0)
    halo_part(0, 0, 1)
    send_core(0, 0)
    send_sums(0, 0)
    send_pairs(0, 1, early_pairs, lx)
    halo_part(0, 1, 0)
    send_scaled(0, 0)
    halo_part(0, 1, 1)
    send_core(0, 1)
    relay(0, 0)
    send_sums(0, 1)
    gathered(0, 0)
    update(0, mid_pairs)
    local_part(1, 0)
    send_scaled(0, 1)
    send_pairs(1, 0, mid_pairs, lx)
    halo_part(1, 0, 0)
    relay(0, 1)
    gathered(0, 1)
    update(1, late_pairs)
    local_part(1, 1)
    halo_part(1, 0, 1)
    send_core(1, 0)
    send_sums(1, 0)
    send_pairs(1, 1, late_pairs, lx)
    halo_part(1, 1, 0)
    send_scaled(1, 0)
    for c in range(CHUNKS):
        drain_fields(0, c)
        drain_coefficients(0, c)
    halo_part(1, 1, 1)
    send_core(1, 1)
    send_sums(1, 1)
    relay(1, 0)
    gathered(1, 0)
    pass_on(0)
    bases(0)
    send_scaled(1, 1)
    finish(0)
    bases(1)
    drain_fields(1, 0)
    drain_coefficients(1, 0)
    drain_fields(1, 1)
    relay(1, 1)
    gathered(1, 1)
    pass_on(1)
    finish(1)

    drain_coefficients(1, 1)


def finish_kernel(D, res, early, dst, wt, sol_out, res_out, sol, sol_sem, res_sem):
    copies = [pltpu.make_async_copy(res, res_out, res_sem)]
    copies[0].start()
    group = 2
    for start in range(0, D.lx, group):
        outs = expansion(D, wt[start:start + group], dst[...])
        for i in range(group):
            for y in range(D.ly):
                site = y * D.lx + start + i
                sol[site] = join(early[0, site], early[1, site] + outs[i][y])
                copies.append(pltpu.make_async_copy(sol.at[site], sol_out.at[site], sol_sem.at[site]))
                copies[-1].start()
    for copy in copies:
        copy.wait()


def solve(mesh, couplings, source, initial, vectors, inverse_eigen):
    nine, _, _, ly, lx, nc, _ = couplings.shape
    full = source.shape[-1]
    nv = vectors.shape[0]
    D = Dims(mesh, ly, lx, nc, full, nv)
    sites, width = D.sites, D.width
    field = (sites, nc, full)
    mine = (CHUNKS, lx, nc, width)
    units = ITERS * CHUNKS
    block_k = ly * 2 * nc
    vecs = vectors.reshape(nv, sites, 2 * nc).transpose(1, 2, 0)
    any_spec = pl.BlockSpec(memory_space=pl.ANY)
    vmem = pl.BlockSpec(memory_space=pltpu.VMEM)
    dma = pltpu.SemaphoreType.DMA
    out = jax.ShapeDtypeStruct(field, F32)
    between = (
        out,
        jax.ShapeDtypeStruct((CHUNKS, sites, nc, width), F32),
        jax.ShapeDtypeStruct((2 * nv, 2 * width), BF16),
        jax.ShapeDtypeStruct((lx, ly, 2 * nc, 2 * nv), BF16),
    )
    held = pl.pallas_call(
        functools.partial(kernel, D),
        out_shape=between,
        in_specs=[any_spec] * 5,
        out_specs=(vmem,) * 4,
        scratch_shapes=[
            pltpu.VMEM((nine, sites, nc, 2 * nc), F32),
            pltpu.VMEM(field, F32),
            pltpu.VMEM(field, F32),
            pltpu.VMEM((sites, 2 * nc, nv), F32),
            pltpu.VMEM((2, nv), F32),
            dma((5,)),
        ]
        + [pltpu.VMEM(mine, F32)] * 8
        + [
            pltpu.VMEM((lx, 2 * nc, 4 * block_k), BF16),
            pltpu.VMEM((lx, 2 * nc, 4 * block_k), BF16),
            pltpu.VMEM((lx // 2, 2 * nv, 2 * block_k), BF16),
            pltpu.VMEM((lx, 4 * block_k, 2 * width), BF16),
            pltpu.VMEM((4 * block_k, 2 * width), BF16),
            pltpu.VMEM((lx // 2 * block_k, 2 * width), BF16),
            pltpu.VMEM((nv, width), F32),
            pltpu.VMEM((units, 4, lx, nc, width), F32),
            pltpu.VMEM((units, D.packed, width), F32),
            pltpu.VMEM((units, D.half, width), F32),
            pltpu.VMEM((units, D.half, width), F32),
            pltpu.VMEM((units, D.members, D.rows, width), F32),
            pltpu.VMEM((units, D.packed, width), F32),
            pltpu.VMEM((CHUNKS, D.packed, width), F32),
            pltpu.VMEM((D.packed, 8), F32),
            dma((units, 4, lx)),
            dma((units, 4, lx)),
            dma((units,)),
            dma((units,)),
            dma((units, D.members)),
            dma((units, D.members)),
            dma((units, D.pieces)),
            dma((units, D.pieces)),
            dma((units, D.pieces)),
            dma((units, D.pieces)),
            dma((CHUNKS, D.pieces)),
            dma((CHUNKS, D.pieces)),
            dma((CHUNKS, lx)),
            dma((CHUNKS, lx)),
            dma((CHUNKS, lx)),
            dma((CHUNKS, lx)),
            dma((CHUNKS, D.pieces)),
            dma((CHUNKS, D.pieces)),
        ],
        compiler_params=pltpu.CompilerParams(
            collective_id=0, has_side_effects=True, vmem_limit_bytes=44 * 1024 * 1024
        ),
    )(
        pltpu.with_memory_space_constraint(couplings.reshape(nine, sites, nc, 2 * nc), pltpu.HBM),
        pltpu.with_memory_space_constraint(source.reshape(field), pltpu.HBM),
        pltpu.with_memory_space_constraint(initial.reshape(field), pltpu.HBM),
        pltpu.with_memory_space_constraint(vecs, pltpu.HBM),
        pltpu.with_memory_space_constraint(inverse_eigen, pltpu.HBM),
    )
    held = [pltpu.with_memory_space_constraint(value, pltpu.VMEM) for value in held]
    x, r = pl.pallas_call(
        functools.partial(finish_kernel, D),
        out_shape=(out, out),
        in_specs=[vmem] * 4,
        out_specs=(any_spec, any_spec),
        scratch_shapes=[pltpu.VMEM(field, F32), dma((sites,)), dma],
        compiler_params=pltpu.CompilerParams(vmem_limit_bytes=16 * 1024 * 1024),
    )(*held)
    return x.reshape(source.shape), r.reshape(source.shape)


def solution(mesh):
    in_specs = (
        P(None, "tm", "space", None, None, None, None),
        P("tm", "space", None, None, None, None),
        P("tm", "space", None, None, None, None),
        P(None, "tm", "space", None, None, None),
        P(),
    )
    out_specs = (
        P(("groups", "tm"), "space", None, None, None, None),
        P(("groups", "tm"), "space", None, None, None, None),
    )
    return jax.shard_map(
        functools.partial(solve, mesh), mesh=mesh, in_specs=in_specs, out_specs=out_specs, check_vma=False
    )
```

```python
import functools

import jax
import jax.numpy as jnp
from jax import lax
from jax.experimental import pallas as pl
from jax.experimental.pallas import tpu as pltpu
from jax.sharding import PartitionSpec as P

ITERS = 2
MESH = pl.DeviceIdType.MESH
F32 = jnp.float32
BF16 = jnp.bfloat16


def split(value):
    high = value.astype(BF16)
    low = (value - high.astype(F32)).astype(BF16)
    return high, low


def dot(a, b):
    return jnp.dot(a, b, preferred_element_type=F32)


def join(c0, c1):
    width = c0.shape[1]
    real = lax.broadcasted_iota(jnp.int32, c0.shape, 1) < width // 2
    turned0, turned1 = pltpu.roll(c0, width // 2, 1), pltpu.roll(c1, width // 2, 1)
    return jnp.concatenate([jnp.where(real, c0, turned1), jnp.where(real, turned0, c1)], axis=1)


def fold(out, count):
    top, bottom = out[0:count], out[count:2 * count]
    width = out.shape[1] // 2
    return (top[:, 0:width] + top[:, width:2 * width]) + (bottom[:, 0:width] + bottom[:, width:2 * width])


def expansion(D, matrices, rhs):
    count = matrices.shape[0]
    out = dot(matrices.reshape(count * D.ly * 2 * D.nc, 2 * D.nv), rhs)
    out = out.reshape(count, D.ly, 2 * D.nc, 2 * D.width)
    return [[fold(out[i, y], D.nc) for y in range(D.ly)] for i in range(count)]


class Dims:
    def __init__(self, mesh, ly, lx, nc, full, nv):
        self.ng, self.ns, self.nt = mesh.shape["groups"], mesh.shape["space"], mesh.shape["tm"]
        self.ly, self.lx, self.nc, self.full, self.nv = ly, lx, nc, full, nv
        assert self.ng == 2 and ly == 2 and lx % 4 == 0
        self.width = full // 2
        self.sites = ly * lx
        self.members = self.ns // 2 * self.nt
        self.packed = nv // 2
        self.half = self.packed // 2
        self.pieces = min(self.members, self.half // 8)
        self.rows = self.half // self.pieces


CHUNKS = 2


def kernel(
    D, coup_h, src_h, x0_h, vec_h, eig_h, res, early, dst, wt,
    coup, srcf, x0f, vec, eig, local_sem,
    x0, x1, r0, r1, src, x1o, r1o, acc,
    m_loc, m_halo, wk, rhs_loc, rhs_halo, rhs_res, proj,
    halo, part, core_in, mine, rs_in, dfull, dother, eig_t,
    halo_send, halo_recv, core_send, core_recv, rs_send, rs_recv, ag_send, ag_recv, re_send, re_recv,
    y_send, y_recv, yx_send, yx_recv, yr_send, yr_recv, r2_send, r2_recv,
):
    ns, nt, sites, nc, lx, ly = D.ns, D.nt, D.sites, D.nc, D.lx, D.ly
    nv, packed, half, rows, pieces, members = D.nv, D.packed, D.half, D.rows, D.pieces, D.members
    width, full = D.width, D.full
    quarter = width // 4
    me_g, me_s, me_t = lax.axis_index("groups"), lax.axis_index("space"), lax.axis_index("tm")
    parity = lax.rem(me_s, 2)
    pairs = ns // 2
    rank = me_t * pairs + me_s // 2
    partner = {"groups": me_g, "space": me_s + 1 - 2 * parity, "tm": me_t}
    other_group = {"groups": 1 - me_g, "space": me_s, "tm": me_t}
    last = ITERS - 1
    block_k = ly * 2 * nc

    loads = [
        pltpu.make_async_copy(x0_h, x0f, local_sem.at[0]),
        pltpu.make_async_copy(coup_h, coup, local_sem.at[1]),
        pltpu.make_async_copy(src_h, srcf, local_sem.at[2]),
        pltpu.make_async_copy(eig_h, eig, local_sem.at[3]),
        pltpu.make_async_copy(vec_h, vec, local_sem.at[4]),
    ]
    for load in loads:
        load.start()

    barrier = pltpu.get_barrier_semaphore()
    total = ns * nt
    flat = me_t * ns + me_s

    def greet(o, carry):
        other = lax.rem(flat + o, total)
        pl.semaphore_signal(
            barrier, inc=1,
            device_id={"groups": me_g, "space": lax.rem(other, ns), "tm": other // ns}, device_id_type=MESH,
        )
        return carry

    lax.fori_loop(1, total, greet, 0)
    pl.semaphore_signal(barrier, inc=1, device_id=other_group, device_id_type=MESH)

    def lane(shape):
        return lax.broadcasted_iota(jnp.int32, shape, 1)

    def turn(v):
        return pltpu.roll(v, width // 2, 1)

    def later(v):
        return pltpu.roll(v, quarter, 1)

    def sooner(v):
        return pltpu.roll(v, width - quarter, 1)

    def real_lanes(v):
        return lane(v.shape) < width // 2

    def first_lanes(v):
        return lax.rem(lane(v.shape), width // 2) < quarter

    def times_i(v):
        turned = turn(v)
        return jnp.where(real_lanes(v), -turned, turned)

    def pack(even, odd):
        return jnp.where(first_lanes(even), even, later(odd)), jnp.where(first_lanes(even), sooner(even), odd)

    def take(c, value):
        re, im = value[:, 0:width], value[:, width:full]
        if c == 0:
            return jnp.where(real_lanes(re), re, turn(im))
        return jnp.where(real_lanes(re), turn(re), im)

    def take_pair(c, x, ref):
        of_g0, of_g1 = pack(take(c, ref[x]), take(c, ref[lx + x]))
        return jnp.where(me_g == 0, of_g0, of_g1)

    def groups_of(own, other):
        return pack(jnp.where(me_g == 0, own, other), jnp.where(me_g == 0, other, own))

    def stacked(value, turned):
        high, low = split(value)
        t_high, t_low = split(turned)
        return jnp.concatenate(
            [jnp.concatenate([high, t_high], axis=0), jnp.concatenate([low, t_low], axis=0)], axis=1
        )

    keep = jnp.where(lax.rem(lane((2 * nc, 2 * width)), width // 2) < quarter, 1.0, 0.0).astype(BF16)

    def masked(value, turned):
        both = stacked(value, turned)
        even = both * keep
        return jnp.concatenate([even, both - even], axis=0)

    up_s, down_s = lax.rem(me_s + 1, ns), lax.rem(me_s + ns - 1, ns)
    up_t, down_t = lax.rem(me_t + 1, nt), lax.rem(me_t + nt - 1, nt)
    targets = (
        (2, {"groups": me_g, "space": me_s, "tm": down_t}),
        (3, {"groups": me_g, "space": me_s, "tm": up_t}),
        (0, {"groups": me_g, "space": down_s, "tm": me_t}),
        (1, {"groups": me_g, "space": up_s, "tm": me_t}),
    )
    target_of = dict(targets)

    def index(it, c):
        return it * CHUNKS + c

    def halo_copy(it, c, x, slot):
        source = x0 if it == 0 else x1
        u = index(it, c)
        return pltpu.make_async_remote_copy(
            src_ref=source.at[c, x],
            dst_ref=halo.at[u, slot, x],
            send_sem=halo_send.at[u, slot, x],
            recv_sem=halo_recv.at[u, slot, x],
            device_id=target_of[slot],
            device_id_type=MESH,
        )

    def send_halo(it, c, x):
        for slot, _ in targets:
            halo_copy(it, c, x, slot).start()

    def x1_copy(c, x):
        return pltpu.make_async_remote_copy(
            src_ref=x1.at[c, x], dst_ref=x1o.at[c, x], send_sem=yx_send.at[c, x], recv_sem=yx_recv.at[c, x],
            device_id=other_group, device_id_type=MESH,
        )

    def r1_copy(c, x):
        return pltpu.make_async_remote_copy(
            src_ref=r1.at[c, x], dst_ref=r1o.at[c, x], send_sem=yr_send.at[c, x], recv_sem=yr_recv.at[c, x],
            device_id=other_group, device_id_type=MESH,
        )

    def loop(start, stop, action):
        def body(o, carry):
            action(o)
            return carry

        lax.fori_loop(start, stop, body, 0)

    sign_up = jnp.where(me_t == nt - 1, -1.0, 1.0).astype(F32)
    sign_down = jnp.where(me_t == 0, -1.0, 1.0).astype(F32)

    def prepare_matrices(x):
        def both(value_of):
            high, low = split(jnp.concatenate([value_of(x), value_of(lx + x)], axis=1))
            return jnp.concatenate([high, low], axis=0)

        for d in range(3):
            m_loc[x, :, d * block_k:(d + 1) * block_k] = both(lambda site: coup[d, site])
        m_loc[x, :, 3 * block_k:4 * block_k] = both(lambda site: coup[3, site] + coup[4, site])
        for d, sign in enumerate((None, None, sign_up, sign_down)):
            m_halo[x, :, d * block_k:(d + 1) * block_k] = both(
                lambda site: coup[5 + d, site] if sign is None else coup[5 + d, site] * sign
            )

    def prepare_vectors(h):
        for i in range(2):
            x = 2 * h + i
            even, odd = vec[x], vec[lx + x]
            high, low = split(jnp.concatenate([even, odd], axis=0).T)
            wk[h, 0:nv, i * block_k:(i + 1) * block_k] = high
            wk[h, nv:2 * nv, i * block_k:(i + 1) * block_k] = low
            for y, value in enumerate((even, odd)):
                high, low = split(value)
                wt[x, y, 0:nc, 0:nv] = high[0:nc]
                wt[x, y, 0:nc, nv:2 * nv] = high[nc:2 * nc]
                wt[x, y, nc:2 * nc, 0:nv] = low[0:nc]
                wt[x, y, nc:2 * nc, nv:2 * nv] = low[nc:2 * nc]

    def local_part(it, c):
        field = x0 if it == 0 else x1

        def place(x):
            value = field[c, x]
            mine = masked(value, times_i(value))
            rhs_loc[x, 0:block_k, :] = mine
            rhs_loc[lax.rem(x + lx - 1, lx), block_k:2 * block_k, :] = mine
            rhs_loc[lax.rem(x + 1, lx), 2 * block_k:3 * block_k, :] = mine
            other = jnp.where(first_lanes(value), sooner(value), later(value))
            rhs_loc[x, 3 * block_k:4 * block_k, :] = masked(other, times_i(other))

        loop(0, lx, place)

        def multiply(x):
            acc[c, x] = src[c, x] - fold(dot(m_loc[x], rhs_loc[x]), nc)

        loop(0, lx, multiply)

    def halo_part(it, c, part_of):
        out = r0 if it == 0 else r1

        def body(j):
            x = part_of * (lx // 2) + j
            for slot in range(4):
                halo_copy(it, c, x, slot).wait_recv()
                value = halo[index(it, c), slot, x]
                rhs_halo[slot * block_k:(slot + 1) * block_k, :] = masked(value, times_i(value))
            residual = acc[c, x] - fold(dot(m_halo[x], rhs_halo[...]), nc)
            out[c, x] = residual
            if it == last:
                r1_copy(c, x).start()
            rhs_res[pl.ds(pl.multiple_of(j * block_k, 16), block_k), :] = masked(residual, -times_i(residual))

        loop(0, lx // 2, body)
        total = None
        for h in range(lx // 4):
            value = fold(dot(wk[part_of * (lx // 4) + h], rhs_res[2 * h * block_k:2 * (h + 1) * block_k, :]), nv)
            total = value if total is None else total + value
        if part_of == 0:
            proj[...] = total
        else:
            total = total + proj[...]
            top, bottom = total[0:packed], total[packed:nv]
            part[index(it, c)] = jnp.where(first_lanes(top), top + sooner(top), bottom + later(bottom))

    def member(q):
        return {"groups": me_g, "space": lax.rem(q, pairs) * 2 + parity, "tm": q // pairs}

    my_rows = pl.multiple_of(parity * half, 8)
    other_rows = pl.multiple_of((1 - parity) * half, 8)
    piece = lax.rem(rank, pieces)
    block = rank - piece
    piece_row = pl.multiple_of(my_rows + piece * rows, 8)

    def core_copy(u):
        return pltpu.make_async_remote_copy(
            src_ref=part.at[u, pl.ds(other_rows, half)],
            dst_ref=core_in.at[u],
            send_sem=core_send.at[u],
            recv_sem=core_recv.at[u],
            device_id=partner,
            device_id_type=MESH,
        )

    def rs_copy(u, o):
        q = lax.rem(rank + o, members)
        row = pl.multiple_of(lax.rem(q, pieces) * rows, 8)
        return pltpu.make_async_remote_copy(
            src_ref=mine.at[u, pl.ds(row, rows)],
            dst_ref=rs_in.at[u, o],
            send_sem=rs_send.at[u, o],
            recv_sem=rs_recv.at[u, o],
            device_id=member(q),
            device_id_type=MESH,
        )

    def ag_copy(u, o):
        q = block + lax.rem(piece + o, pieces)
        return pltpu.make_async_remote_copy(
            src_ref=dfull.at[u, pl.ds(piece_row, rows)],
            dst_ref=dfull.at[u, pl.ds(piece_row, rows)],
            send_sem=ag_send.at[u, o],
            recv_sem=ag_recv.at[u, o],
            device_id=member(q),
            device_id_type=MESH,
        )

    def row_of(o):
        return pl.multiple_of(my_rows + lax.rem(piece + pieces - o, pieces) * rows, 8)

    def relay_copy(u, o):
        return pltpu.make_async_remote_copy(
            src_ref=dfull.at[u, pl.ds(row_of(o), rows)],
            dst_ref=dfull.at[u, pl.ds(row_of(o), rows)],
            send_sem=re_send.at[u, o],
            recv_sem=re_recv.at[u, o],
            device_id=partner,
            device_id_type=MESH,
        )

    def y_copy(c, o):
        return pltpu.make_async_remote_copy(
            src_ref=dfull.at[index(last, c), pl.ds(row_of(o), rows)],
            dst_ref=dother.at[c, pl.ds(row_of(o), rows)],
            send_sem=y_send.at[c, o],
            recv_sem=y_recv.at[c, o],
            device_id=other_group,
            device_id_type=MESH,
        )

    def relay_other(c, o):
        return pltpu.make_async_remote_copy(
            src_ref=dother.at[c, pl.ds(row_of(o), rows)],
            dst_ref=dother.at[c, pl.ds(row_of(o), rows)],
            send_sem=r2_send.at[c, o],
            recv_sem=r2_recv.at[c, o],
            device_id=partner,
            device_id_type=MESH,
        )

    def send_core(it, c):
        core_copy(index(it, c)).start()

    def send_sums(it, c):
        u = index(it, c)
        core_copy(u).wait_recv()
        mine[u] = part[u, pl.ds(my_rows, half), :] + core_in[u]
        loop(1, members, lambda o: rs_copy(u, o).start())

    def send_scaled(it, c):
        u = index(it, c)
        own = mine[u, pl.ds(pl.multiple_of(piece * rows, 8), rows), :]

        def gather(o, total):
            rs_copy(u, o).wait_recv()
            return total + rs_in[u, o]

        coef = lax.fori_loop(1, members, gather, own)
        eigen = eig_t[pl.ds(piece_row, rows), :]
        first = first_lanes(coef)
        real = jnp.where(first, eigen[:, 0:1], eigen[:, 2:3])
        imag = jnp.where(first, eigen[:, 1:2], eigen[:, 3:4])
        dfull[u, pl.ds(piece_row, rows), :] = real * coef + imag * times_i(coef)
        loop(1, pieces, lambda o: ag_copy(u, o).start())
        relay_copy(u, 0).start()
        if it == last:
            y_copy(c, 0).start()

    def relay(it, c):
        u = index(it, c)

        def forward(o):
            ag_copy(u, o).wait_recv()
            relay_copy(u, o).start()
            if it == last:
                y_copy(c, o).start()

        loop(1, pieces, forward)

    def gathered(it, c):
        loop(0, pieces, lambda o: relay_copy(index(it, c), o).wait_recv())

    group = 2

    def fill(even, odd):
        upper = jnp.where(first_lanes(even), even, later(odd))
        lower = jnp.where(first_lanes(even), sooner(even), odd)
        value = jnp.concatenate([upper, lower], axis=0)
        dst[...] = stacked(value, times_i(value))

    def expand(start, count):
        return expansion(D, wt[pl.ds(start, count)], dst[...])

    def update(c, pairs_now):
        group = 1
        u = index(0, c)
        fill(dfull[u], dfull[u])

        def body(j):
            outs = expand(j * group, group)
            for i in range(group):
                x = j * group + i
                even, odd = outs[i]
                x1[c, x] = x0[c, x] + jnp.where(first_lanes(even), even, odd) + 0.5 * r0[c, x]

                @pl.when(x < pairs_now)
                def _():
                    send_halo(1, c, x)

                x1_copy(c, x).start()

        loop(0, lx // group, body)

    def pass_on(c):
        def body(o):
            y_copy(c, o).wait_recv()
            relay_other(c, o).start()

        loop(0, pieces, body)

    def bases(c):
        def body(x):
            x1_copy(c, x).wait_recv()
            r1_copy(c, x).wait_recv()
            own_r, other_r = r1[c, x], r1o[c, x]
            one = groups_of(x1[c, x] + 0.5 * own_r, x1o[c, x] + 0.5 * other_r)
            two = groups_of(own_r, other_r)
            for y in range(2):
                early[c, y * lx + x] = one[y]
                if c == 0:
                    res[y * lx + x, :, 0:width] = two[y]
                else:
                    res[y * lx + x] = join(res[y * lx + x, :, 0:width], two[y])

        loop(0, lx, body)

    def finish(c):
        u = index(last, c)
        loop(0, pieces, lambda o: relay_other(c, o).wait_recv())
        own, other = dfull[u], dother[c]
        fill(jnp.where(me_g == 0, own, other), jnp.where(me_g == 0, other, own))

        def body(j):
            outs = expand(j * group, group)
            for i in range(group):
                for y in range(2):
                    early[c, y * lx + j * group + i] += outs[i][y]

        if c == 0:
            loop(0, lx // group, body)

    def drain_fields(it, c):
        u = index(it, c)
        core_copy(u).wait_send()
        loop(1, members, lambda o: rs_copy(u, o).wait_send())

        def body(x):
            for slot in range(4):
                halo_copy(it, c, x, slot).wait_send()
            if it == last:
                x1_copy(c, x).wait_send()
                r1_copy(c, x).wait_send()

        loop(0, lx, body)

    def drain_coefficients(it, c):
        u = index(it, c)
        loop(1, pieces, lambda o: ag_copy(u, o).wait_send())
        loop(0, pieces, lambda o: relay_copy(u, o).wait_send())
        if it == last:
            loop(0, pieces, lambda o: y_copy(c, o).wait_send())
            loop(0, pieces, lambda o: relay_other(c, o).wait_send())

    def begin(c):
        def body(x):
            x0[c, x] = take_pair(c, x, x0f)

        loop(0, lx, body)

    def send_pairs(it, c, start, stop):
        loop(start, stop, lambda x: send_halo(it, c, x))

    early_pairs, mid_pairs, late_pairs = 2, 2, 3
    loads[0].wait()
    begin(0)
    pl.semaphore_wait(barrier, total)
    send_pairs(0, 0, 0, lx)
    begin(1)
    send_pairs(0, 1, 0, early_pairs)

    loads[1].wait()
    loop(0, lx, prepare_matrices)
    loads[2].wait()

    def take_source(x):
        for c in range(CHUNKS):
            src[c, x] = take_pair(c, x, srcf)

    loop(0, lx, take_source)
    local_part(0, 0)
    loads[3].wait()
    rows_of_eigen = jnp.concatenate([eig[:, 0:packed], eig[:, packed:nv]], axis=0)
    eig_t[...] = jnp.concatenate([rows_of_eigen, rows_of_eigen], axis=0).T
    loads[4].wait()
    loop(0, lx // 2, prepare_vectors)
    local_part(0, 1)

    halo_part(0, 0, 0)
    halo_part(0, 0, 1)
    send_core(0, 0)
    send_sums(0, 0)
    send_pairs(0, 1, early_pairs, lx)
    halo_part(0, 1, 0)
    send_scaled(0, 0)
    halo_part(0, 1, 1)
    send_core(0, 1)
    relay(0, 0)
    send_sums(0, 1)
    gathered(0, 0)
    update(0, mid_pairs)
    send_scaled(0, 1)
    send_pairs(1, 0, mid_pairs, lx)
    local_part(1, 0)
    halo_part(1, 0, 0)
    relay(0, 1)
    gathered(0, 1)
    update(1, late_pairs)
    halo_part(1, 0, 1)
    send_core(1, 0)
    send_sums(1, 0)
    send_pairs(1, 1, late_pairs, lx)
    local_part(1, 1)
    halo_part(1, 1, 0)
    send_scaled(1, 0)
    for c in range(CHUNKS):
        drain_fields(0, c)
        drain_coefficients(0, c)
    halo_part(1, 1, 1)
    send_core(1, 1)
    send_sums(1, 1)
    relay(1, 0)
    gathered(1, 0)
    pass_on(0)
    bases(0)
    send_scaled(1, 1)
    finish(0)
    bases(1)
    drain_fields(1, 0)
    drain_coefficients(1, 0)
    drain_fields(1, 1)
    relay(1, 1)
    gathered(1, 1)
    pass_on(1)
    finish(1)

    drain_coefficients(1, 1)


def finish_kernel(D, res, early, dst, wt, sol_out, res_out, sol, sol_sem, res_sem):
    copies = [pltpu.make_async_copy(res, res_out, res_sem)]
    copies[0].start()
    group = 2
    for start in range(0, D.lx, group):
        outs = expansion(D, wt[start:start + group], dst[...])
        for i in range(group):
            for y in range(D.ly):
                site = y * D.lx + start + i
                sol[site] = join(early[0, site], early[1, site] + outs[i][y])
                copies.append(pltpu.make_async_copy(sol.at[site], sol_out.at[site], sol_sem.at[site]))
                copies[-1].start()
    for copy in copies:
        copy.wait()


def solve(mesh, couplings, source, initial, vectors, inverse_eigen):
    nine, _, _, ly, lx, nc, _ = couplings.shape
    full = source.shape[-1]
    nv = vectors.shape[0]
    D = Dims(mesh, ly, lx, nc, full, nv)
    sites, width = D.sites, D.width
    field = (sites, nc, full)
    mine = (CHUNKS, lx, nc, width)
    units = ITERS * CHUNKS
    block_k = ly * 2 * nc
    vecs = vectors.reshape(nv, sites, 2 * nc).transpose(1, 2, 0)
    any_spec = pl.BlockSpec(memory_space=pl.ANY)
    vmem = pl.BlockSpec(memory_space=pltpu.VMEM)
    dma = pltpu.SemaphoreType.DMA
    out = jax.ShapeDtypeStruct(field, F32)
    between = (
        out,
        jax.ShapeDtypeStruct((CHUNKS, sites, nc, width), F32),
        jax.ShapeDtypeStruct((2 * nv, 2 * width), BF16),
        jax.ShapeDtypeStruct((lx, ly, 2 * nc, 2 * nv), BF16),
    )
    held = pl.pallas_call(
        functools.partial(kernel, D),
        out_shape=between,
        in_specs=[any_spec] * 5,
        out_specs=(vmem,) * 4,
        scratch_shapes=[
            pltpu.VMEM((nine, sites, nc, 2 * nc), F32),
            pltpu.VMEM(field, F32),
            pltpu.VMEM(field, F32),
            pltpu.VMEM((sites, 2 * nc, nv), F32),
            pltpu.VMEM((2, nv), F32),
            dma((5,)),
        ]
        + [pltpu.VMEM(mine, F32)] * 8
        + [
            pltpu.VMEM((lx, 2 * nc, 4 * block_k), BF16),
            pltpu.VMEM((lx, 2 * nc, 4 * block_k), BF16),
            pltpu.VMEM((lx // 2, 2 * nv, 2 * block_k), BF16),
            pltpu.VMEM((lx, 4 * block_k, 2 * width), BF16),
            pltpu.VMEM((4 * block_k, 2 * width), BF16),
            pltpu.VMEM((lx // 2 * block_k, 2 * width), BF16),
            pltpu.VMEM((nv, width), F32),
            pltpu.VMEM((units, 4, lx, nc, width), F32),
            pltpu.VMEM((units, D.packed, width), F32),
            pltpu.VMEM((units, D.half, width), F32),
            pltpu.VMEM((units, D.half, width), F32),
            pltpu.VMEM((units, D.members, D.rows, width), F32),
            pltpu.VMEM((units, D.packed, width), F32),
            pltpu.VMEM((CHUNKS, D.packed, width), F32),
            pltpu.VMEM((D.packed, 8), F32),
            dma((units, 4, lx)),
            dma((units, 4, lx)),
            dma((units,)),
            dma((units,)),
            dma((units, D.members)),
            dma((units, D.members)),
            dma((units, D.pieces)),
            dma((units, D.pieces)),
            dma((units, D.pieces)),
            dma((units, D.pieces)),
            dma((CHUNKS, D.pieces)),
            dma((CHUNKS, D.pieces)),
            dma((CHUNKS, lx)),
            dma((CHUNKS, lx)),
            dma((CHUNKS, lx)),
            dma((CHUNKS, lx)),
            dma((CHUNKS, D.pieces)),
            dma((CHUNKS, D.pieces)),
        ],
        compiler_params=pltpu.CompilerParams(
            collective_id=0, has_side_effects=True, vmem_limit_bytes=44 * 1024 * 1024
        ),
    )(
        pltpu.with_memory_space_constraint(couplings.reshape(nine, sites, nc, 2 * nc), pltpu.HBM),
        pltpu.with_memory_space_constraint(source.reshape(field), pltpu.HBM),
        pltpu.with_memory_space_constraint(initial.reshape(field), pltpu.HBM),
        pltpu.with_memory_space_constraint(vecs, pltpu.HBM),
        pltpu.with_memory_space_constraint(inverse_eigen, pltpu.HBM),
    )
    held = [pltpu.with_memory_space_constraint(value, pltpu.VMEM) for value in held]
    x, r = pl.pallas_call(
        functools.partial(finish_kernel, D),
        out_shape=(out, out),
        in_specs=[vmem] * 4,
        out_specs=(any_spec, any_spec),
        scratch_shapes=[pltpu.VMEM(field, F32), dma((sites,)), dma],
        compiler_params=pltpu.CompilerParams(vmem_limit_bytes=16 * 1024 * 1024),
    )(*held)
    return x.reshape(source.shape), r.reshape(source.shape)


def solution(mesh):
    in_specs = (
        P(None, "tm", "space", None, None, None, None),
        P("tm", "space", None, None, None, None),
        P("tm", "space", None, None, None, None),
        P(None, "tm", "space", None, None, None),
        P(),
    )
    out_specs = (
        P(("groups", "tm"), "space", None, None, None, None),
        P(("groups", "tm"), "space", None, None, None, None),
    )
    return jax.shard_map(
        functools.partial(solve, mesh), mesh=mesh, in_specs=in_specs, out_specs=out_specs, check_vma=False
    )
```
